32 devices in a mesh: lat: 8 (over z, y), lev: 4 (over x, core).
Axes of the slice: x: 2, y: 2, z: 4, core: 2. Of those that a mesh axis runs over, the one named last changes fastest.
Arguments:
- field: float32 [4, 320, 4096], P(None, 'lat', 'lev'), may hold values from -6 to 6
- weights: bfloat16 [4, 320, 4096], P(None, 'lat', 'lev'), may hold values from 0 to 0.5
- depart_row: int32 [320, 4096], P('lat', 'lev'), may hold values from -2 to 1
- depart_col: int32 [320, 4096], P('lat', 'lev'), may hold values from -2 to 1
- legendre: bfloat16 [320, 16, 640], P('lat'), may hold values from -6 to 6
- wave_slot: int32 [16], replicated, may hold values from 0 to 15, each once
Outputs:
- updated: float32 [4, 320, 4096], P(None, 'lat', 'lev')
- spectral: float32 [16, 2, 4, 2, 640], P('lat', None, 'lev')
The draws below stay inside these ranges and needn't reach their ends.
Inputs may be any that keep to these rules, and one draw needn't show every extreme that they name: `depart_row`: latitude offsets of departure cells, so that rows i - 2 to i + 2 are read. `depart_col`: longitude offsets of departure cells, so that columns j - 2 to j + 2 are read, periodically. `wave_slot`: A permutation of 0 to 15.
All inputs are finite; a program needn't handle non-finite values.
Results may differ from the reference program's by a relative error of at most 0.0033.
Values may be sent and summed in bfloat16 or wider, within the bound.
A program may use at most 128 MiB of HBM per device.

```python
import math
import jax
import jax.numpy as jnp
from jax import lax

NLON = 4096
NT = 1279
NJ = 640
NLAT = 320
LEV = 4
M_WIN = 16


def place_ends(result, key, low, high):
    index_at = [jax.random.randint(jax.random.fold_in(key, axis), (), 0, length) for axis, length in enumerate(result.shape)]
    main_axis = result.shape.index(max(result.shape))
    next_to = index_at[:main_axis] + [(index_at[main_axis] + 1) % result.shape[main_axis]] + index_at[main_axis + 1:]
    return result.at[tuple(index_at)].set(low).at[tuple(next_to)].set(high)


def shard_levels(rng, dims, split, smallest, top_value):
    def one(axis_at, parts):
        draws = jax.random.uniform(jax.random.fold_in(jax.random.fold_in(rng, 6), axis_at), (parts,), jnp.float32, smallest / len(split), top_value / len(split))
        return jnp.repeat(jnp.exp(draws), dims[axis_at] // parts).reshape((-1,) + (1,) * (len(dims) - axis_at - 1))

    level = one(*split[0])
    for cut in split[1:]:
        level = level * one(*cut)
    return level


def gaussian(rng, shape, spread, reach, split=(), held_as=jnp.bfloat16):
    entries = spread * jax.random.normal(rng, shape, jnp.float32)
    if split:
        entries = entries * shard_levels(rng, shape, split, -0.22, 0.18)
    return jnp.clip(entries, -reach, reach).astype(held_as)


def setup_inputs(seed: int = 0) -> dict:
    streams_of = jax.random.split(jax.random.key(seed), 7)
    field = gaussian(streams_of[0], (LEV, NLAT, NLON), 1.0, 6.0, ((1, 8), (2, 4)), jnp.float32)
    weights = jnp.clip(0.5 * jax.random.uniform(streams_of[1], (4, NLAT, NLON), jnp.float32) ** shard_levels(streams_of[1], (4, NLAT, NLON), ((1, 8), (2, 4)), -0.2, 0.2), 0.0, 0.5).astype(jnp.bfloat16)
    depart_row = place_ends(jax.random.randint(streams_of[2], (NLAT, NLON), -2, 2), jax.random.fold_in(streams_of[2], 1), -2, 1).astype(jnp.int32)
    depart_col = place_ends(jax.random.randint(streams_of[3], (NLAT, NLON), -2, 2), jax.random.fold_in(streams_of[3], 1), -2, 1).astype(jnp.int32)
    legendre = gaussian(streams_of[4], (NLAT, M_WIN, NJ), 1.0, 6.0, ((0, 8),))
    wave_slot = jax.random.permutation(streams_of[5], M_WIN).astype(jnp.int32)
    return {"field": field, "weights": weights, "depart_row": depart_row, "depart_col": depart_col, "legendre": legendre, "wave_slot": wave_slot}


DAMPING = 4.0

def advect(field, weights, depart_row, depart_col):
    padded = jnp.pad(field, ((0, 0), (2, 2), (0, 0)))
    flattened = padded.reshape(LEV, (NLAT + 4) * NLON)
    row_index = jnp.arange(NLAT, dtype=jnp.int32)[:, None] + 2 + depart_row
    col_index = jnp.arange(NLON, dtype=jnp.int32)[None, :] + depart_col
    summed = jnp.zeros((LEV, NLAT * NLON), jnp.float32)
    for row_step in range(2):
        for col_step in range(2):
            source = ((row_index + row_step) * NLON + (col_index + col_step) % NLON).reshape(-1).astype(jnp.int32)
            corner = weights[2 * row_step + col_step].reshape(-1).astype(jnp.float32)
            summed = summed + corner[None, :] * jnp.take(flattened, source, axis=1)
    return summed.reshape(LEV, NLAT, NLON)

def reference(field, weights, depart_row, depart_col, legendre, wave_slot):
    advected = advect(field, weights, depart_row, depart_col)
    wavenumbers = jnp.arange(M_WIN, dtype=jnp.int32) * (NT + 1) // M_WIN
    spectrum = jnp.fft.rfft(advected, axis=2)[:, :, wavenumbers]
    fourier = (jnp.stack([spectrum.real, spectrum.imag], axis=2) / math.sqrt(NLON)).astype(jnp.bfloat16)
    half_lat = NLAT // 2
    north_rows = fourier[:, :half_lat].astype(jnp.float32)
    south_rows = jnp.flip(fourier[:, half_lat:], axis=1).astype(jnp.float32)
    leg_north = legendre[:half_lat].astype(jnp.float32)
    leg_south = jnp.flip(legendre[half_lat:], axis=0).astype(jnp.float32)
    hp = lax.Precision.HIGHEST
    norm_scale = 1.0 / math.sqrt(half_lat)
    even_sums = (jnp.einsum('lkq,vlck->kvcq', leg_north, north_rows, precision=hp) + jnp.einsum('lkq,vlck->kvcq', leg_north, south_rows, precision=hp)) * norm_scale
    odd_sums = (jnp.einsum('lkq,vlck->kvcq', leg_south, north_rows, precision=hp) - jnp.einsum('lkq,vlck->kvcq', leg_south, south_rows, precision=hp)) * norm_scale
    raw_sums = jnp.stack([even_sums, odd_sums], axis=1)
    degree = wavenumbers[:, None, None] + 2 * jnp.arange(NJ, dtype=jnp.int32)[None, None, :] + jnp.arange(2, dtype=jnp.int32)[None, :, None]
    inside = degree <= NT
    factor = 1.0 / (1.0 + DAMPING * (degree * (degree + 1)).astype(jnp.float32) / float(NT * (NT + 1)))
    masked = jnp.where(inside[:, :, None, None, :], raw_sums, jnp.zeros_like(raw_sums))
    damped = masked * factor[:, :, None, None, :]
    change = (damped - masked).astype(jnp.bfloat16).astype(jnp.float32)
    slot_order = jnp.argsort(wave_slot).astype(jnp.int32)
    spectral = jnp.take(damped, slot_order, axis=0)
    inverse_scale = 1.0 / math.sqrt(NJ)
    upper = jnp.einsum('lkq,kvcq->vlck', leg_north, change[:, 0], precision=hp) * inverse_scale
    lower = jnp.einsum('lkq,kvcq->vlck', leg_south, change[:, 1], precision=hp) * inverse_scale
    synthesis = jnp.concatenate([upper + lower, jnp.flip(upper - lower, axis=1)], axis=1)
    real_full = jnp.zeros((LEV, NLAT, NLON // 2 + 1), synthesis.dtype).at[:, :, wavenumbers].set(synthesis[:, :, 0])
    imag_full = jnp.zeros((LEV, NLAT, NLON // 2 + 1), synthesis.dtype).at[:, :, wavenumbers].set(synthesis[:, :, 1])
    increment = jnp.fft.irfft(lax.complex(real_full, imag_full), n=NLON, axis=2) * (NLON / math.sqrt(M_WIN))
    updated = advected + increment
    return (updated, spectral)
```

```python
import functools
import math

import jax
import jax.numpy as jnp
import numpy as np
from jax import lax
from jax.experimental import pallas as pl
from jax.experimental.pallas import tpu as pltpu
from jax.sharding import PartitionSpec as P

NLON = 4096
NT = 1279
DAMPING = 4.0
LANES = 128
HALF = 64
MESH = pl.DeviceIdType.MESH
F32 = jnp.float32
BF16 = jnp.bfloat16


def lon_table(waves):
    m = (np.arange(waves, dtype=np.int64) * (NT + 1)) // waves
    phases = (m[:, None] * np.arange(NLON, dtype=np.int64)[None, :]) % NLON
    angles = phases.astype(np.float64) * (2.0 * math.pi / NLON)
    table = np.concatenate([np.cos(angles), -np.sin(angles)], axis=0) / math.sqrt(NLON)
    table = table.astype(np.float32)
    lead = table.astype(BF16)
    rest = (table - lead.astype(np.float32)).astype(BF16)
    return np.concatenate([lead, rest], axis=0)


def each(start, stop):
    def run(body):
        if stop - start <= 64:
            for i in range(start, stop):
                body(i)
        else:
            lax.fori_loop(start, stop, lambda i, carry: (body(i), carry)[1], 0)

    return run


def one_hot(mask):
    return jnp.where(mask, 1.0, 0.0).astype(BF16)


def kernel(
    n_lat, n_lev,
    slot_ref, field_hbm, weights_hbm, drow_hbm, dcol_hbm, leg_hbm, table_hbm,
    adv, synth, wide, spec_ref,
    ext, shifted, wts, drow, dcol, leg, tab, tabs,
    pack_row, pack_col, got_row, got_col, got_corner,
    send_leg, basis, stage, send_1, got_1, both_f, both_b, send_2, got_2, cross, send_p, got_p,
    load_sem, halo_send, halo_recv, leg_send, leg_recv, one_send, one_recv,
    two_send, two_recv, p_send, p_recv,
):
    levels, _, _, _ = ext.shape
    rows, width = drow.shape
    tiles = width // LANES
    steps = leg.shape[1]
    waves = leg.shape[0] // rows
    n = n_lat * n_lev
    half = n_lat // 2
    group = waves // half
    rep = n_lev // group
    lv = levels // rep
    own = waves // n_lat
    l, e = lax.axis_index("lat"), lax.axis_index("lev")
    me = l * n_lev + e
    parity, lh = lax.div(l, half), lax.rem(l, half)
    share = lax.rem(e, rep)
    slot = group * lh + lax.div(e, rep)
    has_up, has_down = l > 0, l < n_lat - 1
    east, west = lax.rem(e + 1, n_lev), lax.rem(e + n_lev - 1, n_lev)

    def device(off):
        d = lax.rem(me + off, n)
        return lax.div(d, n_lev), lax.rem(d, n_lev)

    loads = []

    def load(src, dst):
        copy = pltpu.make_async_copy(src, dst, load_sem.at[len(loads)])
        copy.start()
        loads.append(copy)

    for t in range(tiles):
        load(
            field_hbm.at[:, :, pl.ds(t * LANES, LANES)],
            ext.at[:, t + 1, pl.ds(8, rows), :],
        )
    load(weights_hbm, wts)
    load(drow_hbm, drow)
    load(dcol_hbm, dcol)
    load(table_hbm.at[:, pl.ds(pl.multiple_of(e * width, LANES), width)], tab)
    load(leg_hbm, leg)

    barrier = pltpu.get_barrier_semaphore()

    @each(1, n)
    def _(off):
        lat, lev = device(off)
        pl.semaphore_signal(barrier, inc=1, device_id=(lat, lev), device_id_type=MESH)

    lane = lax.broadcasted_iota(jnp.int32, (rows, LANES), 1)
    for t in range(tiles):
        loads[t].wait()
    for v in range(levels):
        for t in range(tiles):
            cols = slice(t * LANES, (t + 1) * LANES)
            pack_row[0, 2 * v : 2 * v + 2, cols] = ext[v, t + 1, 6 + rows : 8 + rows, :]
            pack_row[1, 2 * v : 2 * v + 2, cols] = ext[v, t + 1, 8:10, :]
    last = jnp.zeros((rows, LANES), F32)
    first = jnp.zeros((rows, LANES), F32)
    for v in range(levels):
        here = (lane == 2 * v) | (lane == 2 * v + 1)
        tail = pltpu.roll(ext[v, tiles, 8 : 8 + rows, :], (2 * v + 2) % LANES, 1)
        last = jnp.where(here, tail, last)
        head = ext[v, 1, 8 : 8 + rows, :]
        if v:
            head = pltpu.roll(head, 2 * v, 1)
        first = jnp.where(here, head, first)
    pack_col[0] = last
    pack_col[1] = first

    def shift_block(v, t, row0, size, moves=(-2, -1, 1, 2)):
        at = pl.ds(row0, size)
        at_lane = lax.broadcasted_iota(jnp.int32, (size, LANES), 1)
        here = ext[v, t + 1, at, :]
        left = ext[v, t, at, :] if min(moves) < 0 else None
        right = ext[v, t + 2, at, :] if max(moves) > 0 else None
        for move in moves:
            n_move = (-2, -1, 1, 2).index(move)
            amount = (-move) % LANES
            mine = pltpu.roll(here, amount, 1)
            if move < 0:
                moved = jnp.where(at_lane < -move, pltpu.roll(left, amount, 1), mine)
            else:
                moved = jnp.where(at_lane >= LANES - move, pltpu.roll(right, amount, 1), mine)
            shifted[n_move, v, t, at, :] = moved

    def shift_inner(chosen):
        def step(t, carry):
            for v in chosen:
                shift_block(v, t, 8, rows)
            return carry

        lax.fori_loop(1, tiles - 1, step, 0)

    groups = rows // 8

    def advect(t, chosen):
        cols = pl.ds(pl.multiple_of(t * LANES, LANES), LANES)
        corner = [wts[ab, :, cols].astype(F32) for ab in range(4)]
        for g in chosen:
            band = slice(8 * g, 8 * g + 8)
            dr, dc = drow[band, cols], dcol[band, cols]
            zero = jnp.zeros((8, LANES), F32)
            in_col = {c: dc == c for c in range(-2, 2)}
            in_row = {r: dr == r for r in range(-2, 2)}

            def pick(masks, at, one, two):
                value = zero
                if at - 1 in masks:
                    value = jnp.where(masks[at - 1], two, value)
                if at in masks:
                    value = jnp.where(masks[at], one, value)
                return value

            part = [
                [pick(in_col, c, corner[2 * a][band], corner[2 * a + 1][band]) for c in range(-2, 3)]
                for a in range(2)
            ]
            coef = [
                [pick(in_row, r, part[0][c], part[1][c]) for c in range(5)] for r in range(-2, 3)
            ]
            for v in range(levels):
                total = None
                for r in range(5):
                    at = pl.ds(8 * g + 6 + r, 8)
                    for c in range(5):
                        if c == 2:
                            value = ext[v, t + 1, at, :]
                        else:
                            value = shifted[c if c < 2 else c - 1, v, t, at, :]
                        term = coef[r][c] * value
                        total = term if total is None else total + term
                adv[v * rows + 8 * g : v * rows + 8 * g + 8, cols] = total

    def advect_inner(t, carry):
        advect(t, range(1, groups - 1))
        return carry

    shift_inner(range(levels // 2))

    pl.semaphore_wait(barrier, n - 1)

    def remote(src, dst, ssem, rsem, lat, lev):
        return pltpu.make_async_remote_copy(
            src_ref=src, dst_ref=dst, send_sem=ssem, recv_sem=rsem,
            device_id=(lat, lev), device_id_type=MESH,
        )

    def halo(n, src, dst, lat, lev):
        return remote(src, dst, halo_send.at[n], halo_recv.at[n], lat, lev)

    bottom, top = pl.ds(rows - 8, 8), pl.ds(0, 8)
    flat = [
        halo(0, pack_col.at[0], got_col.at[0], l, east),
        halo(1, pack_col.at[1], got_col.at[1], l, west),
    ]
    below = [
        halo(2, pack_row.at[0], got_row.at[0], l + 1, e),
        halo(3, pack_col.at[0, bottom], got_corner.at[0], l + 1, east),
        halo(4, pack_col.at[1, bottom], got_corner.at[1], l + 1, west),
    ]
    above = [
        halo(5, pack_row.at[1], got_row.at[1], l - 1, e),
        halo(6, pack_col.at[0, top], got_corner.at[2], l - 1, east),
        halo(7, pack_col.at[1, top], got_corner.at[3], l - 1, west),
    ]

    @pl.when(has_down)
    def _():
        for copy in below:
            copy.start()

    @pl.when(has_up)
    def _():
        for copy in above:
            copy.start()

    for copy in flat:
        copy.start()

    first = lax.broadcasted_iota(jnp.int32, (1, 4 * waves), 1)
    slot_row = jnp.zeros((1, 4 * waves), jnp.int32)
    for k in range(waves):
        slot_row = jnp.where(lax.rem(first, waves) == k, slot_ref[k], slot_row)
    at = lambda shape, dim: lax.broadcasted_iota(jnp.int32, shape, dim)
    iota_f = (4 * waves, 4 * waves)
    order = one_hot(
        (lax.div(at(iota_f, 0), waves) == lax.div(at(iota_f, 1), waves))
        & (lax.rem(at(iota_f, 0), waves) == slot_row)
    )
    stage[...] = jnp.zeros_like(stage)
    cross[...] = jnp.zeros_like(cross)
    padded = send_leg.shape[1]
    basis[:, padded:, :] = jnp.zeros((half, HALF - padded, steps), BF16)

    shift_inner(range(levels // 2, levels))
    if tiles > 1:
        for v in range(levels):
            shift_block(v, 0, 8, rows, (1, 2))
            shift_block(v, tiles - 1, 8, rows, (-2, -1))
    for t in range(tiles, tiles + 3):
        loads[t].wait()
    lax.fori_loop(1, tiles - 1, advect_inner, 0)

    loads[tiles + 4].wait()
    send_leg[...] = jnp.zeros_like(send_leg)
    band = 8
    iota_g = (half * band, band * waves)
    slot_cols = jnp.zeros((1, band * waves), jnp.int32)
    lane_k = lax.rem(lax.broadcasted_iota(jnp.int32, (1, band * waves), 1), waves)
    for k in range(waves):
        slot_cols = jnp.where(lane_k == k, slot_ref[k], slot_cols)
    choose = one_hot(
        (lax.rem(at(iota_g, 0), band) == lax.div(at(iota_g, 1), waves))
        & (group * lax.div(at(iota_g, 0), band) + lax.div(e, rep) == slot_cols)
    )
    for i in range(0, rows, band):
        picked = jnp.dot(
            choose, leg[i * waves : (i + band) * waves, :], preferred_element_type=F32
        ).astype(BF16)
        for t in range(half):
            send_leg[t, i : i + band, :] = picked[t * band : (t + 1) * band]
    slots_of = lambda t: basis.at[t, pl.ds(0, padded), :]
    copies_g = []
    for off in range(1, half):
        t = lax.rem(lh + off, half)
        copy = remote(
            send_leg.at[t], slots_of(lh), leg_send.at[off], leg_recv.at[lh],
            parity * half + t, e,
        )
        copy.start()
        copies_g.append(copy)
    basis[lh, 0:padded, :] = send_leg[lh]

    loads[tiles + 3].wait()
    tabs[...] = jnp.dot(order, tab[...], preferred_element_type=F32).astype(BF16)


    def spread(piece, v):
        return pltpu.roll(piece, LANES - 2 - 2 * v, 1)

    def spread_east(piece, v):
        return pltpu.roll(piece, LANES - 2 * v, 1) if v else piece

    def rim(row0, size, from_west, from_east):
        for v in range(levels):
            ext[v, 0, row0 : row0 + size, :] = spread(from_west, v)
            ext[v, tiles + 1, row0 : row0 + size, :] = spread_east(from_east, v)

    def fill_rows(which, row0):
        for v in range(levels):
            for t in range(tiles):
                cols = slice(t * LANES, (t + 1) * LANES)
                ext[v, t + 1, row0 : row0 + 2, :] = got_row[which, 2 * v : 2 * v + 2, cols]

    @pl.when(has_up)
    def _():
        for copy in below:
            copy.wait_recv()
        fill_rows(0, 6)
        rim(0, 8, got_corner[0], got_corner[1])

    @pl.when(jnp.logical_not(has_up))
    def _():
        ext[:, :, 0:8, :] = jnp.zeros((levels, tiles + 2, 8, LANES), F32)

    @pl.when(has_down)
    def _():
        for copy in above:
            copy.wait_recv()
        fill_rows(1, rows + 8)
        rim(rows + 8, 8, got_corner[2], got_corner[3])

    @pl.when(jnp.logical_not(has_down))
    def _():
        ext[:, :, rows + 8 : rows + 16, :] = jnp.zeros((levels, tiles + 2, 8, LANES), F32)

    for copy in flat:
        copy.wait_recv()
    rim(8, rows, got_col[0], got_col[1])

    def shift_rims(t, carry):
        for v in range(levels):
            shift_block(v, t, 0, 8)
            shift_block(v, t, rows + 8, 8)
        return carry

    edges = min(tiles, 2)
    for v in range(levels):
        shift_block(v, 0, 8, rows, (-2, -1))
        shift_block(v, tiles - 1, 8, rows, (1, 2))
    lax.fori_loop(0, tiles, shift_rims, 0)
    outer = sorted({0, groups - 1})

    def advect_rims(t, carry):
        advect(t, outer)
        return carry

    def advect_edge(n, carry):
        advect(n * (tiles - 1), range(groups))
        return carry

    lax.fori_loop(0, edges, advect_edge, 0)
    lax.fori_loop(1, tiles - 1, advect_rims, 0)

    contract_last = (((1,), (1,)), ((), ()))
    for v in range(levels):
        value = adv[v * rows : (v + 1) * rows, :]
        lead = value.astype(BF16)
        rest = (value - lead.astype(F32)).astype(BF16)
        both = lax.dot_general(tabs[...], lead, contract_last, preferred_element_type=F32)
        more = lax.dot_general(
            tabs[0 : 2 * waves, :], rest, contract_last, preferred_element_type=F32
        )
        coeffs = both[0 : 2 * waves] + both[2 * waves :] + more
        stage[v * waves : (v + 1) * waves, 0:rows] = coeffs[0:waves]
        stage[v * waves : (v + 1) * waves, HALF : HALF + rows] = coeffs[waves:]
    owners = half * n_lev
    for s in range(waves):
        for g in range(rep):
            send_1[s * rep + g] = stage[pl.ds(g * lv * waves + s, lv, stride=waves), :]

    def copy_1(off):
        lat, lev = device(off)
        owner = lax.rem(lat, half) * n_lev + lev
        return remote(
            send_1.at[owner], got_1.at[me], one_send.at[off], one_recv.at[me], lat, lev
        )

    @each(1, n)
    def _(off):
        copy_1(off).start()

    got_1[me] = send_1[lh * n_lev + e]

    spread_rows = 2 * waves * levels
    iota_w = (spread_rows, 2 * waves)
    repeat = one_hot(lax.div(at(iota_w, 0), levels) == at(iota_w, 1))
    for q in range(2):
        wide[q] = jnp.dot(
            repeat, tabs[2 * waves * q : 2 * waves * (q + 1), :], preferred_element_type=F32
        ).astype(BF16)

    at_row, at_col = at((LANES, LANES), 0), at((LANES, LANES), 1)
    flip = one_hot(
        ((at_row + at_col == rows - 1) & (at_row < HALF) & (at_col < HALF))
        | ((at_row + at_col == 2 * HALF + rows - 1) & (at_row >= HALF) & (at_col >= HALF))
    )
    sign = jnp.where(parity == 0, 1.0, -1.0).astype(F32)
    iota_e = (rows, 4 * LANES)
    row_e, col_e = at(iota_e, 0), at(iota_e, 1)
    part_e, lane_e = lax.div(col_e, LANES), lax.rem(col_e, LANES)
    place = HALF * lax.div(part_e, 2)
    natural = (lax.rem(part_e, 2) == 1) & (lane_e == row_e + place)
    turned = (lax.rem(part_e, 2) == 0) & (lane_e == rows - 1 - row_e + place)
    gather = (jnp.where(natural, sign, 0.0) + jnp.where(turned, 1.0, 0.0)).astype(BF16)

    wave_own = jnp.int32(0)
    for k in range(waves):
        wave_own = jnp.where(slot_ref[k] == slot, k, wave_own)
    wave_own = wave_own * (NT + 1) // waves
    column = lax.broadcasted_iota(jnp.int32, (2 * lv, steps), 1)
    degree = wave_own + 2 * column + parity
    factor = 1.0 / (
        1.0 + DAMPING * (degree * (degree + 1)).astype(F32) / float(NT * (NT + 1))
    )
    forward_scale = 1.0 / math.sqrt(rows * n_lat // 2)
    inverse_scale = math.sqrt(NLON) / math.sqrt(waves) / math.sqrt(steps)
    scale = jnp.where(wave_own == 0, inverse_scale, 2.0 * inverse_scale).astype(F32)

    for off in range(1, half):
        t = lax.rem(lh + off, half)
        remote(
            send_leg.at[t], slots_of(t), leg_send.at[off], leg_recv.at[t], parity * half + t, e
        ).wait_recv()

    def wait_1(off):
        lat, lev = device(off)
        d = lat * n_lev + lev
        remote(send_1.at[0], got_1.at[d], one_send.at[off], one_recv.at[d], lat, lev).wait_recv()

    @each(1, n)
    def _(off):
        wait_1(off)

    low = lax.broadcasted_iota(jnp.int32, (lv, LANES), 1) < HALF

    def total_1(lat):
        value = got_1[lat * n_lev]
        for d in range(1, n_lev):
            value = value + got_1[lat * n_lev + d]
        return value

    for b in range(0, half, 2):
        cols = slice(b * HALF, b * HALF + LANES)
        for which in range(2):
            lat = parity * half + b
            one = total_1(lat if which == 0 else n_lat - 1 - lat)
            two = total_1(lat + 1 if which == 0 else n_lat - 2 - lat)
            row0 = which * 2 * lv
            both_f[row0 : row0 + lv, cols] = jnp.where(low, one, pltpu.roll(two, HALF, 1))
            both_f[row0 + lv : row0 + 2 * lv, cols] = jnp.where(
                low, pltpu.roll(one, HALF, 1), two
            )
    near = both_f[0 : 2 * lv, :].astype(BF16)
    both_b[0 : 2 * lv, :] = near
    for c0 in range(0, half * HALF, LANES):
        cols = slice(c0, c0 + LANES)
        both_b[2 * lv :, cols] = jnp.dot(
            both_f[2 * lv :, cols].astype(BF16), flip, preferred_element_type=F32
        ).astype(BF16)
    matrix = basis[...].reshape(half * HALF, steps)
    raw = jnp.dot(both_b[...], matrix, preferred_element_type=F32)
    raw = (raw[2 * lv :] + sign * raw[0 : 2 * lv]) * forward_scale
    masked = jnp.where(degree <= NT, raw, 0.0)
    damped = masked * factor
    change = (damped - masked).astype(BF16)
    back = lax.dot_general(change, matrix, contract_last, preferred_element_type=F32) * scale
    both_f[0 : 2 * lv, :] = back
    for b in range(0, half, 2):
        cols = slice(b * HALF, b * HALF + LANES)
        real, imag = both_f[0:lv, cols], both_f[lv : 2 * lv, cols]
        send_2[b] = jnp.where(low, real, pltpu.roll(imag, HALF, 1))
        send_2[b + 1] = jnp.where(low, pltpu.roll(real, HALF, 1), imag)

    def copy_2(off):
        lat, lev = device(off)
        inside = lax.div(lat, half) == parity
        block = jnp.where(inside, lat, n_lat - 1 - lat) - parity * half
        return remote(
            send_2.at[block], got_2.at[me], two_send.at[off], two_recv.at[me], lat, lev
        )

    @each(1, n)
    def _(off):
        copy_2(off).start()

    got_2[me] = send_2[lh]

    for vv in range(lv):
        for c in range(2):
            send_p[vv, c : c + 1, :] = damped[c * lv + vv : c * lv + vv + 1]
    home, place_p = lax.div(slot, own), lax.rem(slot, own)
    for vv in range(lv):
        lev = share * lv + vv
        mine = (home == l) & (lev == e)
        copy = remote(
            send_p.at[vv], got_p.at[place_p, parity], p_send.at[vv],
            p_recv.at[place_p, parity], home, lev,
        )
        pl.when(jnp.logical_not(mine))(copy.start)

        @pl.when(mine)
        def _():
            got_p[place_p, parity] = send_p[vv]

    def wait_2(off):
        lat, lev = device(off)
        d = lat * n_lev + lev
        remote(send_2.at[0], got_2.at[d], two_send.at[off], two_recv.at[d], lat, lev).wait_recv()

    @each(1, n)
    def _(off):
        wait_2(off)

    pairs = waves * levels
    for which in range(2):
        start = jnp.where(which == 1, parity, 1 - parity) * owners
        for o in range(owners):
            stage[which * pairs + o * lv : which * pairs + (o + 1) * lv, :] = got_2[start + o]
    for which in range(2):
        value = stage[which * pairs : (which + 1) * pairs, :]
        lead = value.astype(BF16)
        rest = (value - lead.astype(F32)).astype(BF16)
        for c in range(2):
            cols = slice((2 * c + which) * LANES, (2 * c + which + 1) * LANES)
            cross[0, c * pairs : (c + 1) * pairs, cols] = lead
            cross[1, c * pairs : (c + 1) * pairs, cols] = rest
    synth[...] = lax.dot_general(
        gather, cross[0], contract_last, preferred_element_type=F32
    ) + lax.dot_general(gather, cross[1], contract_last, preferred_element_type=F32)

    for so in range(own):
        for pp in range(2):
            from_slot = own * l + so
            lat = pp * half + lax.div(from_slot, group)
            lev = lax.rem(from_slot, group) * rep + lax.div(e, lv)
            copy = remote(
                send_p.at[0], got_p.at[so, pp], p_send.at[0], p_recv.at[so, pp], lat, lev
            )
            pl.when(jnp.logical_not((lat == l) & (lev == e)))(copy.wait_recv)
    spec_ref[...] = got_p[...]

    for copy in flat + copies_g:
        copy.wait_send()

    @each(1, n)
    def _(off):
        copy_1(off).wait_send()
        copy_2(off).wait_send()

    for vv in range(lv):
        lev = share * lv + vv
        copy = remote(
            send_p.at[vv], got_p.at[place_p, parity], p_send.at[vv],
            p_recv.at[place_p, parity], home, lev,
        )
        pl.when(jnp.logical_not((home == l) & (lev == e)))(copy.wait_send)

    @pl.when(has_down)
    def _():
        for copy in below:
            copy.wait_send()

    @pl.when(has_up)
    def _():
        for copy in above:
            copy.wait_send()


def finish(adv, synth, wide, spec, out_hbm, spec_hbm, lead_all, rest_all, result, sems):
    levels, rows, width = result.shape
    spec_copy = pltpu.make_async_copy(spec, spec_hbm, sems.at[0])
    spec_copy.start()
    value = synth[...]
    lead = value.astype(BF16).astype(F32)
    rest = value - lead
    level_of = lax.rem(lax.broadcasted_iota(jnp.int32, value.shape, 1), levels)
    for v in range(levels):
        at = slice(v * rows, (v + 1) * rows)
        lead_all[at, :] = jnp.where(level_of == v, lead, 0.0).astype(BF16)
        rest_all[at, :] = jnp.where(level_of == v, rest, 0.0).astype(BF16)
    chunk = min(width, 256)
    copies = []
    for j in range(0, width, chunk):
        cols = slice(j, j + chunk)
        increment = (
            jnp.dot(lead_all[...], wide[0, :, cols], preferred_element_type=F32)
            + jnp.dot(lead_all[...], wide[1, :, cols], preferred_element_type=F32)
            + jnp.dot(rest_all[...], wide[0, :, cols], preferred_element_type=F32)
        )
        updated = adv[:, cols] + increment
        for v in range(levels):
            result[v, :, cols] = updated[v * rows : (v + 1) * rows]
        copy = pltpu.make_async_copy(
            result.at[:, :, cols], out_hbm.at[:, :, cols], sems.at[1 + j // chunk]
        )
        copy.start()
        copies.append(copy)
    for copy in copies + [spec_copy]:
        copy.wait()


def solution(mesh):
    n_lat, n_lev = mesh.shape["lat"], mesh.shape["lev"]

    def on_device(field, weights, depart_row, depart_col, legendre, wave_slot):
        levels, rows, width = field.shape
        _, waves, steps = legendre.shape
        tiles = width // LANES
        own = waves // n_lat
        n, half = n_lat * n_lev, n_lat // 2
        owners = half * n_lev
        rep = n_lev // (waves // half)
        lv = levels // rep
        pairs = waves * levels
        table = jnp.asarray(lon_table(waves))
        vmem, dma = pltpu.VMEM, pltpu.SemaphoreType.DMA
        anywhere = pl.BlockSpec(memory_space=pltpu.HBM)
        in_vmem = pl.BlockSpec(memory_space=pltpu.VMEM)
        adv, synth, wide, spec = pl.pallas_call(
            functools.partial(kernel, n_lat, n_lev),
            out_shape=(
                vmem((levels * rows, width), F32),
                vmem((rows, 2 * pairs), F32),
                vmem((2, 2 * pairs, width), BF16),
                vmem((own, 2, 2, steps), F32),
            ),
            in_specs=[pl.BlockSpec(memory_space=pltpu.SMEM)] + [anywhere] * 6,
            out_specs=(in_vmem,) * 4,
            scratch_shapes=[
                vmem((levels, tiles + 2, rows + 16, LANES), F32),
                vmem((4, levels, tiles, rows + 16, LANES), F32),
                vmem((4, rows, width), BF16),
                vmem((rows, width), jnp.int32),
                vmem((rows, width), jnp.int32),
                vmem((rows * waves, steps), BF16),
                vmem((4 * waves, width), BF16),
                vmem((4 * waves, width), BF16),
                vmem((2, 2 * levels, width), F32),
                vmem((2, rows, LANES), F32),
                vmem((2, 2 * levels, width), F32),
                vmem((2, rows, LANES), F32),
                vmem((4, 8, LANES), F32),
                vmem((half, -(-rows // 16) * 16, steps), BF16),
                vmem((half, HALF, steps), BF16),
                vmem((2 * pairs, LANES), F32),
                vmem((owners, lv, LANES), F32),
                vmem((n, lv, LANES), F32),
                vmem((4 * lv, half * HALF), F32),
                vmem((4 * lv, half * HALF), BF16),
                vmem((half, lv, LANES), F32),
                vmem((n, lv, LANES), F32),
                vmem((2, 2 * pairs, 4 * LANES), BF16),
                vmem((lv, 2, steps), F32),
                vmem((own, 2, 2, steps), F32),
                dma((tiles + 5,)),
                dma((8,)), dma((8,)),
                dma((half,)), dma((half,)),
                dma((n,)), dma((n,)),
                dma((n,)), dma((n,)),
                dma((lv,)), dma((own, 2)),
            ],
            compiler_params=pltpu.CompilerParams(
                collective_id=0, has_side_effects=True, vmem_limit_bytes=40 << 20
            ),
        )(
            wave_slot,
            *(
                pltpu.with_memory_space_constraint(x, pltpu.HBM)
                for x in (
                    field, weights, depart_row, depart_col,
                    legendre.reshape(rows * waves, steps), table,
                )
            ),
        )
        chunks = width // min(width, 256)
        updated, spectral = pl.pallas_call(
            finish,
            out_shape=(
                jax.ShapeDtypeStruct((levels, rows, width), F32),
                jax.ShapeDtypeStruct((own, 2, 2, steps), F32),
            ),
            in_specs=[in_vmem] * 4,
            out_specs=(anywhere,) * 2,
            scratch_shapes=[
                vmem((levels * rows, 2 * pairs), BF16),
                vmem((levels * rows, 2 * pairs), BF16),
                vmem((levels, rows, width), F32),
                dma((1 + chunks,)),
            ],
            compiler_params=pltpu.CompilerParams(vmem_limit_bytes=20 << 20),
        )(*(pltpu.with_memory_space_constraint(x, vmem) for x in (adv, synth, wide, spec)))
        return updated, spectral.reshape(own, 2, 1, 2, steps)

    placed = (
        P(None, "lat", "lev"),
        P(None, "lat", "lev"),
        P("lat", "lev"),
        P("lat", "lev"),
        P("lat", None, None),
        P(),
    )
    return jax.shard_map(
        on_device,
        mesh=mesh,
        in_specs=placed,
        out_specs=(P(None, "lat", "lev"), P("lat", None, "lev", None, None)),
        check_vma=False,
    )
```

```python
import functools
import math

import jax
import jax.numpy as jnp
import numpy as np
from jax import lax
from jax.experimental import pallas as pl
from jax.experimental.pallas import tpu as pltpu
from jax.sharding import PartitionSpec as P

NLON = 4096
NT = 1279
DAMPING = 4.0
LANES = 128
HALF = 64
MESH = pl.DeviceIdType.MESH
F32 = jnp.float32
BF16 = jnp.bfloat16


def lon_table(waves):
    m = (np.arange(waves, dtype=np.int64) * (NT + 1)) // waves
    phases = (m[:, None] * np.arange(NLON, dtype=np.int64)[None, :]) % NLON
    angles = phases.astype(np.float64) * (2.0 * math.pi / NLON)
    table = np.concatenate([np.cos(angles), -np.sin(angles)], axis=0) / math.sqrt(NLON)
    table = table.astype(np.float32)
    lead = table.astype(BF16)
    rest = (table - lead.astype(np.float32)).astype(BF16)
    return np.concatenate([lead, rest], axis=0)


def each(start, stop):
    def run(body):
        if stop - start <= 64:
            for i in range(start, stop):
                body(i)
        else:
            lax.fori_loop(start, stop, lambda i, carry: (body(i), carry)[1], 0)

    return run


def one_hot(mask):
    return jnp.where(mask, 1.0, 0.0).astype(BF16)


def kernel(
    n_lat, n_lev,
    slot_hbm, field_hbm, weights_hbm, drow_hbm, dcol_hbm, leg_hbm, table_hbm,
    adv, synth, wide, spec_ref,
    slot_ref, ext, shifted, wts, drow, dcol, leg, tab, tabs,
    pack_row, pack_col, got_row, got_col, got_corner,
    send_leg, basis, stage, send_1, got_1, both_f, both_b, send_2, got_2, cross, send_p, got_p,
    load_sem, halo_send, halo_recv, leg_send, leg_recv, one_send, one_recv,
    two_send, two_recv, p_send, p_recv,
):
    levels, _, _, _ = ext.shape
    rows, width = drow.shape
    tiles = width // LANES
    steps = leg.shape[1]
    waves = leg.shape[0] // rows
    n = n_lat * n_lev
    half = n_lat // 2
    group = waves // half
    rep = n_lev // group
    lv = levels // rep
    own = waves // n_lat
    l, e = lax.axis_index("lat"), lax.axis_index("lev")
    me = l * n_lev + e
    parity, lh = lax.div(l, half), lax.rem(l, half)
    share = lax.rem(e, rep)
    slot = group * lh + lax.div(e, rep)
    has_up, has_down = l > 0, l < n_lat - 1
    east, west = lax.rem(e + 1, n_lev), lax.rem(e + n_lev - 1, n_lev)

    def device(off):
        d = lax.rem(me + off, n)
        return lax.div(d, n_lev), lax.rem(d, n_lev)

    loads = []

    def load(src, dst):
        copy = pltpu.make_async_copy(src, dst, load_sem.at[len(loads)])
        copy.start()
        loads.append(copy)

    for t in range(tiles):
        load(
            field_hbm.at[:, :, pl.ds(t * LANES, LANES)],
            ext.at[:, t + 1, pl.ds(8, rows), :],
        )
    load(weights_hbm, wts)
    load(drow_hbm, drow)
    load(dcol_hbm, dcol)
    load(table_hbm.at[:, pl.ds(pl.multiple_of(e * width, LANES), width)], tab)
    load(leg_hbm, leg)
    load(slot_hbm, slot_ref)

    barrier = pltpu.get_barrier_semaphore()

    @each(1, n)
    def _(off):
        lat, lev = device(off)
        pl.semaphore_signal(barrier, inc=1, device_id=(lat, lev), device_id_type=MESH)

    lane = lax.broadcasted_iota(jnp.int32, (rows, LANES), 1)
    for t in range(tiles):
        loads[t].wait()
    for v in range(levels):
        for t in range(tiles):
            cols = slice(t * LANES, (t + 1) * LANES)
            pack_row[0, 2 * v : 2 * v + 2, cols] = ext[v, t + 1, 6 + rows : 8 + rows, :]
            pack_row[1, 2 * v : 2 * v + 2, cols] = ext[v, t + 1, 8:10, :]
    last = jnp.zeros((rows, LANES), F32)
    first = jnp.zeros((rows, LANES), F32)
    for v in range(levels):
        here = (lane == 2 * v) | (lane == 2 * v + 1)
        tail = pltpu.roll(ext[v, tiles, 8 : 8 + rows, :], (2 * v + 2) % LANES, 1)
        last = jnp.where(here, tail, last)
        head = ext[v, 1, 8 : 8 + rows, :]
        if v:
            head = pltpu.roll(head, 2 * v, 1)
        first = jnp.where(here, head, first)
    pack_col[0] = last
    pack_col[1] = first

    def shift_block(v, t, row0, size, moves=(-2, -1, 1, 2)):
        at = pl.ds(row0, size)
        at_lane = lax.broadcasted_iota(jnp.int32, (size, LANES), 1)
        here = ext[v, t + 1, at, :]
        left = ext[v, t, at, :] if min(moves) < 0 else None
        right = ext[v, t + 2, at, :] if max(moves) > 0 else None
        for move in moves:
            n_move = (-2, -1, 1, 2).index(move)
            amount = (-move) % LANES
            mine = pltpu.roll(here, amount, 1)
            if move < 0:
                moved = jnp.where(at_lane < -move, pltpu.roll(left, amount, 1), mine)
            else:
                moved = jnp.where(at_lane >= LANES - move, pltpu.roll(right, amount, 1), mine)
            shifted[n_move, v, t, at, :] = moved

    def shift_inner(chosen):
        def step(t, carry):
            for v in chosen:
                shift_block(v, t, 8, rows)
            return carry

        lax.fori_loop(1, tiles - 1, step, 0)

    groups = rows // 8

    def advect(t, chosen):
        cols = pl.ds(pl.multiple_of(t * LANES, LANES), LANES)
        corner = [wts[ab, :, cols].astype(F32) for ab in range(4)]
        for g in chosen:
            band = slice(8 * g, 8 * g + 8)
            dr, dc = drow[band, cols], dcol[band, cols]
            zero = jnp.zeros((8, LANES), F32)
            in_col = {c: dc == c for c in range(-2, 2)}
            in_row = {r: dr == r for r in range(-2, 2)}

            def pick(masks, at, one, two):
                value = zero
                if at - 1 in masks:
                    value = jnp.where(masks[at - 1], two, value)
                if at in masks:
                    value = jnp.where(masks[at], one, value)
                return value

            part = [
                [pick(in_col, c, corner[2 * a][band], corner[2 * a + 1][band]) for c in range(-2, 3)]
                for a in range(2)
            ]
            coef = [
                [pick(in_row, r, part[0][c], part[1][c]) for c in range(5)] for r in range(-2, 3)
            ]
            for v in range(levels):
                total = None
                for r in range(5):
                    at = pl.ds(8 * g + 6 + r, 8)
                    for c in range(5):
                        if c == 2:
                            value = ext[v, t + 1, at, :]
                        else:
                            value = shifted[c if c < 2 else c - 1, v, t, at, :]
                        term = coef[r][c] * value
                        total = term if total is None else total + term
                adv[v * rows + 8 * g : v * rows + 8 * g + 8, cols] = total

    def advect_inner(t, carry):
        advect(t, range(1, groups - 1))
        return carry

    pl.semaphore_wait(barrier, n - 1)

    def remote(src, dst, ssem, rsem, lat, lev):
        return pltpu.make_async_remote_copy(
            src_ref=src, dst_ref=dst, send_sem=ssem, recv_sem=rsem,
            device_id=(lat, lev), device_id_type=MESH,
        )

    def halo(n, src, dst, lat, lev):
        return remote(src, dst, halo_send.at[n], halo_recv.at[n], lat, lev)

    bottom, top = pl.ds(rows - 8, 8), pl.ds(0, 8)
    flat = [
        halo(0, pack_col.at[0], got_col.at[0], l, east),
        halo(1, pack_col.at[1], got_col.at[1], l, west),
    ]
    below = [
        halo(2, pack_row.at[0], got_row.at[0], l + 1, e),
        halo(3, pack_col.at[0, bottom], got_corner.at[0], l + 1, east),
        halo(4, pack_col.at[1, bottom], got_corner.at[1], l + 1, west),
    ]
    above = [
        halo(5, pack_row.at[1], got_row.at[1], l - 1, e),
        halo(6, pack_col.at[0, top], got_corner.at[2], l - 1, east),
        halo(7, pack_col.at[1, top], got_corner.at[3], l - 1, west),
    ]

    @pl.when(has_down)
    def _():
        for copy in below:
            copy.start()

    @pl.when(has_up)
    def _():
        for copy in above:
            copy.start()

    for copy in flat:
        copy.start()

    loads[tiles + 5].wait()
    first = lax.broadcasted_iota(jnp.int32, (1, 4 * waves), 1)
    slot_row = jnp.zeros((1, 4 * waves), jnp.int32)
    for k in range(waves):
        slot_row = jnp.where(lax.rem(first, waves) == k, slot_ref[k], slot_row)
    at = lambda shape, dim: lax.broadcasted_iota(jnp.int32, shape, dim)
    iota_f = (4 * waves, 4 * waves)
    order = one_hot(
        (lax.div(at(iota_f, 0), waves) == lax.div(at(iota_f, 1), waves))
        & (lax.rem(at(iota_f, 0), waves) == slot_row)
    )
    stage[...] = jnp.zeros_like(stage)
    cross[...] = jnp.zeros_like(cross)
    padded = send_leg.shape[1]
    basis[:, padded:, :] = jnp.zeros((half, HALF - padded, steps), BF16)

    shift_inner(range(levels))
    if tiles > 1:
        for v in range(levels):
            shift_block(v, 0, 8, rows, (1, 2))
            shift_block(v, tiles - 1, 8, rows, (-2, -1))
    for t in range(tiles, tiles + 3):
        loads[t].wait()
    lax.fori_loop(1, tiles - 1, advect_inner, 0)

    loads[tiles + 4].wait()
    send_leg[...] = jnp.zeros_like(send_leg)
    band = 8
    iota_g = (half * band, band * waves)
    slot_cols = jnp.zeros((1, band * waves), jnp.int32)
    lane_k = lax.rem(lax.broadcasted_iota(jnp.int32, (1, band * waves), 1), waves)
    for k in range(waves):
        slot_cols = jnp.where(lane_k == k, slot_ref[k], slot_cols)
    choose = one_hot(
        (lax.rem(at(iota_g, 0), band) == lax.div(at(iota_g, 1), waves))
        & (group * lax.div(at(iota_g, 0), band) + lax.div(e, rep) == slot_cols)
    )
    for i in range(0, rows, band):
        picked = jnp.dot(
            choose, leg[i * waves : (i + band) * waves, :], preferred_element_type=F32
        ).astype(BF16)
        for t in range(half):
            send_leg[t, i : i + band, :] = picked[t * band : (t + 1) * band]
    slots_of = lambda t: basis.at[t, pl.ds(0, padded), :]
    copies_g = []
    for off in range(1, half):
        t = lax.rem(lh + off, half)
        copy = remote(
            send_leg.at[t], slots_of(lh), leg_send, leg_recv,
            parity * half + t, e,
        )
        copy.start()
        copies_g.append(copy)
    basis[lh, 0:padded, :] = send_leg[lh]

    loads[tiles + 3].wait()
    tabs[...] = jnp.dot(order, tab[...], preferred_element_type=F32).astype(BF16)


    def spread(piece, v):
        return pltpu.roll(piece, LANES - 2 - 2 * v, 1)

    def spread_east(piece, v):
        return pltpu.roll(piece, LANES - 2 * v, 1) if v else piece

    def rim(row0, size, from_west, from_east):
        for v in range(levels):
            ext[v, 0, row0 : row0 + size, :] = spread(from_west, v)
            ext[v, tiles + 1, row0 : row0 + size, :] = spread_east(from_east, v)

    def fill_rows(which, row0):
        for v in range(levels):
            for t in range(tiles):
                cols = slice(t * LANES, (t + 1) * LANES)
                ext[v, t + 1, row0 : row0 + 2, :] = got_row[which, 2 * v : 2 * v + 2, cols]

    @pl.when(has_up)
    def _():
        for copy in below:
            copy.wait_recv()
        fill_rows(0, 6)
        rim(0, 8, got_corner[0], got_corner[1])

    @pl.when(jnp.logical_not(has_up))
    def _():
        ext[:, :, 0:8, :] = jnp.zeros((levels, tiles + 2, 8, LANES), F32)

    @pl.when(has_down)
    def _():
        for copy in above:
            copy.wait_recv()
        fill_rows(1, rows + 8)
        rim(rows + 8, 8, got_corner[2], got_corner[3])

    @pl.when(jnp.logical_not(has_down))
    def _():
        ext[:, :, rows + 8 : rows + 16, :] = jnp.zeros((levels, tiles + 2, 8, LANES), F32)

    for copy in flat:
        copy.wait_recv()
    rim(8, rows, got_col[0], got_col[1])

    def shift_rims(t, carry):
        for v in range(levels):
            shift_block(v, t, 0, 8)
            shift_block(v, t, rows + 8, 8)
        return carry

    edges = min(tiles, 2)
    for v in range(levels):
        shift_block(v, 0, 8, rows, (-2, -1))
        shift_block(v, tiles - 1, 8, rows, (1, 2))
    lax.fori_loop(0, tiles, shift_rims, 0)
    outer = sorted({0, groups - 1})

    def advect_rims(t, carry):
        advect(t, outer)
        return carry

    def advect_edge(n, carry):
        advect(n * (tiles - 1), range(groups))
        return carry

    lax.fori_loop(0, edges, advect_edge, 0)
    lax.fori_loop(1, tiles - 1, advect_rims, 0)

    contract_last = (((1,), (1,)), ((), ()))
    for v in range(levels):
        value = adv[v * rows : (v + 1) * rows, :]
        lead = value.astype(BF16)
        rest = (value - lead.astype(F32)).astype(BF16)
        both = lax.dot_general(tabs[...], lead, contract_last, preferred_element_type=F32)
        more = lax.dot_general(
            tabs[0 : 2 * waves, :], rest, contract_last, preferred_element_type=F32
        )
        coeffs = both[0 : 2 * waves] + both[2 * waves :] + more
        stage[v * waves : (v + 1) * waves, 0:rows] = coeffs[0:waves]
        stage[v * waves : (v + 1) * waves, HALF : HALF + rows] = coeffs[waves:]
    owners = half * n_lev
    for s in range(waves):
        for g in range(rep):
            send_1[s * rep + g] = stage[pl.ds(g * lv * waves + s, lv, stride=waves), :]

    def copy_1(off):
        lat, lev = device(off)
        owner = lax.rem(lat, half) * n_lev + lev
        return remote(
            send_1.at[owner], got_1.at[me], one_send, one_recv, lat, lev
        )

    @each(1, n)
    def _(off):
        copy_1(off).start()

    got_1[me] = send_1[lh * n_lev + e]

    spread_rows = 2 * waves * levels
    iota_w = (spread_rows, 2 * waves)
    repeat = one_hot(lax.div(at(iota_w, 0), levels) == at(iota_w, 1))
    for q in range(2):
        wide[q] = jnp.dot(
            repeat, tabs[2 * waves * q : 2 * waves * (q + 1), :], preferred_element_type=F32
        ).astype(BF16)

    at_row, at_col = at((LANES, LANES), 0), at((LANES, LANES), 1)
    flip = one_hot(
        ((at_row + at_col == rows - 1) & (at_row < HALF) & (at_col < HALF))
        | ((at_row + at_col == 2 * HALF + rows - 1) & (at_row >= HALF) & (at_col >= HALF))
    )
    sign = jnp.where(parity == 0, 1.0, -1.0).astype(F32)
    iota_e = (rows, 4 * LANES)
    row_e, col_e = at(iota_e, 0), at(iota_e, 1)
    part_e, lane_e = lax.div(col_e, LANES), lax.rem(col_e, LANES)
    place = HALF * lax.div(part_e, 2)
    natural = (lax.rem(part_e, 2) == 1) & (lane_e == row_e + place)
    turned = (lax.rem(part_e, 2) == 0) & (lane_e == rows - 1 - row_e + place)
    gather = (jnp.where(natural, sign, 0.0) + jnp.where(turned, 1.0, 0.0)).astype(BF16)

    wave_own = jnp.int32(0)
    for k in range(waves):
        wave_own = jnp.where(slot_ref[k] == slot, k, wave_own)
    wave_own = wave_own * (NT + 1) // waves
    column = lax.broadcasted_iota(jnp.int32, (2 * lv, steps), 1)
    degree = wave_own + 2 * column + parity
    factor = 1.0 / (
        1.0 + DAMPING * (degree * (degree + 1)).astype(F32) / float(NT * (NT + 1))
    )
    forward_scale = 1.0 / math.sqrt(rows * n_lat // 2)
    inverse_scale = math.sqrt(NLON) / math.sqrt(waves) / math.sqrt(steps)
    scale = jnp.where(wave_own == 0, inverse_scale, 2.0 * inverse_scale).astype(F32)

    legs = send_leg.at[pl.ds(0, half - 1)]
    pltpu.make_async_copy(legs, legs, leg_recv).wait()

    def all_of(ref, sem, count=n - 1):
        return pltpu.make_async_copy(ref.at[pl.ds(0, count)], ref.at[pl.ds(0, count)], sem)

    all_of(got_1, one_recv).wait()

    low = lax.broadcasted_iota(jnp.int32, (lv, LANES), 1) < HALF

    def total_1(lat):
        value = got_1[lat * n_lev]
        for d in range(1, n_lev):
            value = value + got_1[lat * n_lev + d]
        return value

    for b in range(0, half, 2):
        cols = slice(b * HALF, b * HALF + LANES)
        for which in range(2):
            lat = parity * half + b
            one = total_1(lat if which == 0 else n_lat - 1 - lat)
            two = total_1(lat + 1 if which == 0 else n_lat - 2 - lat)
            row0 = which * 2 * lv
            both_f[row0 : row0 + lv, cols] = jnp.where(low, one, pltpu.roll(two, HALF, 1))
            both_f[row0 + lv : row0 + 2 * lv, cols] = jnp.where(
                low, pltpu.roll(one, HALF, 1), two
            )
    near = both_f[0 : 2 * lv, :].astype(BF16)
    both_b[0 : 2 * lv, :] = near
    for c0 in range(0, half * HALF, LANES):
        cols = slice(c0, c0 + LANES)
        both_b[2 * lv :, cols] = jnp.dot(
            both_f[2 * lv :, cols].astype(BF16), flip, preferred_element_type=F32
        ).astype(BF16)
    matrix = basis[...].reshape(half * HALF, steps)
    raw = jnp.dot(both_b[...], matrix, preferred_element_type=F32)
    raw = (raw[2 * lv :] + sign * raw[0 : 2 * lv]) * forward_scale
    masked = jnp.where(degree <= NT, raw, 0.0)
    damped = masked * factor
    change = (damped - masked).astype(BF16)
    back = lax.dot_general(change, matrix, contract_last, preferred_element_type=F32) * scale
    both_f[0 : 2 * lv, :] = back
    for b in range(0, half, 2):
        cols = slice(b * HALF, b * HALF + LANES)
        real, imag = both_f[0:lv, cols], both_f[lv : 2 * lv, cols]
        send_2[b] = jnp.where(low, real, pltpu.roll(imag, HALF, 1))
        send_2[b + 1] = jnp.where(low, pltpu.roll(real, HALF, 1), imag)

    def copy_2(off):
        lat, lev = device(off)
        inside = lax.div(lat, half) == parity
        block = jnp.where(inside, lat, n_lat - 1 - lat) - parity * half
        return remote(
            send_2.at[block], got_2.at[me], two_send, two_recv, lat, lev
        )

    @each(1, n)
    def _(off):
        copy_2(off).start()

    got_2[me] = send_2[lh]

    for vv in range(lv):
        for c in range(2):
            send_p[vv, c : c + 1, :] = damped[c * lv + vv : c * lv + vv + 1]
    home, place_p = lax.div(slot, own), lax.rem(slot, own)
    for vv in range(lv):
        lev = share * lv + vv
        mine = (home == l) & (lev == e)
        copy = remote(
            send_p.at[vv], got_p.at[2 * place_p + parity], p_send, p_recv, home, lev
        )
        pl.when(jnp.logical_not(mine))(copy.start)

        @pl.when(mine)
        def _():
            got_p[2 * place_p + parity] = send_p[vv]

    all_of(got_2, two_recv).wait()

    pairs = waves * levels
    for which in range(2):
        start = jnp.where(which == 1, parity, 1 - parity) * owners
        for o in range(owners):
            stage[which * pairs + o * lv : which * pairs + (o + 1) * lv, :] = got_2[start + o]
    for which in range(2):
        value = stage[which * pairs : (which + 1) * pairs, :]
        lead = value.astype(BF16)
        rest = (value - lead.astype(F32)).astype(BF16)
        for c in range(2):
            cols = slice((2 * c + which) * LANES, (2 * c + which + 1) * LANES)
            cross[0, c * pairs : (c + 1) * pairs, cols] = lead
            cross[1, c * pairs : (c + 1) * pairs, cols] = rest
    synth[...] = lax.dot_general(
        gather, cross[0], contract_last, preferred_element_type=F32
    ) + lax.dot_general(gather, cross[1], contract_last, preferred_element_type=F32)

    keeps = (home == l) & (share == lax.div(e, lv))
    spec_waits = [
        (keeps, all_of(got_p, p_recv, 2 * own - 1)),
        (jnp.logical_not(keeps), all_of(got_p, p_recv, 2 * own)),
    ]
    for case, copy in spec_waits:
        pl.when(case)(copy.wait)
    for k in range(2 * own):
        spec_ref[k] = got_p[k]

    for copy in flat:
        copy.wait_send()
    pltpu.make_async_copy(legs, legs, leg_send).wait()
    all_of(got_1, one_send).wait()
    all_of(got_2, two_send).wait()
    pl.when(keeps)(all_of(send_p, p_send, lv - 1).wait)
    pl.when(jnp.logical_not(keeps))(all_of(send_p, p_send, lv).wait)

    @pl.when(has_down)
    def _():
        for copy in below:
            copy.wait_send()

    @pl.when(has_up)
    def _():
        for copy in above:
            copy.wait_send()


def finish(adv, synth, wide, spec, out_hbm, spec_hbm, lead_all, rest_all, result, sems):
    levels, rows, width = result.shape
    spec_copy = pltpu.make_async_copy(spec, spec_hbm, sems.at[0])
    spec_copy.start()
    value = synth[...]
    lead = value.astype(BF16).astype(F32)
    rest = value - lead
    level_of = lax.rem(lax.broadcasted_iota(jnp.int32, value.shape, 1), levels)
    for v in range(levels):
        at = slice(v * rows, (v + 1) * rows)
        lead_all[at, :] = jnp.where(level_of == v, lead, 0.0).astype(BF16)
        rest_all[at, :] = jnp.where(level_of == v, rest, 0.0).astype(BF16)
    chunk = min(width, 256)
    copies = []
    for j in range(0, width, chunk):
        cols = slice(j, j + chunk)
        increment = (
            jnp.dot(lead_all[...], wide[0, :, cols], preferred_element_type=F32)
            + jnp.dot(lead_all[...], wide[1, :, cols], preferred_element_type=F32)
            + jnp.dot(rest_all[...], wide[0, :, cols], preferred_element_type=F32)
        )
        updated = adv[:, cols] + increment
        for v in range(levels):
            result[v, :, cols] = updated[v * rows : (v + 1) * rows]
        copy = pltpu.make_async_copy(
            result.at[:, :, cols], out_hbm.at[:, :, cols], sems.at[1 + j // chunk]
        )
        copy.start()
        copies.append(copy)
    for copy in copies + [spec_copy]:
        copy.wait()


def solution(mesh):
    n_lat, n_lev = mesh.shape["lat"], mesh.shape["lev"]

    def on_device(field, weights, depart_row, depart_col, legendre, wave_slot):
        levels, rows, width = field.shape
        _, waves, steps = legendre.shape
        tiles = width // LANES
        own = waves // n_lat
        n, half = n_lat * n_lev, n_lat // 2
        owners = half * n_lev
        rep = n_lev // (waves // half)
        lv = levels // rep
        pairs = waves * levels
        table = jnp.asarray(lon_table(waves))
        vmem, dma = pltpu.VMEM, pltpu.SemaphoreType.DMA
        anywhere = pl.BlockSpec(memory_space=pltpu.HBM)
        in_vmem = pl.BlockSpec(memory_space=pltpu.VMEM)
        adv, synth, wide, spec = pl.pallas_call(
            functools.partial(kernel, n_lat, n_lev),
            out_shape=(
                vmem((levels * rows, width), F32),
                vmem((rows, 2 * pairs), F32),
                vmem((2, 2 * pairs, width), BF16),
                vmem((2 * own, 2, steps), F32),
            ),
            in_specs=[anywhere] * 7,
            out_specs=(in_vmem,) * 4,
            scratch_shapes=[
                pltpu.SMEM((waves,), jnp.int32),
                vmem((levels, tiles + 2, rows + 16, LANES), F32),
                vmem((4, levels, tiles, rows + 16, LANES), F32),
                vmem((4, rows, width), BF16),
                vmem((rows, width), jnp.int32),
                vmem((rows, width), jnp.int32),
                vmem((rows * waves, steps), BF16),
                vmem((4 * waves, width), BF16),
                vmem((4 * waves, width), BF16),
                vmem((2, 2 * levels, width), F32),
                vmem((2, rows, LANES), F32),
                vmem((2, 2 * levels, width), F32),
                vmem((2, rows, LANES), F32),
                vmem((4, 8, LANES), F32),
                vmem((half, -(-rows // 16) * 16, steps), BF16),
                vmem((half, HALF, steps), BF16),
                vmem((2 * pairs, LANES), F32),
                vmem((owners, lv, LANES), F32),
                vmem((n, lv, LANES), F32),
                vmem((4 * lv, half * HALF), F32),
                vmem((4 * lv, half * HALF), BF16),
                vmem((half, lv, LANES), F32),
                vmem((n, lv, LANES), F32),
                vmem((2, 2 * pairs, 4 * LANES), BF16),
                vmem((lv, 2, steps), F32),
                vmem((2 * own, 2, steps), F32),
                dma((tiles + 6,)),
                dma((8,)), dma((8,)),
                dma, dma,
                dma, dma,
                dma, dma,
                dma, dma,
            ],
            compiler_params=pltpu.CompilerParams(
                collective_id=0, has_side_effects=True, vmem_limit_bytes=40 << 20
            ),
        )(
            *(
                pltpu.with_memory_space_constraint(x, pltpu.HBM)
                for x in (
                    wave_slot, field, weights, depart_row, depart_col,
                    legendre.reshape(rows * waves, steps), table,
                )
            ),
        )
        chunks = width // min(width, 256)
        updated, spectral = pl.pallas_call(
            finish,
            out_shape=(
                jax.ShapeDtypeStruct((levels, rows, width), F32),
                jax.ShapeDtypeStruct((2 * own, 2, steps), F32),
            ),
            in_specs=[in_vmem] * 4,
            out_specs=(anywhere,) * 2,
            scratch_shapes=[
                vmem((levels * rows, 2 * pairs), BF16),
                vmem((levels * rows, 2 * pairs), BF16),
                vmem((levels, rows, width), F32),
                dma((1 + chunks,)),
            ],
            compiler_params=pltpu.CompilerParams(vmem_limit_bytes=20 << 20),
        )(*(pltpu.with_memory_space_constraint(x, vmem) for x in (adv, synth, wide, spec)))
        return updated, spectral.reshape(own, 2, 1, 2, steps)

    placed = (
        P(None, "lat", "lev"),
        P(None, "lat", "lev"),
        P("lat", "lev"),
        P("lat", "lev"),
        P("lat", None, None),
        P(),
    )
    return jax.shard_map(
        on_device,
        mesh=mesh,
        in_specs=placed,
        out_specs=(P(None, "lat", "lev"), P("lat", None, "lev", None, None)),
        check_vma=False,
    )
```

```python
import functools
import math

import jax
import jax.numpy as jnp
import numpy as np
from jax import lax
from jax.experimental import pallas as pl
from jax.experimental.pallas import tpu as pltpu
from jax.sharding import PartitionSpec as P

NLON = 4096
NT = 1279
DAMPING = 4.0
LANES = 128
HALF = 64
MESH = pl.DeviceIdType.MESH
F32 = jnp.float32
BF16 = jnp.bfloat16


def lon_table(waves):
    m = (np.arange(waves, dtype=np.int64) * (NT + 1)) // waves
    phases = (m[:, None] * np.arange(NLON, dtype=np.int64)[None, :]) % NLON
    angles = phases.astype(np.float64) * (2.0 * math.pi / NLON)
    table = np.concatenate([np.cos(angles), -np.sin(angles)], axis=0) / math.sqrt(NLON)
    table = table.astype(np.float32)
    lead = table.astype(BF16)
    rest = (table - lead.astype(np.float32)).astype(BF16)
    return np.concatenate([lead, rest], axis=0)


def each(start, stop):
    def run(body):
        if stop - start <= 64:
            for i in range(start, stop):
                body(i)
        else:
            lax.fori_loop(start, stop, lambda i, carry: (body(i), carry)[1], 0)

    return run


def one_hot(mask):
    return jnp.where(mask, 1.0, 0.0).astype(BF16)


def kernel(
    n_lat, n_lev,
    slot_hbm, field_hbm, weights_hbm, drow_hbm, dcol_hbm, leg_hbm, table_hbm,
    adv, synth, wide, spec_ref,
    slot_ref, ext, shifted, points, drow, dcol, leg, tab, tabs,
    pack_row, pack_col, got_rim, got_col, rim_points, side_points, side,
    send_leg, basis, stage, send_1, got_1, both_f, both_b, send_2, got_2, cross, send_p, got_p,
    load_sem, halo_send, halo_recv, leg_send, leg_recv, one_send, one_recv,
    two_send, two_recv, p_send, p_recv,
):
    levels, _, _, _ = ext.shape
    rows, width = drow.shape
    tiles = width // LANES
    steps = leg.shape[1]
    waves = leg.shape[0] // rows
    n = n_lat * n_lev
    half = n_lat // 2
    group = waves // half
    rep = n_lev // group
    lv = levels // rep
    own = waves // n_lat
    l, e = lax.axis_index("lat"), lax.axis_index("lev")
    me = l * n_lev + e
    parity, lh = lax.div(l, half), lax.rem(l, half)
    share = lax.rem(e, rep)
    slot = group * lh + lax.div(e, rep)
    has_up, has_down = l > 0, l < n_lat - 1
    east, west = lax.rem(e + 1, n_lev), lax.rem(e + n_lev - 1, n_lev)

    def device(off):
        d = lax.rem(me + off, n)
        return lax.div(d, n_lev), lax.rem(d, n_lev)

    def load(k, src, dst):
        copy = pltpu.make_async_copy(src, dst, load_sem.at[k])
        copy.start()
        return copy

    for t in range(tiles):
        load(0, field_hbm.at[:, :, pl.ds(t * LANES, LANES)], ext.at[:, t, pl.ds(8, rows), :])
    load_leg = load(1, leg_hbm, leg)
    load_slot = load(2, slot_hbm, slot_ref)
    load_wts = load(3, weights_hbm, points.at[pl.ds(0, 4 * rows), :])
    load_row = load(4, drow_hbm, drow)
    load_col = load(5, dcol_hbm, dcol)
    load_tab = load(
        6, table_hbm.at[:, pl.ds(pl.multiple_of(e * width, LANES), width)], tab
    )

    barrier = pltpu.get_barrier_semaphore()

    @each(1, n)
    def _(off):
        lat, lev = device(off)
        pl.semaphore_signal(barrier, inc=1, device_id=(lat, lev), device_id_type=MESH)

    at = lambda shape, dim: lax.broadcasted_iota(jnp.int32, shape, dim)
    for row0 in (0, rows + 8):
        zero = jnp.zeros((levels, tiles, 8, LANES), F32)
        ext[:, :, row0 : row0 + 8, :] = zero
        for move in range(4):
            shifted[move, :, :, row0 : row0 + 8, :] = zero
        for k in range(2):
            side[k, row0 : row0 + 8, :] = zero[0, 0]
    stage[...] = jnp.zeros_like(stage)
    cross[...] = jnp.zeros_like(cross)
    padded = send_leg.shape[1]
    basis[:, padded:, :] = jnp.zeros((half, HALF - padded, steps), BF16)
    send_leg[:, rows:, :] = jnp.zeros((half, padded - rows, steps), BF16)

    lane = at((rows, LANES), 1)
    pltpu.make_async_copy(adv, adv, load_sem.at[0]).wait()
    for v in range(levels):
        for t in range(tiles):
            pack_row[0, t, 2 * v : 2 * v + 2, :] = ext[v, t, 6 + rows : 8 + rows, :]
            pack_row[1, t, 2 * v : 2 * v + 2, :] = ext[v, t, 8:10, :]
    last = jnp.zeros((rows, LANES), F32)
    first = jnp.zeros((rows, LANES), F32)
    for v in range(levels):
        tail = pltpu.roll(ext[v, tiles - 1, 8 : 8 + rows, :], (2 * v + 2) % LANES, 1)
        last = jnp.where(lax.div(lane, 2) == v, tail, last)
        head = pltpu.roll(ext[v, 0, 8 : 8 + rows, :], HALF + 2 * v, 1)
        first = jnp.where(lax.div(lane - HALF, 2) == v, head, first)
    pack_col[0] = last
    pack_col[1] = first

    def remote(src, dst, ssem, rsem, lat, lev):
        return pltpu.make_async_remote_copy(
            src_ref=src, dst_ref=dst, send_sem=ssem, recv_sem=rsem,
            device_id=(lat, lev), device_id_type=MESH,
        )

    def halo(k, src, dst, lat, lev):
        return remote(src, dst, halo_send.at[k], halo_recv.at[k], lat, lev)

    flat = [
        halo(2, pack_col.at[0], got_col.at[0], l, east),
        halo(2, pack_col.at[1], got_col.at[1], l, west),
    ]
    rims = [
        [
            halo(k, pack_row.at[k], got_rim.at[k, pl.ds(1, tiles)], lat, e),
            halo(k, pack_row.at[k, tiles - 1], got_rim.at[k, 0], lat, east),
            halo(k, pack_row.at[k, 0], got_rim.at[k, tiles + 1], lat, west),
        ]
        for k, lat in ((0, l + 1), (1, l - 1))
    ]

    pl.semaphore_wait(barrier, n - 1)

    @pl.when(has_down)
    def _():
        for copy in rims[0]:
            copy.start()

    @pl.when(has_up)
    def _():
        for copy in rims[1]:
            copy.start()

    for copy in flat:
        copy.start()

    load_slot.wait()
    first = lax.broadcasted_iota(jnp.int32, (1, 4 * waves), 1)
    slot_row = jnp.zeros((1, 4 * waves), jnp.int32)
    for k in range(waves):
        slot_row = jnp.where(lax.rem(first, waves) == k, slot_ref[k], slot_row)
    iota_f = (4 * waves, 4 * waves)
    order = one_hot(
        (lax.div(at(iota_f, 0), waves) == lax.div(at(iota_f, 1), waves))
        & (lax.rem(at(iota_f, 0), waves) == slot_row)
    )
    load_leg.wait()
    band = 8
    iota_g = (half * band, band * waves)
    slot_cols = jnp.zeros((1, band * waves), jnp.int32)
    lane_k = lax.rem(lax.broadcasted_iota(jnp.int32, (1, band * waves), 1), waves)
    for k in range(waves):
        slot_cols = jnp.where(lane_k == k, slot_ref[k], slot_cols)
    choose = one_hot(
        (lax.rem(at(iota_g, 0), band) == lax.div(at(iota_g, 1), waves))
        & (group * lax.div(at(iota_g, 0), band) + lax.div(e, rep) == slot_cols)
    )
    for i in range(0, rows, band):
        picked = jnp.dot(
            choose, leg[i * waves : (i + band) * waves, :], preferred_element_type=F32
        ).astype(BF16)
        for t in range(half):
            send_leg[t, i : i + band, :] = picked[t * band : (t + 1) * band]
    slots_of = lambda t: basis.at[t, pl.ds(0, padded), :]
    copies_g = []
    for off in range(1, half):
        t = lax.rem(lh + off, half)
        copy = remote(
            send_leg.at[t], slots_of(lh), leg_send, leg_recv,
            parity * half + t, e,
        )
        copy.start()
        copies_g.append(copy)
    basis[lh, 0:padded, :] = send_leg[lh]

    lane = at((8, LANES), 1)
    moves = (-2, -1, 1, 2)

    def move_blocks(blocks, move):
        turned = [x if x is None else pltpu.roll(x, (-move) % LANES, 1) for x in blocks]
        zero = jnp.zeros((8, LANES), F32)
        result = []
        for t in range(1, len(blocks) - 1):
            near = turned[t - 1] if move < 0 else turned[t + 1]
            wrapped = (lane < -move) if move < 0 else (lane >= LANES - move)
            result.append(jnp.where(wrapped, zero if near is None else near, turned[t]))
        return result

    groups = rows // 8

    def shift_level(v, carry):
        for g in range(groups):
            band = slice(8 + 8 * g, 16 + 8 * g)
            blocks = [None] + [ext[v, t, band, :] for t in range(tiles)] + [None]
            for k, move in enumerate(moves):
                for t, value in enumerate(move_blocks(blocks, move)):
                    shifted[k, v, t, band, :] = value
        return carry

    lax.fori_loop(0, levels, shift_level, 0)

    def choose_two(high, low, values):
        one = jnp.where(high, values[2], values[0])
        two = jnp.where(high, values[3], values[1])
        three = jnp.where(high, values[4], values[2])
        return jnp.where(low, two, one), jnp.where(low, three, two)

    load_wts.wait()
    load_row.wait()
    load_col.wait()

    def advect(t, carry):
        cols = pl.ds(pl.multiple_of(t * LANES, LANES), LANES)
        corner = [points[k * rows : (k + 1) * rows, cols].astype(F32) for k in range(4)]
        for g in range(groups):
            band = slice(8 * g, 8 * g + 8)
            dr, dc = drow[band, cols], dcol[band, cols]
            row_high, row_low = dr >= 0, (dr & 1) == 1
            col_high, col_low = dc >= 0, (dc & 1) == 1
            w = [corner[k][band] for k in range(4)]
            for v in range(levels):
                picked = []
                for c in range(5):
                    ref = ext.at[v, t] if c == 2 else shifted.at[c if c < 2 else c - 1, v, t]
                    picked.append(
                        choose_two(
                            row_high, row_low,
                            [ref[8 * g + 6 + r : 8 * g + 14 + r, :] for r in range(5)],
                        )
                    )
                upper = choose_two(col_high, col_low, [x[0] for x in picked])
                lower = choose_two(col_high, col_low, [x[1] for x in picked])
                total = w[0] * upper[0] + w[1] * upper[1] + w[2] * lower[0] + w[3] * lower[1]
                adv[v * rows + 8 * g : v * rows + 8 * g + 8, cols] = total
        return carry

    lax.fori_loop(0, tiles, advect, 0)

    load_tab.wait()
    tabs[...] = jnp.dot(order, tab[...], preferred_element_type=F32).astype(BF16)

    points[4 * rows : 5 * rows, :] = drow[...].astype(F32).astype(BF16)
    points[5 * rows : 6 * rows, :] = dcol[...].astype(F32).astype(BF16)
    iota_r = (6 * 16, 6 * rows)
    row_r, col_r = at(iota_r, 0), at(iota_r, 1)
    odd = row_r & 1
    repeat_rows = one_hot(
        (lax.div(row_r, 16) == lax.div(col_r, rows))
        & (lax.rem(col_r, rows) == jnp.where((row_r & 15) < 8, odd, rows - 2 + odd))
    )
    rim_points[...] = jnp.dot(repeat_rows, points[...], preferred_element_type=F32)
    row_c, col_c = at((LANES, LANES), 0), at((LANES, LANES), 1)
    from_first = one_hot((col_c < HALF) & (row_c == (col_c & 1)))
    from_last = one_hot((col_c >= HALF) & (row_c == LANES - 2 + (col_c & 1)))
    side_points[...] = jnp.dot(
        points[:, 0:LANES], from_first, preferred_element_type=F32
    ) + jnp.dot(points[:, width - LANES :], from_last, preferred_element_type=F32)

    even = (at((8, LANES), 0) & 1) == 0

    def fix_rows(k):
        for c0 in range(0, 2 * levels, 8):
            blocks = [got_rim[k, t, c0 : c0 + 8, :] for t in range(tiles + 2)]
            moved = [move_blocks(blocks, move) for move in moves]
            moved.insert(2, blocks[1:-1])
            for t in range(tiles):
                cols = slice(t * LANES, (t + 1) * LANES)
                w0, w1, w2, w3, dr, dc = [
                    rim_points[16 * q + 8 * k : 16 * q + 8 * k + 8, cols] for q in range(6)
                ]
                col_high, col_low = dc >= 0.0, (dc == -1.0) | (dc == 1.0)
                same = [moved[c][t] for c in range(5)]
                other = [pltpu.roll(x, 1 if k else 7, 0) for x in same]
                s0, s1 = choose_two(col_high, col_low, same)
                o0, o1 = choose_two(col_high, col_low, other)
                if k == 0:
                    far = jnp.where(dr == -2.0, w0 * s0 + w1 * s1, 0.0)
                    near = jnp.where(
                        dr == -1.0, w0 * o0 + w1 * o1,
                        jnp.where(dr == -2.0, w2 * o0 + w3 * o1, 0.0),
                    )
                    near = jnp.where(even, near, 0.0)
                else:
                    far = jnp.where(dr == 1.0, w2 * s0 + w3 * s1, 0.0)
                    near = jnp.where(
                        dr == 1.0, w0 * o0 + w1 * o1,
                        jnp.where(dr == 0.0, w2 * o0 + w3 * o1, 0.0),
                    )
                    near = jnp.where(even, 0.0, near)
                extra = far + near
                for i in range(0, 8, 2):
                    row0 = (c0 + i) // 2 * rows + k * (rows - 2)
                    adv[row0 : row0 + 2, cols] += extra[i : i + 2]

    @pl.when(has_up)
    def _():
        pltpu.make_async_copy(got_rim.at[0], got_rim.at[0], halo_recv.at[0]).wait()
        fix_rows(0)

    @pl.when(has_down)
    def _():
        pltpu.make_async_copy(got_rim.at[1], got_rim.at[1], halo_recv.at[1]).wait()
        fix_rows(1)

    pltpu.make_async_copy(got_col, got_col, halo_recv.at[2]).wait()
    here = jnp.where(at((rows, LANES), 1) < HALF, got_col[0], got_col[1])
    side[0, 8 : 8 + rows, :] = here
    side[1, 8 : 8 + rows, :] = jnp.where(
        at((rows, LANES), 1) < HALF, pltpu.roll(here, LANES - 1, 1), pltpu.roll(here, 1, 1)
    )
    in_west = lane < HALF
    edge = jnp.where(in_west, -1.0, 1.0)
    inner = (lane & 1) == jnp.where(in_west, 0, 1)
    for g in range(groups):
        w0, w1, w2, w3, dr, dc = [
            side_points[q * rows + 8 * g : q * rows + 8 * g + 8, :] for q in range(6)
        ]
        row_high, row_low = dr >= 0.0, (dr == -1.0) | (dr == 1.0)
        s0, s1 = choose_two(
            row_high, row_low, [side[0, 8 * g + 6 + r : 8 * g + 14 + r, :] for r in range(5)]
        )
        o0, o1 = choose_two(
            row_high, row_low, [side[1, 8 * g + 6 + r : 8 * g + 14 + r, :] for r in range(5)]
        )
        far = jnp.where(
            dc == jnp.where(in_west, -2.0, 1.0),
            jnp.where(in_west, w0, w1) * s0 + jnp.where(in_west, w2, w3) * s1,
            0.0,
        )
        near = jnp.where(
            dc == edge, w0 * o0 + w2 * o1,
            jnp.where(dc == edge - 1.0, w1 * o0 + w3 * o1, 0.0),
        )
        extra = far + jnp.where(inner, near, 0.0)
        for v in range(levels):
            band = slice(v * rows + 8 * g, v * rows + 8 * g + 8)
            west_part = pltpu.roll(extra, (LANES - 2 * v) % LANES, 1) if v else extra
            adv[band, 0:LANES] += jnp.where(lane < 2, west_part, 0.0)
            east_part = pltpu.roll(extra, (LANES - 2 - HALF - 2 * v) % LANES, 1)
            adv[band, width - LANES :] += jnp.where(lane >= LANES - 2, east_part, 0.0)

    contract_last = (((1,), (1,)), ((), ()))
    for v in range(levels):
        value = adv[v * rows : (v + 1) * rows, :]
        lead = value.astype(BF16)
        rest = (value - lead.astype(F32)).astype(BF16)
        both = lax.dot_general(tabs[...], lead, contract_last, preferred_element_type=F32)
        more = lax.dot_general(
            tabs[0 : 2 * waves, :], rest, contract_last, preferred_element_type=F32
        )
        coeffs = both[0 : 2 * waves] + both[2 * waves :] + more
        stage[v * waves : (v + 1) * waves, 0:rows] = coeffs[0:waves]
        stage[v * waves : (v + 1) * waves, HALF : HALF + rows] = coeffs[waves:]
    owners = half * n_lev
    for s in range(waves):
        for g in range(rep):
            send_1[s * rep + g] = stage[pl.ds(g * lv * waves + s, lv, stride=waves), :]

    def copy_1(off):
        lat, lev = device(off)
        owner = lax.rem(lat, half) * n_lev + lev
        return remote(
            send_1.at[owner], got_1.at[me], one_send, one_recv, lat, lev
        )

    @each(1, n)
    def _(off):
        copy_1(off).start()

    got_1[me] = send_1[lh * n_lev + e]

    spread_rows = 2 * waves * levels
    iota_w = (spread_rows, 2 * waves)
    repeat = one_hot(lax.div(at(iota_w, 0), levels) == at(iota_w, 1))
    for q in range(2):
        wide[q] = jnp.dot(
            repeat, tabs[2 * waves * q : 2 * waves * (q + 1), :], preferred_element_type=F32
        ).astype(BF16)

    at_row, at_col = at((LANES, LANES), 0), at((LANES, LANES), 1)
    flip = one_hot(
        ((at_row + at_col == rows - 1) & (at_row < HALF) & (at_col < HALF))
        | ((at_row + at_col == 2 * HALF + rows - 1) & (at_row >= HALF) & (at_col >= HALF))
    )
    sign = jnp.where(parity == 0, 1.0, -1.0).astype(F32)
    iota_e = (rows, 4 * LANES)
    row_e, col_e = at(iota_e, 0), at(iota_e, 1)
    part_e, lane_e = lax.div(col_e, LANES), lax.rem(col_e, LANES)
    place = HALF * lax.div(part_e, 2)
    natural = (lax.rem(part_e, 2) == 1) & (lane_e == row_e + place)
    turned = (lax.rem(part_e, 2) == 0) & (lane_e == rows - 1 - row_e + place)
    gather = (jnp.where(natural, sign, 0.0) + jnp.where(turned, 1.0, 0.0)).astype(BF16)

    wave_own = jnp.int32(0)
    for k in range(waves):
        wave_own = jnp.where(slot_ref[k] == slot, k, wave_own)
    wave_own = wave_own * (NT + 1) // waves
    column = lax.broadcasted_iota(jnp.int32, (2 * lv, steps), 1)
    degree = wave_own + 2 * column + parity
    factor = 1.0 / (
        1.0 + DAMPING * (degree * (degree + 1)).astype(F32) / float(NT * (NT + 1))
    )
    forward_scale = 1.0 / math.sqrt(rows * n_lat // 2)
    inverse_scale = math.sqrt(NLON) / math.sqrt(waves) / math.sqrt(steps)
    scale = jnp.where(wave_own == 0, inverse_scale, 2.0 * inverse_scale).astype(F32)

    legs = send_leg.at[pl.ds(0, half - 1)]
    pltpu.make_async_copy(legs, legs, leg_recv).wait()

    def all_of(ref, sem, count=n - 1):
        return pltpu.make_async_copy(ref.at[pl.ds(0, count)], ref.at[pl.ds(0, count)], sem)

    all_of(got_1, one_recv).wait()

    low = lax.broadcasted_iota(jnp.int32, (lv, LANES), 1) < HALF

    def total_1(lat):
        value = got_1[lat * n_lev]
        for d in range(1, n_lev):
            value = value + got_1[lat * n_lev + d]
        return value

    for b in range(0, half, 2):
        cols = slice(b * HALF, b * HALF + LANES)
        for which in range(2):
            lat = parity * half + b
            one = total_1(lat if which == 0 else n_lat - 1 - lat)
            two = total_1(lat + 1 if which == 0 else n_lat - 2 - lat)
            row0 = which * 2 * lv
            both_f[row0 : row0 + lv, cols] = jnp.where(low, one, pltpu.roll(two, HALF, 1))
            both_f[row0 + lv : row0 + 2 * lv, cols] = jnp.where(
                low, pltpu.roll(one, HALF, 1), two
            )
    near = both_f[0 : 2 * lv, :].astype(BF16)
    both_b[0 : 2 * lv, :] = near
    for c0 in range(0, half * HALF, LANES):
        cols = slice(c0, c0 + LANES)
        both_b[2 * lv :, cols] = jnp.dot(
            both_f[2 * lv :, cols].astype(BF16), flip, preferred_element_type=F32
        ).astype(BF16)
    matrix = basis[...].reshape(half * HALF, steps)
    raw = jnp.dot(both_b[...], matrix, preferred_element_type=F32)
    raw = (raw[2 * lv :] + sign * raw[0 : 2 * lv]) * forward_scale
    masked = jnp.where(degree <= NT, raw, 0.0)
    damped = masked * factor
    change = (damped - masked).astype(BF16)
    back = lax.dot_general(change, matrix, contract_last, preferred_element_type=F32) * scale
    both_f[0 : 2 * lv, :] = back
    for b in range(0, half, 2):
        cols = slice(b * HALF, b * HALF + LANES)
        real, imag = both_f[0:lv, cols], both_f[lv : 2 * lv, cols]
        send_2[b] = jnp.where(low, real, pltpu.roll(imag, HALF, 1))
        send_2[b + 1] = jnp.where(low, pltpu.roll(real, HALF, 1), imag)

    def copy_2(off):
        lat, lev = device(off)
        inside = lax.div(lat, half) == parity
        block = jnp.where(inside, lat, n_lat - 1 - lat) - parity * half
        return remote(
            send_2.at[block], got_2.at[me], two_send, two_recv, lat, lev
        )

    @each(1, n)
    def _(off):
        copy_2(off).start()

    got_2[me] = send_2[lh]

    for vv in range(lv):
        for c in range(2):
            send_p[vv, c : c + 1, :] = damped[c * lv + vv : c * lv + vv + 1]
    home, place_p = lax.div(slot, own), lax.rem(slot, own)
    for vv in range(lv):
        lev = share * lv + vv
        mine = (home == l) & (lev == e)
        copy = remote(
            send_p.at[vv], got_p.at[2 * place_p + parity], p_send, p_recv, home, lev
        )
        pl.when(jnp.logical_not(mine))(copy.start)

        @pl.when(mine)
        def _():
            got_p[2 * place_p + parity] = send_p[vv]

    all_of(got_2, two_recv).wait()

    pairs = waves * levels
    for which in range(2):
        start = jnp.where(which == 1, parity, 1 - parity) * owners
        for o in range(owners):
            stage[which * pairs + o * lv : which * pairs + (o + 1) * lv, :] = got_2[start + o]
    for which in range(2):
        value = stage[which * pairs : (which + 1) * pairs, :]
        lead = value.astype(BF16)
        rest = (value - lead.astype(F32)).astype(BF16)
        for c in range(2):
            cols = slice((2 * c + which) * LANES, (2 * c + which + 1) * LANES)
            cross[0, c * pairs : (c + 1) * pairs, cols] = lead
            cross[1, c * pairs : (c + 1) * pairs, cols] = rest
    synth[...] = lax.dot_general(
        gather, cross[0], contract_last, preferred_element_type=F32
    ) + lax.dot_general(gather, cross[1], contract_last, preferred_element_type=F32)

    keeps = (home == l) & (share == lax.div(e, lv))
    spec_waits = [
        (keeps, all_of(got_p, p_recv, 2 * own - 1)),
        (jnp.logical_not(keeps), all_of(got_p, p_recv, 2 * own)),
    ]
    for case, copy in spec_waits:
        pl.when(case)(copy.wait)
    for k in range(2 * own):
        spec_ref[k] = got_p[k]

    pltpu.make_async_copy(got_col, got_col, halo_send.at[2]).wait()
    pltpu.make_async_copy(legs, legs, leg_send).wait()
    all_of(got_1, one_send).wait()
    all_of(got_2, two_send).wait()
    pl.when(keeps)(all_of(send_p, p_send, lv - 1).wait)
    pl.when(jnp.logical_not(keeps))(all_of(send_p, p_send, lv).wait)

    for k, there in ((0, has_down), (1, has_up)):
        pl.when(there)(
            pltpu.make_async_copy(got_rim.at[k], got_rim.at[k], halo_send.at[k]).wait
        )


def finish(adv, synth, wide, spec, out_hbm, spec_hbm, lead_all, rest_all, result, sems):
    levels, rows, width = result.shape
    spec_copy = pltpu.make_async_copy(spec, spec_hbm, sems.at[0])
    spec_copy.start()
    value = synth[...]
    lead = value.astype(BF16).astype(F32)
    rest = value - lead
    level_of = lax.rem(lax.broadcasted_iota(jnp.int32, value.shape, 1), levels)
    for v in range(levels):
        at = slice(v * rows, (v + 1) * rows)
        lead_all[at, :] = jnp.where(level_of == v, lead, 0.0).astype(BF16)
        rest_all[at, :] = jnp.where(level_of == v, rest, 0.0).astype(BF16)
    chunk = min(width, 256)
    copies = []
    for j in range(0, width, chunk):
        cols = slice(j, j + chunk)
        increment = (
            jnp.dot(lead_all[...], wide[0, :, cols], preferred_element_type=F32)
            + jnp.dot(lead_all[...], wide[1, :, cols], preferred_element_type=F32)
            + jnp.dot(rest_all[...], wide[0, :, cols], preferred_element_type=F32)
        )
        updated = adv[:, cols] + increment
        for v in range(levels):
            result[v, :, cols] = updated[v * rows : (v + 1) * rows]
        copy = pltpu.make_async_copy(
            result.at[:, :, cols], out_hbm.at[:, :, cols], sems.at[1 + j // chunk]
        )
        copy.start()
        copies.append(copy)
    for copy in copies + [spec_copy]:
        copy.wait()


def solution(mesh):
    n_lat, n_lev = mesh.shape["lat"], mesh.shape["lev"]

    def on_device(field, weights, depart_row, depart_col, legendre, wave_slot):
        levels, rows, width = field.shape
        _, waves, steps = legendre.shape
        tiles = width // LANES
        own = waves // n_lat
        n, half = n_lat * n_lev, n_lat // 2
        owners = half * n_lev
        rep = n_lev // (waves // half)
        lv = levels // rep
        pairs = waves * levels
        table = jnp.asarray(lon_table(waves))
        vmem, dma = pltpu.VMEM, pltpu.SemaphoreType.DMA
        anywhere = pl.BlockSpec(memory_space=pltpu.HBM)
        in_vmem = pl.BlockSpec(memory_space=pltpu.VMEM)
        adv, synth, wide, spec = pl.pallas_call(
            functools.partial(kernel, n_lat, n_lev),
            out_shape=(
                vmem((levels * rows, width), F32),
                vmem((rows, 2 * pairs), F32),
                vmem((2, 2 * pairs, width), BF16),
                vmem((2 * own, 2, steps), F32),
            ),
            in_specs=[anywhere] * 7,
            out_specs=(in_vmem,) * 4,
            scratch_shapes=[
                pltpu.SMEM((waves,), jnp.int32),
                vmem((levels, tiles, rows + 16, LANES), F32),
                vmem((4, levels, tiles, rows + 16, LANES), F32),
                vmem((6 * rows, width), BF16),
                vmem((rows, width), jnp.int32),
                vmem((rows, width), jnp.int32),
                vmem((rows * waves, steps), BF16),
                vmem((4 * waves, width), BF16),
                vmem((4 * waves, width), BF16),
                vmem((2, tiles, 2 * levels, LANES), F32),
                vmem((2, rows, LANES), F32),
                vmem((2, tiles + 2, 2 * levels, LANES), F32),
                vmem((2, rows, LANES), F32),
                vmem((6 * 16, width), F32),
                vmem((6 * rows, LANES), F32),
                vmem((2, rows + 16, LANES), F32),
                vmem((half, -(-rows // 16) * 16, steps), BF16),
                vmem((half, HALF, steps), BF16),
                vmem((2 * pairs, LANES), F32),
                vmem((owners, lv, LANES), F32),
                vmem((n, lv, LANES), F32),
                vmem((4 * lv, half * HALF), F32),
                vmem((4 * lv, half * HALF), BF16),
                vmem((half, lv, LANES), F32),
                vmem((n, lv, LANES), F32),
                vmem((2, 2 * pairs, 4 * LANES), BF16),
                vmem((lv, 2, steps), F32),
                vmem((2 * own, 2, steps), F32),
                dma((7,)),
                dma((3,)), dma((3,)),
                dma, dma,
                dma, dma,
                dma, dma,
                dma, dma,
            ],
            compiler_params=pltpu.CompilerParams(
                collective_id=0, has_side_effects=True, vmem_limit_bytes=40 << 20
            ),
        )(
            *(
                pltpu.with_memory_space_constraint(x, pltpu.HBM)
                for x in (
                    wave_slot, field, weights.reshape(4 * rows, width), depart_row, depart_col,
                    legendre.reshape(rows * waves, steps), table,
                )
            ),
        )
        chunks = width // min(width, 256)
        updated, spectral = pl.pallas_call(
            finish,
            out_shape=(
                jax.ShapeDtypeStruct((levels, rows, width), F32),
                jax.ShapeDtypeStruct((2 * own, 2, steps), F32),
            ),
            in_specs=[in_vmem] * 4,
            out_specs=(anywhere,) * 2,
            scratch_shapes=[
                vmem((levels * rows, 2 * pairs), BF16),
                vmem((levels * rows, 2 * pairs), BF16),
                vmem((levels, rows, width), F32),
                dma((1 + chunks,)),
            ],
            compiler_params=pltpu.CompilerParams(vmem_limit_bytes=20 << 20),
        )(*(pltpu.with_memory_space_constraint(x, vmem) for x in (adv, synth, wide, spec)))
        return updated, spectral.reshape(own, 2, 1, 2, steps)

    placed = (
        P(None, "lat", "lev"),
        P(None, "lat", "lev"),
        P("lat", "lev"),
        P("lat", "lev"),
        P("lat", None, None),
        P(),
    )
    return jax.shard_map(
        on_device,
        mesh=mesh,
        in_specs=placed,
        out_specs=(P(None, "lat", "lev"), P("lat", None, "lev", None, None)),
        check_vma=False,
    )
```

```python
import functools
import math

import jax
import jax.numpy as jnp
import numpy as np
from jax import lax
from jax.experimental import pallas as pl
from jax.experimental.pallas import tpu as pltpu
from jax.sharding import PartitionSpec as P

NLON = 4096
NT = 1279
DAMPING = 4.0
LANES = 128
HALF = 64
MESH = pl.DeviceIdType.MESH
F32 = jnp.float32
BF16 = jnp.bfloat16


def lon_table(waves):
    m = (np.arange(waves, dtype=np.int64) * (NT + 1)) // waves
    phases = (m[:, None] * np.arange(NLON, dtype=np.int64)[None, :]) % NLON
    angles = phases.astype(np.float64) * (2.0 * math.pi / NLON)
    table = np.concatenate([np.cos(angles), -np.sin(angles)], axis=0) / math.sqrt(NLON)
    table = table.astype(np.float32)
    lead = table.astype(BF16)
    rest = (table - lead.astype(np.float32)).astype(BF16)
    return np.concatenate([lead, rest], axis=0)


def each(start, stop):
    def run(body):
        if stop - start <= 64:
            for i in range(start, stop):
                body(i)
        else:
            lax.fori_loop(start, stop, lambda i, carry: (body(i), carry)[1], 0)

    return run


def one_hot(mask):
    return jnp.where(mask, 1.0, 0.0).astype(BF16)


def kernel(
    n_lat, n_lev,
    slot_hbm, field_hbm, weights_hbm, drow_hbm, dcol_hbm, leg_hbm, table_hbm,
    adv, synth, wide, spec_ref,
    slot_ref, ext, shifted, points, drow, dcol, leg, tab, tabs,
    pack_row, pack_col, got_rim, got_col, rim_points, side_points, side,
    send_leg, basis, stage, send_1, got_1, both_f, both_b, send_2, got_2, cross, send_p, got_p,
    load_sem, halo_send, halo_recv, leg_send, leg_recv, one_send, one_recv,
    two_send, two_recv, p_send, p_recv, round_sem,
):
    levels, _, _, _ = ext.shape
    rows, width = drow.shape
    tiles = width // LANES
    steps = leg.shape[1]
    waves = leg.shape[0] // rows
    n = n_lat * n_lev
    half = n_lat // 2
    group = waves // half
    rep = n_lev // group
    lv = levels // rep
    own = waves // n_lat
    l, e = lax.axis_index("lat"), lax.axis_index("lev")
    me = l * n_lev + e
    parity, lh = lax.div(l, half), lax.rem(l, half)
    share = lax.rem(e, rep)
    slot = group * lh + lax.div(e, rep)
    has_up, has_down = l > 0, l < n_lat - 1
    east, west = lax.rem(e + 1, n_lev), lax.rem(e + n_lev - 1, n_lev)

    def device(off):
        d = lax.rem(me + off, n)
        return lax.div(d, n_lev), lax.rem(d, n_lev)

    def load(k, src, dst):
        copy = pltpu.make_async_copy(src, dst, load_sem.at[k])
        copy.start()
        return copy

    for t in range(tiles):
        load(0, field_hbm.at[:, :, pl.ds(t * LANES, LANES)], ext.at[:, t, pl.ds(8, rows), :])
    load_leg = load(1, leg_hbm, leg)
    load_slot = load(2, slot_hbm, slot_ref)
    load_wts = load(3, weights_hbm, points.at[pl.ds(0, 4 * rows), :])
    load_row = load(4, drow_hbm, drow)
    load_col = load(5, dcol_hbm, dcol)
    load_tab = load(
        6, table_hbm.at[:, pl.ds(pl.multiple_of(e * width, LANES), width)], tab
    )

    barrier = pltpu.get_barrier_semaphore()

    def greet(lat, lev):
        pl.semaphore_signal(barrier, inc=1, device_id=(lat, lev), device_id_type=MESH)

    def flipped(i, bit):
        return i + bit - 2 * bit * lax.rem(lax.div(i, bit), 2)

    bits = lambda size: [1 << k for k in range((size - 1).bit_length())]
    rounds = [(l, flipped(e, bit)) for bit in bits(n_lev)]
    rounds += [(flipped(l, bit), e) for bit in bits(n_lat)]
    partners = [(l, east), (l, west), (flipped(l, half), e)]
    partners += [(l, flipped(e, bit)) for bit in bits(n_lev)[1:]]
    partners += [(parity * half + lax.rem(lh + off, half), e) for off in range(1, half)]
    for there, lat in ((has_down, l + 1), (has_up, l - 1)):

        @pl.when(there)
        def _():
            for lev in (e, east, west):
                greet(lat, lev)

    for lat, lev in partners:
        greet(lat, lev)
    n_greet = len(partners) + jnp.where(has_up, 3, 0) + jnp.where(has_down, 3, 0)

    passed = []

    def advance():
        k = len(passed)
        if k > len(rounds):
            return
        if k:
            pl.semaphore_wait(round_sem.at[k - 1], 1)
        if k < len(rounds):
            pl.semaphore_signal(
                round_sem.at[k], inc=1, device_id=rounds[k], device_id_type=MESH
            )
        passed.append(k)

    at = lambda shape, dim: lax.broadcasted_iota(jnp.int32, shape, dim)
    for row0 in (0, rows + 8):
        zero = jnp.zeros((levels, tiles, 8, LANES), F32)
        ext[:, :, row0 : row0 + 8, :] = zero
        for move in range(4):
            shifted[move, :, :, row0 : row0 + 8, :] = zero
        for k in range(2):
            side[k, row0 : row0 + 8, :] = zero[0, 0]
    stage[...] = jnp.zeros_like(stage)
    cross[...] = jnp.zeros_like(cross)
    padded = send_leg.shape[1]
    basis[:, padded:, :] = jnp.zeros((half, HALF - padded, steps), BF16)
    send_leg[:, rows:, :] = jnp.zeros((half, padded - rows, steps), BF16)

    lane = at((rows, LANES), 1)
    pltpu.make_async_copy(adv, adv, load_sem.at[0]).wait()
    for v in range(levels):
        for t in range(tiles):
            pack_row[0, t, 2 * v : 2 * v + 2, :] = ext[v, t, 6 + rows : 8 + rows, :]
            pack_row[1, t, 2 * v : 2 * v + 2, :] = ext[v, t, 8:10, :]
    last = jnp.zeros((rows, LANES), F32)
    first = jnp.zeros((rows, LANES), F32)
    for v in range(levels):
        tail = pltpu.roll(ext[v, tiles - 1, 8 : 8 + rows, :], (2 * v + 2) % LANES, 1)
        last = jnp.where(lax.div(lane, 2) == v, tail, last)
        head = pltpu.roll(ext[v, 0, 8 : 8 + rows, :], HALF + 2 * v, 1)
        first = jnp.where(lax.div(lane - HALF, 2) == v, head, first)
    pack_col[0] = last
    pack_col[1] = first

    def remote(src, dst, ssem, rsem, lat, lev):
        return pltpu.make_async_remote_copy(
            src_ref=src, dst_ref=dst, send_sem=ssem, recv_sem=rsem,
            device_id=(lat, lev), device_id_type=MESH,
        )

    def halo(k, src, dst, lat, lev):
        return remote(src, dst, halo_send.at[k], halo_recv.at[k], lat, lev)

    flat = [
        halo(2, pack_col.at[0], got_col.at[0], l, east),
        halo(2, pack_col.at[1], got_col.at[1], l, west),
    ]
    rims = [
        [
            halo(k, pack_row.at[k], got_rim.at[k, pl.ds(1, tiles)], lat, e),
            halo(k, pack_row.at[k, tiles - 1], got_rim.at[k, 0], lat, east),
            halo(k, pack_row.at[k, 0], got_rim.at[k, tiles + 1], lat, west),
        ]
        for k, lat in ((0, l + 1), (1, l - 1))
    ]

    pl.semaphore_wait(barrier, n_greet)

    @pl.when(has_down)
    def _():
        for copy in rims[0]:
            copy.start()

    @pl.when(has_up)
    def _():
        for copy in rims[1]:
            copy.start()

    for copy in flat:
        copy.start()

    advance()
    load_slot.wait()
    first = lax.broadcasted_iota(jnp.int32, (1, 4 * waves), 1)
    slot_row = jnp.zeros((1, 4 * waves), jnp.int32)
    for k in range(waves):
        slot_row = jnp.where(lax.rem(first, waves) == k, slot_ref[k], slot_row)
    iota_f = (4 * waves, 4 * waves)
    order = one_hot(
        (lax.div(at(iota_f, 0), waves) == lax.div(at(iota_f, 1), waves))
        & (lax.rem(at(iota_f, 0), waves) == slot_row)
    )
    load_leg.wait()
    band = 8
    iota_g = (half * band, band * waves)
    slot_cols = jnp.zeros((1, band * waves), jnp.int32)
    lane_k = lax.rem(lax.broadcasted_iota(jnp.int32, (1, band * waves), 1), waves)
    for k in range(waves):
        slot_cols = jnp.where(lane_k == k, slot_ref[k], slot_cols)
    choose = one_hot(
        (lax.rem(at(iota_g, 0), band) == lax.div(at(iota_g, 1), waves))
        & (group * lax.div(at(iota_g, 0), band) + lax.div(e, rep) == slot_cols)
    )
    for i in range(0, rows, band):
        picked = jnp.dot(
            choose, leg[i * waves : (i + band) * waves, :], preferred_element_type=F32
        ).astype(BF16)
        for t in range(half):
            send_leg[t, i : i + band, :] = picked[t * band : (t + 1) * band]
    slots_of = lambda t: basis.at[t, pl.ds(0, padded), :]
    copies_g = []
    for off in range(1, half):
        t = lax.rem(lh + off, half)
        copy = remote(
            send_leg.at[t], slots_of(lh), leg_send, leg_recv,
            parity * half + t, e,
        )
        copy.start()
        copies_g.append(copy)
    basis[lh, 0:padded, :] = send_leg[lh]

    advance()
    lane = at((8, LANES), 1)
    moves = (-2, -1, 1, 2)

    def move_blocks(blocks, move):
        turned = [x if x is None else pltpu.roll(x, (-move) % LANES, 1) for x in blocks]
        zero = jnp.zeros((8, LANES), F32)
        result = []
        for t in range(1, len(blocks) - 1):
            near = turned[t - 1] if move < 0 else turned[t + 1]
            wrapped = (lane < -move) if move < 0 else (lane >= LANES - move)
            result.append(jnp.where(wrapped, zero if near is None else near, turned[t]))
        return result

    groups = rows // 8

    def shift_level(v, carry):
        for g in range(groups):
            band = slice(8 + 8 * g, 16 + 8 * g)
            blocks = [None] + [ext[v, t, band, :] for t in range(tiles)] + [None]
            for k, move in enumerate(moves):
                for t, value in enumerate(move_blocks(blocks, move)):
                    shifted[k, v, t, band, :] = value
        return carry

    lax.fori_loop(0, levels, shift_level, 0)

    def choose_two(high, low, values):
        one = jnp.where(high, values[2], values[0])
        two = jnp.where(high, values[3], values[1])
        three = jnp.where(high, values[4], values[2])
        return jnp.where(low, two, one), jnp.where(low, three, two)

    advance()
    load_wts.wait()
    load_row.wait()
    load_col.wait()

    sub = at((8, LANES), 0)

    def advect(t, carry):
        cols = pl.ds(pl.multiple_of(t * LANES, LANES), LANES)
        corner = [points[k * rows : (k + 1) * rows, cols].astype(F32) for k in range(4)]
        zero = jnp.zeros((8, LANES), F32)
        turned = {}

        def turn(v, c, g, amount):
            if g < 0 or g >= groups:
                return zero
            key = (v, c, g, amount)
            if key not in turned:
                turned[key] = pltpu.roll(plane(v, c)[8 * g + 8 : 8 * g + 16, :], amount, 0)
            return turned[key]

        def plane(v, c):
            return ext.at[v, t] if c == 2 else shifted.at[c if c < 2 else c - 1, v, t]

        def five(v, c, g):
            ref = plane(v, c)
            load_at = lambda r: ref[8 * g + 8 + r : 8 * g + 16 + r, :]
            values = [load_at(r) for r in (-1, 0, 1)]
            if c in (0, 1, 3, 4):
                before = jnp.where(sub < 2, turn(v, c, g - 1, 2), turn(v, c, g, 2))
                after = jnp.where(sub < 6, turn(v, c, g, 6), turn(v, c, g + 1, 6))
            else:
                before, after = load_at(-2), load_at(2)
            return [before] + values + [after]

        for v in range(levels):
            for g in range(groups):
                band = slice(8 * g, 8 * g + 8)
                dr, dc = drow[band, cols], dcol[band, cols]
                row_high, row_low = dr >= 0, (dr & 1) == 1
                col_high, col_low = dc >= 0, (dc & 1) == 1
                w = [corner[k][band] for k in range(4)]
                picked = [choose_two(row_high, row_low, five(v, c, g)) for c in range(5)]
                upper = choose_two(col_high, col_low, [x[0] for x in picked])
                lower = choose_two(col_high, col_low, [x[1] for x in picked])
                total = w[0] * upper[0] + w[1] * upper[1] + w[2] * lower[0] + w[3] * lower[1]
                adv[v * rows + 8 * g : v * rows + 8 * g + 8, cols] = total
        return carry

    lax.fori_loop(0, tiles // 2, advect, 0)
    advance()
    lax.fori_loop(tiles // 2, tiles, advect, 0)
    advance()

    load_tab.wait()
    tabs[...] = jnp.dot(order, tab[...], preferred_element_type=F32).astype(BF16)

    points[4 * rows : 5 * rows, :] = drow[...].astype(F32).astype(BF16)
    points[5 * rows : 6 * rows, :] = dcol[...].astype(F32).astype(BF16)
    iota_r = (6 * 16, 6 * rows)
    row_r, col_r = at(iota_r, 0), at(iota_r, 1)
    odd = row_r & 1
    repeat_rows = one_hot(
        (lax.div(row_r, 16) == lax.div(col_r, rows))
        & (lax.rem(col_r, rows) == jnp.where((row_r & 15) < 8, odd, rows - 2 + odd))
    )
    rim_points[...] = jnp.dot(repeat_rows, points[...], preferred_element_type=F32)
    row_c, col_c = at((LANES, LANES), 0), at((LANES, LANES), 1)
    from_first = one_hot((col_c < HALF) & (row_c == (col_c & 1)))
    from_last = one_hot((col_c >= HALF) & (row_c == LANES - 2 + (col_c & 1)))
    side_points[...] = jnp.dot(
        points[:, 0:LANES], from_first, preferred_element_type=F32
    ) + jnp.dot(points[:, width - LANES :], from_last, preferred_element_type=F32)

    even = (at((8, LANES), 0) & 1) == 0

    def fix_rows(k):
        for c0 in range(0, 2 * levels, 8):
            blocks = [got_rim[k, t, c0 : c0 + 8, :] for t in range(tiles + 2)]
            moved = [move_blocks(blocks, move) for move in moves]
            moved.insert(2, blocks[1:-1])
            for t in range(tiles):
                cols = slice(t * LANES, (t + 1) * LANES)
                w0, w1, w2, w3, dr, dc = [
                    rim_points[16 * q + 8 * k : 16 * q + 8 * k + 8, cols] for q in range(6)
                ]
                col_high, col_low = dc >= 0.0, (dc == -1.0) | (dc == 1.0)
                same = [moved[c][t] for c in range(5)]
                other = [pltpu.roll(x, 1 if k else 7, 0) for x in same]
                s0, s1 = choose_two(col_high, col_low, same)
                o0, o1 = choose_two(col_high, col_low, other)
                if k == 0:
                    far = jnp.where(dr == -2.0, w0 * s0 + w1 * s1, 0.0)
                    near = jnp.where(
                        dr == -1.0, w0 * o0 + w1 * o1,
                        jnp.where(dr == -2.0, w2 * o0 + w3 * o1, 0.0),
                    )
                    near = jnp.where(even, near, 0.0)
                else:
                    far = jnp.where(dr == 1.0, w2 * s0 + w3 * s1, 0.0)
                    near = jnp.where(
                        dr == 1.0, w0 * o0 + w1 * o1,
                        jnp.where(dr == 0.0, w2 * o0 + w3 * o1, 0.0),
                    )
                    near = jnp.where(even, 0.0, near)
                extra = far + near
                for i in range(0, 8, 2):
                    row0 = (c0 + i) // 2 * rows + k * (rows - 2)
                    adv[row0 : row0 + 2, cols] += extra[i : i + 2]

    @pl.when(has_up)
    def _():
        pltpu.make_async_copy(got_rim.at[0], got_rim.at[0], halo_recv.at[0]).wait()
        fix_rows(0)

    @pl.when(has_down)
    def _():
        pltpu.make_async_copy(got_rim.at[1], got_rim.at[1], halo_recv.at[1]).wait()
        fix_rows(1)

    pltpu.make_async_copy(got_col, got_col, halo_recv.at[2]).wait()
    here = jnp.where(at((rows, LANES), 1) < HALF, got_col[0], got_col[1])
    side[0, 8 : 8 + rows, :] = here
    side[1, 8 : 8 + rows, :] = jnp.where(
        at((rows, LANES), 1) < HALF, pltpu.roll(here, LANES - 1, 1), pltpu.roll(here, 1, 1)
    )
    in_west = lane < HALF
    edge = jnp.where(in_west, -1.0, 1.0)
    inner = (lane & 1) == jnp.where(in_west, 0, 1)
    for g in range(groups):
        w0, w1, w2, w3, dr, dc = [
            side_points[q * rows + 8 * g : q * rows + 8 * g + 8, :] for q in range(6)
        ]
        row_high, row_low = dr >= 0.0, (dr == -1.0) | (dr == 1.0)
        s0, s1 = choose_two(
            row_high, row_low, [side[0, 8 * g + 6 + r : 8 * g + 14 + r, :] for r in range(5)]
        )
        o0, o1 = choose_two(
            row_high, row_low, [side[1, 8 * g + 6 + r : 8 * g + 14 + r, :] for r in range(5)]
        )
        far = jnp.where(
            dc == jnp.where(in_west, -2.0, 1.0),
            jnp.where(in_west, w0, w1) * s0 + jnp.where(in_west, w2, w3) * s1,
            0.0,
        )
        near = jnp.where(
            dc == edge, w0 * o0 + w2 * o1,
            jnp.where(dc == edge - 1.0, w1 * o0 + w3 * o1, 0.0),
        )
        extra = far + jnp.where(inner, near, 0.0)
        for v in range(levels):
            band = slice(v * rows + 8 * g, v * rows + 8 * g + 8)
            west_part = pltpu.roll(extra, (LANES - 2 * v) % LANES, 1) if v else extra
            adv[band, 0:LANES] += jnp.where(lane < 2, west_part, 0.0)
            east_part = pltpu.roll(extra, (LANES - 2 - HALF - 2 * v) % LANES, 1)
            adv[band, width - LANES :] += jnp.where(lane >= LANES - 2, east_part, 0.0)

    contract_last = (((1,), (1,)), ((), ()))
    for v in range(levels):
        value = adv[v * rows : (v + 1) * rows, :]
        lead = value.astype(BF16)
        rest = (value - lead.astype(F32)).astype(BF16)
        both = lax.dot_general(tabs[...], lead, contract_last, preferred_element_type=F32)
        more = lax.dot_general(
            tabs[0 : 2 * waves, :], rest, contract_last, preferred_element_type=F32
        )
        coeffs = both[0 : 2 * waves] + both[2 * waves :] + more
        stage[v * waves : (v + 1) * waves, 0:rows] = coeffs[0:waves]
        stage[v * waves : (v + 1) * waves, HALF : HALF + rows] = coeffs[waves:]
    owners = half * n_lev
    for s in range(waves):
        for g in range(rep):
            send_1[s * rep + g] = stage[pl.ds(g * lv * waves + s, lv, stride=waves), :]

    def copy_1(off):
        lat, lev = device(off)
        owner = lax.rem(lat, half) * n_lev + lev
        return remote(
            send_1.at[owner], got_1.at[me], one_send, one_recv, lat, lev
        )

    while len(passed) <= len(rounds):
        advance()

    @each(1, n)
    def _(off):
        copy_1(off).start()

    got_1[me] = send_1[lh * n_lev + e]

    spread_rows = 2 * waves * levels
    iota_w = (spread_rows, 2 * waves)
    repeat = one_hot(lax.div(at(iota_w, 0), levels) == at(iota_w, 1))
    for q in range(2):
        wide[q] = jnp.dot(
            repeat, tabs[2 * waves * q : 2 * waves * (q + 1), :], preferred_element_type=F32
        ).astype(BF16)

    at_row, at_col = at((LANES, LANES), 0), at((LANES, LANES), 1)
    flip = one_hot(
        ((at_row + at_col == rows - 1) & (at_row < HALF) & (at_col < HALF))
        | ((at_row + at_col == 2 * HALF + rows - 1) & (at_row >= HALF) & (at_col >= HALF))
    )
    sign = jnp.where(parity == 0, 1.0, -1.0).astype(F32)
    iota_e = (rows, 4 * LANES)
    row_e, col_e = at(iota_e, 0), at(iota_e, 1)
    part_e, lane_e = lax.div(col_e, LANES), lax.rem(col_e, LANES)
    place = HALF * lax.div(part_e, 2)
    natural = (lax.rem(part_e, 2) == 1) & (lane_e == row_e + place)
    turned = (lax.rem(part_e, 2) == 0) & (lane_e == rows - 1 - row_e + place)
    gather = (jnp.where(natural, sign, 0.0) + jnp.where(turned, 1.0, 0.0)).astype(BF16)

    wave_own = jnp.int32(0)
    for k in range(waves):
        wave_own = jnp.where(slot_ref[k] == slot, k, wave_own)
    wave_own = wave_own * (NT + 1) // waves
    column = lax.broadcasted_iota(jnp.int32, (2 * lv, steps), 1)
    degree = wave_own + 2 * column + parity
    factor = 1.0 / (
        1.0 + DAMPING * (degree * (degree + 1)).astype(F32) / float(NT * (NT + 1))
    )
    forward_scale = 1.0 / math.sqrt(rows * n_lat // 2)
    inverse_scale = math.sqrt(NLON) / math.sqrt(waves) / math.sqrt(steps)
    scale = jnp.where(wave_own == 0, inverse_scale, 2.0 * inverse_scale).astype(F32)

    legs = send_leg.at[pl.ds(0, half - 1)]
    pltpu.make_async_copy(legs, legs, leg_recv).wait()

    def all_of(ref, sem, count=n - 1):
        return pltpu.make_async_copy(ref.at[pl.ds(0, count)], ref.at[pl.ds(0, count)], sem)

    all_of(got_1, one_recv).wait()

    low = lax.broadcasted_iota(jnp.int32, (lv, LANES), 1) < HALF

    def total_1(lat):
        value = got_1[lat * n_lev]
        for d in range(1, n_lev):
            value = value + got_1[lat * n_lev + d]
        return value

    for b in range(0, half, 2):
        cols = slice(b * HALF, b * HALF + LANES)
        for which in range(2):
            lat = parity * half + b
            one = total_1(lat if which == 0 else n_lat - 1 - lat)
            two = total_1(lat + 1 if which == 0 else n_lat - 2 - lat)
            row0 = which * 2 * lv
            both_f[row0 : row0 + lv, cols] = jnp.where(low, one, pltpu.roll(two, HALF, 1))
            both_f[row0 + lv : row0 + 2 * lv, cols] = jnp.where(
                low, pltpu.roll(one, HALF, 1), two
            )
    near = both_f[0 : 2 * lv, :].astype(BF16)
    both_b[0 : 2 * lv, :] = near
    for c0 in range(0, half * HALF, LANES):
        cols = slice(c0, c0 + LANES)
        both_b[2 * lv :, cols] = jnp.dot(
            both_f[2 * lv :, cols].astype(BF16), flip, preferred_element_type=F32
        ).astype(BF16)
    matrix = basis[...].reshape(half * HALF, steps)
    raw = jnp.dot(both_b[...], matrix, preferred_element_type=F32)
    raw = (raw[2 * lv :] + sign * raw[0 : 2 * lv]) * forward_scale
    masked = jnp.where(degree <= NT, raw, 0.0)
    damped = masked * factor
    change = (damped - masked).astype(BF16)
    back = lax.dot_general(change, matrix, contract_last, preferred_element_type=F32) * scale
    both_f[0 : 2 * lv, :] = back
    for b in range(0, half, 2):
        cols = slice(b * HALF, b * HALF + LANES)
        real, imag = both_f[0:lv, cols], both_f[lv : 2 * lv, cols]
        send_2[b] = jnp.where(low, real, pltpu.roll(imag, HALF, 1))
        send_2[b + 1] = jnp.where(low, pltpu.roll(real, HALF, 1), imag)

    def copy_2(off):
        lat, lev = device(off)
        inside = lax.div(lat, half) == parity
        block = jnp.where(inside, lat, n_lat - 1 - lat) - parity * half
        return remote(
            send_2.at[block], got_2.at[me], two_send, two_recv, lat, lev
        )

    @each(1, n)
    def _(off):
        copy_2(off).start()

    got_2[me] = send_2[lh]

    for vv in range(lv):
        for c in range(2):
            send_p[vv, c : c + 1, :] = damped[c * lv + vv : c * lv + vv + 1]
    home, place_p = lax.div(slot, own), lax.rem(slot, own)
    for vv in range(lv):
        lev = share * lv + vv
        mine = (home == l) & (lev == e)
        copy = remote(
            send_p.at[vv], got_p.at[2 * place_p + parity], p_send, p_recv, home, lev
        )
        pl.when(jnp.logical_not(mine))(copy.start)

        @pl.when(mine)
        def _():
            got_p[2 * place_p + parity] = send_p[vv]

    all_of(got_2, two_recv).wait()

    pairs = waves * levels
    for which in range(2):
        start = jnp.where(which == 1, parity, 1 - parity) * owners
        for o in range(owners):
            stage[which * pairs + o * lv : which * pairs + (o + 1) * lv, :] = got_2[start + o]
    for which in range(2):
        value = stage[which * pairs : (which + 1) * pairs, :]
        lead = value.astype(BF16)
        rest = (value - lead.astype(F32)).astype(BF16)
        for c in range(2):
            cols = slice((2 * c + which) * LANES, (2 * c + which + 1) * LANES)
            cross[0, c * pairs : (c + 1) * pairs, cols] = lead
            cross[1, c * pairs : (c + 1) * pairs, cols] = rest
    synth[...] = lax.dot_general(
        gather, cross[0], contract_last, preferred_element_type=F32
    ) + lax.dot_general(gather, cross[1], contract_last, preferred_element_type=F32)

    keeps = (home == l) & (share == lax.div(e, lv))
    spec_waits = [
        (keeps, all_of(got_p, p_recv, 2 * own - 1)),
        (jnp.logical_not(keeps), all_of(got_p, p_recv, 2 * own)),
    ]
    for case, copy in spec_waits:
        pl.when(case)(copy.wait)
    for k in range(2 * own):
        spec_ref[k] = got_p[k]

    pltpu.make_async_copy(got_col, got_col, halo_send.at[2]).wait()
    pltpu.make_async_copy(legs, legs, leg_send).wait()
    all_of(got_1, one_send).wait()
    all_of(got_2, two_send).wait()
    pl.when(keeps)(all_of(send_p, p_send, lv - 1).wait)
    pl.when(jnp.logical_not(keeps))(all_of(send_p, p_send, lv).wait)

    for k, there in ((0, has_down), (1, has_up)):
        pl.when(there)(
            pltpu.make_async_copy(got_rim.at[k], got_rim.at[k], halo_send.at[k]).wait
        )


def finish(adv, synth, wide, spec, out_hbm, spec_hbm, lead_all, rest_all, result, sems):
    levels, rows, width = result.shape
    spec_copy = pltpu.make_async_copy(spec, spec_hbm, sems.at[0])
    spec_copy.start()
    value = synth[...]
    lead = value.astype(BF16).astype(F32)
    rest = value - lead
    level_of = lax.rem(lax.broadcasted_iota(jnp.int32, value.shape, 1), levels)
    for v in range(levels):
        at = slice(v * rows, (v + 1) * rows)
        lead_all[at, :] = jnp.where(level_of == v, lead, 0.0).astype(BF16)
        rest_all[at, :] = jnp.where(level_of == v, rest, 0.0).astype(BF16)
    chunk = min(width, 256)
    copies = []
    for j in range(0, width, chunk):
        cols = slice(j, j + chunk)
        increment = (
            jnp.dot(lead_all[...], wide[0, :, cols], preferred_element_type=F32)
            + jnp.dot(lead_all[...], wide[1, :, cols], preferred_element_type=F32)
            + jnp.dot(rest_all[...], wide[0, :, cols], preferred_element_type=F32)
        )
        updated = adv[:, cols] + increment
        for v in range(levels):
            result[v, :, cols] = updated[v * rows : (v + 1) * rows]
        copy = pltpu.make_async_copy(
            result.at[:, :, cols], out_hbm.at[:, :, cols], sems.at[1 + j // chunk]
        )
        copy.start()
        copies.append(copy)
    for copy in copies + [spec_copy]:
        copy.wait()


def solution(mesh):
    n_lat, n_lev = mesh.shape["lat"], mesh.shape["lev"]

    def on_device(field, weights, depart_row, depart_col, legendre, wave_slot):
        levels, rows, width = field.shape
        _, waves, steps = legendre.shape
        tiles = width // LANES
        own = waves // n_lat
        n, half = n_lat * n_lev, n_lat // 2
        owners = half * n_lev
        rep = n_lev // (waves // half)
        lv = levels // rep
        pairs = waves * levels
        table = jnp.asarray(lon_table(waves))
        vmem, dma = pltpu.VMEM, pltpu.SemaphoreType.DMA
        anywhere = pl.BlockSpec(memory_space=pltpu.HBM)
        in_vmem = pl.BlockSpec(memory_space=pltpu.VMEM)
        adv, synth, wide, spec = pl.pallas_call(
            functools.partial(kernel, n_lat, n_lev),
            out_shape=(
                vmem((levels * rows, width), F32),
                vmem((rows, 2 * pairs), F32),
                vmem((2, 2 * pairs, width), BF16),
                vmem((2 * own, 2, steps), F32),
            ),
            in_specs=[anywhere] * 7,
            out_specs=(in_vmem,) * 4,
            scratch_shapes=[
                pltpu.SMEM((waves,), jnp.int32),
                vmem((levels, tiles, rows + 16, LANES), F32),
                vmem((4, levels, tiles, rows + 16, LANES), F32),
                vmem((6 * rows, width), BF16),
                vmem((rows, width), jnp.int32),
                vmem((rows, width), jnp.int32),
                vmem((rows * waves, steps), BF16),
                vmem((4 * waves, width), BF16),
                vmem((4 * waves, width), BF16),
                vmem((2, tiles, 2 * levels, LANES), F32),
                vmem((2, rows, LANES), F32),
                vmem((2, tiles + 2, 2 * levels, LANES), F32),
                vmem((2, rows, LANES), F32),
                vmem((6 * 16, width), F32),
                vmem((6 * rows, LANES), F32),
                vmem((2, rows + 16, LANES), F32),
                vmem((half, -(-rows // 16) * 16, steps), BF16),
                vmem((half, HALF, steps), BF16),
                vmem((2 * pairs, LANES), F32),
                vmem((owners, lv, LANES), F32),
                vmem((n, lv, LANES), F32),
                vmem((4 * lv, half * HALF), F32),
                vmem((4 * lv, half * HALF), BF16),
                vmem((half, lv, LANES), F32),
                vmem((n, lv, LANES), F32),
                vmem((2, 2 * pairs, 4 * LANES), BF16),
                vmem((lv, 2, steps), F32),
                vmem((2 * own, 2, steps), F32),
                dma((7,)),
                dma((3,)), dma((3,)),
                dma, dma,
                dma, dma,
                dma, dma,
                dma, dma,
                pltpu.SemaphoreType.REGULAR(
                    ((n_lev - 1).bit_length() + (n_lat - 1).bit_length(),)
                ),
            ],
            compiler_params=pltpu.CompilerParams(
                collective_id=0, has_side_effects=True, vmem_limit_bytes=40 << 20
            ),
        )(
            *(
                pltpu.with_memory_space_constraint(x, pltpu.HBM)
                for x in (
                    wave_slot, field, weights.reshape(4 * rows, width), depart_row, depart_col,
                    legendre.reshape(rows * waves, steps), table,
                )
            ),
        )
        chunks = width // min(width, 256)
        updated, spectral = pl.pallas_call(
            finish,
            out_shape=(
                jax.ShapeDtypeStruct((levels, rows, width), F32),
                jax.ShapeDtypeStruct((2 * own, 2, steps), F32),
            ),
            in_specs=[in_vmem] * 4,
            out_specs=(anywhere,) * 2,
            scratch_shapes=[
                vmem((levels * rows, 2 * pairs), BF16),
                vmem((levels * rows, 2 * pairs), BF16),
                vmem((levels, rows, width), F32),
                dma((1 + chunks,)),
            ],
            compiler_params=pltpu.CompilerParams(vmem_limit_bytes=20 << 20),
        )(*(pltpu.with_memory_space_constraint(x, vmem) for x in (adv, synth, wide, spec)))
        return updated, spectral.reshape(own, 2, 1, 2, steps)

    placed = (
        P(None, "lat", "lev"),
        P(None, "lat", "lev"),
        P("lat", "lev"),
        P("lat", "lev"),
        P("lat", None, None),
        P(),
    )
    return jax.shard_map(
        on_device,
        mesh=mesh,
        in_specs=placed,
        out_specs=(P(None, "lat", "lev"), P("lat", None, "lev", None, None)),
        check_vma=False,
    )
```

```python
import functools
import math

import jax
import jax.numpy as jnp
import numpy as np
from jax import lax
from jax.experimental import pallas as pl
from jax.experimental.pallas import tpu as pltpu
from jax.sharding import PartitionSpec as P

NLON = 4096
NT = 1279
DAMPING = 4.0
LANES = 128
HALF = 64
MESH = pl.DeviceIdType.MESH
F32 = jnp.float32
BF16 = jnp.bfloat16


def lon_table(waves):
    m = (np.arange(waves, dtype=np.int64) * (NT + 1)) // waves
    phases = (m[:, None] * np.arange(NLON, dtype=np.int64)[None, :]) % NLON
    angles = phases.astype(np.float64) * (2.0 * math.pi / NLON)
    table = np.concatenate([np.cos(angles), -np.sin(angles)], axis=0) / math.sqrt(NLON)
    table = table.astype(np.float32)
    lead = table.astype(BF16)
    rest = (table - lead.astype(np.float32)).astype(BF16)
    return np.concatenate([lead, rest], axis=0)


def each(start, stop):
    def run(body):
        if stop - start <= 64:
            for i in range(start, stop):
                body(i)
        else:
            lax.fori_loop(start, stop, lambda i, carry: (body(i), carry)[1], 0)

    return run


def one_hot(mask):
    return jnp.where(mask, 1.0, 0.0).astype(BF16)


def kernel(
    n_lat, n_lev,
    slot_hbm, field_hbm, weights_hbm, drow_hbm, dcol_hbm, leg_hbm, table_hbm,
    adv, synth, wide, spec_ref,
    slot_ref, ext, shifted, points, drow, dcol, leg, tab, tabs,
    rim_rows, pack_row, pack_col, got_rim, got_col, rim_inputs, rim_points, side_points, side,
    send_leg, basis, stage, send_1, got_1, both_f, both_b, send_2, got_2, cross, send_p, got_p,
    load_sem, halo_send, halo_recv, leg_send, leg_recv, one_send, one_recv,
    two_send, two_recv, p_send, p_recv, round_sem,
):
    levels, _, _, _ = ext.shape
    rows, width = drow.shape
    tiles = width // LANES
    steps = leg.shape[1]
    waves = leg.shape[0] // rows
    n = n_lat * n_lev
    half = n_lat // 2
    group = waves // half
    rep = n_lev // group
    lv = levels // rep
    own = waves // n_lat
    l, e = lax.axis_index("lat"), lax.axis_index("lev")
    me = l * n_lev + e
    parity, lh = lax.div(l, half), lax.rem(l, half)
    share = lax.rem(e, rep)
    slot = group * lh + lax.div(e, rep)
    has_up, has_down = l > 0, l < n_lat - 1
    east, west = lax.rem(e + 1, n_lev), lax.rem(e + n_lev - 1, n_lev)

    def load(k, src, dst):
        copy = pltpu.make_async_copy(src, dst, load_sem.at[k])
        copy.start()
        return copy

    for t in range(tiles):
        load(0, field_hbm.at[:, :, pl.ds(t * LANES, LANES)], ext.at[:, t, pl.ds(8, rows), :])
    load_leg = load(1, leg_hbm, leg)
    load_slot = load(2, slot_hbm, slot_ref)
    load_wts = load(3, weights_hbm, points.at[pl.ds(0, 4 * rows), :])
    for q in range(4):
        for k in range(2):
            load(
                7, weights_hbm.at[pl.ds(q * rows + k * (rows - 8), 8), :],
                rim_inputs.at[pl.ds(16 * q + 8 * k, 8), :],
            )
    load_row = load(4, drow_hbm, drow)
    load_col = load(5, dcol_hbm, dcol)
    load_tab = load(
        6, table_hbm.at[:, pl.ds(pl.multiple_of(e * width, LANES), width)], tab
    )

    barrier = pltpu.get_barrier_semaphore()

    def greet(lat, lev):
        pl.semaphore_signal(barrier, inc=1, device_id=(lat, lev), device_id_type=MESH)

    column = [(parity * half + lax.rem(lh + off, half), e) for off in range(1, half)]
    across = (lax.rem(l + half, n_lat), e)
    partners = [(l, lax.rem(e + off, n_lev)) for off in range(1, n_lev)]
    partners += column + [across]
    for there, lat in ((has_down, l + 1), (has_up, l - 1)):

        @pl.when(there)
        def _():
            for lev in (e, east, west):
                greet(lat, lev)

    for lat, lev in partners:
        greet(lat, lev)
    n_greet = len(partners) + jnp.where(has_up, 3, 0) + jnp.where(has_down, 3, 0)

    def tell(k, devices):
        for there in devices:
            pl.semaphore_signal(round_sem.at[k], inc=1, device_id=there, device_id_type=MESH)

    at = lambda shape, dim: lax.broadcasted_iota(jnp.int32, shape, dim)
    for row0 in (0, rows + 8):
        zero = jnp.zeros((levels, tiles, 8, LANES), F32)
        ext[:, :, row0 : row0 + 8, :] = zero
        for move in range(4):
            shifted[move, :, :, row0 : row0 + 8, :] = zero
        for k in range(2):
            side[k, row0 : row0 + 8, :] = zero[0, 0]
    stage[...] = jnp.zeros_like(stage)
    cross[...] = jnp.zeros_like(cross)
    padded = send_leg.shape[1]
    basis[:, padded:, :] = jnp.zeros((half, HALF - padded, steps), BF16)

    lane = at((rows, LANES), 1)
    pltpu.make_async_copy(adv, adv, load_sem.at[0]).wait()
    for v in range(levels):
        for t in range(tiles):
            rim_rows[0, t, 2 * v : 2 * v + 2, :] = ext[v, t, 6 + rows : 8 + rows, :]
            rim_rows[1, t, 2 * v : 2 * v + 2, :] = ext[v, t, 8:10, :]
    pack_row[...] = rim_rows[...].astype(BF16)
    last = jnp.zeros((rows, LANES), F32)
    first = jnp.zeros((rows, LANES), F32)
    for v in range(levels):
        tail = pltpu.roll(ext[v, tiles - 1, 8 : 8 + rows, :], (2 * v + 2) % LANES, 1)
        last = jnp.where(lax.div(lane, 2) == v, tail, last)
        head = pltpu.roll(ext[v, 0, 8 : 8 + rows, :], HALF + 2 * v, 1)
        first = jnp.where(lax.div(lane - HALF, 2) == v, head, first)
    pack_col[0] = last.astype(BF16)
    pack_col[1] = first.astype(BF16)

    def remote(src, dst, ssem, rsem, lat, lev):
        return pltpu.make_async_remote_copy(
            src_ref=src, dst_ref=dst, send_sem=ssem, recv_sem=rsem,
            device_id=(lat, lev), device_id_type=MESH,
        )

    def halo(k, src, dst, lat, lev):
        return remote(src, dst, halo_send.at[k], halo_recv.at[k], lat, lev)

    flat = [
        halo(2, pack_col.at[0], got_col.at[0], l, east),
        halo(2, pack_col.at[1], got_col.at[1], l, west),
    ]
    rims = [
        [
            halo(k, pack_row.at[k], got_rim.at[k, pl.ds(1, tiles)], lat, e),
            halo(k, pack_row.at[k, tiles - 1], got_rim.at[k, 0], lat, east),
            halo(k, pack_row.at[k, 0], got_rim.at[k, tiles + 1], lat, west),
        ]
        for k, lat in ((0, l + 1), (1, l - 1))
    ]

    pl.semaphore_wait(barrier, n_greet)

    @pl.when(has_down)
    def _():
        for copy in rims[0]:
            copy.start()

    @pl.when(has_up)
    def _():
        for copy in rims[1]:
            copy.start()

    for copy in flat:
        copy.start()

    tell(0, column)

    lane = at((8, LANES), 1)
    moves = (-2, -1, 1, 2)

    def move_blocks(blocks, move):
        turned = [x if x is None else pltpu.roll(x, (-move) % LANES, 1) for x in blocks]
        zero = jnp.zeros((8, LANES), F32)
        result = []
        for t in range(1, len(blocks) - 1):
            near = turned[t - 1] if move < 0 else turned[t + 1]
            wrapped = (lane < -move) if move < 0 else (lane >= LANES - move)
            result.append(jnp.where(wrapped, zero if near is None else near, turned[t]))
        return result

    groups = rows // 8

    def shift_level(v):
        for g in range(groups):
            band = slice(8 + 8 * g, 16 + 8 * g)
            blocks = [None] + [ext[v, t, band, :] for t in range(tiles)] + [None]
            for k, move in enumerate(moves):
                for t, value in enumerate(move_blocks(blocks, move)):
                    shifted[k, v, t, band, :] = value

    for v in range(levels):
        shift_level(v)

    load_slot.wait()
    first = lax.broadcasted_iota(jnp.int32, (1, 4 * waves), 1)
    slot_row = jnp.zeros((1, 4 * waves), jnp.int32)
    for k in range(waves):
        slot_row = jnp.where(lax.rem(first, waves) == k, slot_ref[k], slot_row)
    iota_f = (4 * waves, 4 * waves)
    order = one_hot(
        (lax.div(at(iota_f, 0), waves) == lax.div(at(iota_f, 1), waves))
        & (lax.rem(at(iota_f, 0), waves) == slot_row)
    )
    load_leg.wait()
    band = 8
    iota_g = (half * band, band * waves)
    slot_cols = jnp.zeros((1, band * waves), jnp.int32)
    lane_k = lax.rem(lax.broadcasted_iota(jnp.int32, (1, band * waves), 1), waves)
    for k in range(waves):
        slot_cols = jnp.where(lane_k == k, slot_ref[k], slot_cols)
    choose = one_hot(
        (lax.rem(at(iota_g, 0), band) == lax.div(at(iota_g, 1), waves))
        & (group * lax.div(at(iota_g, 0), band) + lax.div(e, rep) == slot_cols)
    )
    for i in range(0, rows, band):
        picked = jnp.dot(
            choose, leg[i * waves : (i + band) * waves, :], preferred_element_type=F32
        ).astype(BF16)
        for t in range(half):
            send_leg[t, i : i + band, :] = picked[t * band : (t + 1) * band]
    slots_of = lambda t: basis.at[t, pl.ds(0, padded), :]
    copies_g = []
    for off in range(1, half):
        t = lax.rem(lh + off, half)
        copy = remote(
            send_leg.at[t], slots_of(lh), leg_send, leg_recv,
            parity * half + t, e,
        )
        copy.start()
        copies_g.append(copy)
    basis[lh, 0:padded, :] = send_leg[lh]

    def choose_two(high, low, values):
        one = jnp.where(high, values[2], values[0])
        two = jnp.where(high, values[3], values[1])
        three = jnp.where(high, values[4], values[2])
        return jnp.where(low, two, one), jnp.where(low, three, two)

    load_wts.wait()
    load_row.wait()
    load_col.wait()

    sub = at((8, LANES), 0)

    def advect(t, carry):
        cols = pl.ds(pl.multiple_of(t * LANES, LANES), LANES)
        corner = [points[k * rows : (k + 1) * rows, cols].astype(F32) for k in range(4)]
        zero = jnp.zeros((8, LANES), F32)
        turned = {}

        def turn(v, c, g, amount):
            if g < 0 or g >= groups:
                return zero
            key = (v, c, g, amount)
            if key not in turned:
                turned[key] = pltpu.roll(plane(v, c)[8 * g + 8 : 8 * g + 16, :], amount, 0)
            return turned[key]

        def plane(v, c):
            return ext.at[v, t] if c == 2 else shifted.at[c if c < 2 else c - 1, v, t]

        def five(v, c, g):
            ref = plane(v, c)
            load_at = lambda r: ref[8 * g + 8 + r : 8 * g + 16 + r, :]
            values = [load_at(r) for r in (-1, 0, 1)]
            if c in (0, 1, 3, 4):
                before = jnp.where(sub < 2, turn(v, c, g - 1, 2), turn(v, c, g, 2))
                after = jnp.where(sub < 6, turn(v, c, g, 6), turn(v, c, g + 1, 6))
            else:
                before, after = load_at(-2), load_at(2)
            return [before] + values + [after]

        for v in range(levels):
            for g in range(groups):
                band = slice(8 * g, 8 * g + 8)
                dr, dc = drow[band, cols], dcol[band, cols]
                row_high, row_low = dr >= 0, (dr & 1) == 1
                col_high, col_low = dc >= 0, (dc & 1) == 1
                w = [corner[k][band] for k in range(4)]
                picked = [choose_two(row_high, row_low, five(v, c, g)) for c in range(5)]
                upper = choose_two(col_high, col_low, [x[0] for x in picked])
                lower = choose_two(col_high, col_low, [x[1] for x in picked])
                total = w[0] * upper[0] + w[1] * upper[1] + w[2] * lower[0] + w[3] * lower[1]
                adv[v * rows + 8 * g : v * rows + 8 * g + 8, cols] = total
        return carry

    lax.fori_loop(0, tiles // 2, advect, 0)
    pl.semaphore_wait(round_sem.at[0], half - 1)
    tell(1, [across])
    lax.fori_loop(tiles // 2, tiles, advect, 0)

    load_tab.wait()
    tabs[...] = jnp.dot(order, tab[...], preferred_element_type=F32).astype(BF16)

    weights_in = rim_inputs.at[pl.ds(0, 64), :]
    pltpu.make_async_copy(weights_in, weights_in, load_sem.at[7]).wait()
    for q, ref in ((4, drow), (5, dcol)):
        for k in range(2):
            row0 = 16 * q + 8 * k
            rim_inputs[row0 : row0 + 8, :] = (
                ref[k * (rows - 8) : k * (rows - 8) + 8, :].astype(F32).astype(BF16)
            )
        for cols in (slice(0, LANES), slice(width - LANES, width)):
            points[q * rows : (q + 1) * rows, cols] = ref[:, cols].astype(F32).astype(BF16)
    iota_r = (6 * 16, 6 * 16)
    row_r, col_r = at(iota_r, 0), at(iota_r, 1)
    repeat_rows = one_hot(
        (lax.div(row_r, 8) == lax.div(col_r, 8))
        & ((col_r & 7) == (row_r & 1) + jnp.where((row_r & 15) < 8, 0, 6))
    )
    rim_points[...] = jnp.dot(repeat_rows, rim_inputs[...], preferred_element_type=F32)
    row_c, col_c = at((LANES, LANES), 0), at((LANES, LANES), 1)
    from_first = one_hot((col_c < HALF) & (row_c == (col_c & 1)))
    from_last = one_hot((col_c >= HALF) & (row_c == LANES - 2 + (col_c & 1)))
    side_points[...] = jnp.dot(
        points[:, 0:LANES], from_first, preferred_element_type=F32
    ) + jnp.dot(points[:, width - LANES :], from_last, preferred_element_type=F32)

    even = (at((8, LANES), 0) & 1) == 0

    def fix_rows(k):
        for c0 in range(0, 2 * levels, 8):
            blocks = [got_rim[k, t, c0 : c0 + 8, :].astype(F32) for t in range(tiles + 2)]
            moved = [move_blocks(blocks, move) for move in moves]
            moved.insert(2, blocks[1:-1])
            for t in range(tiles):
                cols = slice(t * LANES, (t + 1) * LANES)
                w0, w1, w2, w3, dr, dc = [
                    rim_points[16 * q + 8 * k : 16 * q + 8 * k + 8, cols] for q in range(6)
                ]
                col_high, col_low = dc >= 0.0, (dc == -1.0) | (dc == 1.0)
                same = [moved[c][t] for c in range(5)]
                other = [pltpu.roll(x, 1 if k else 7, 0) for x in same]
                s0, s1 = choose_two(col_high, col_low, same)
                o0, o1 = choose_two(col_high, col_low, other)
                if k == 0:
                    far = jnp.where(dr == -2.0, w0 * s0 + w1 * s1, 0.0)
                    near = jnp.where(
                        dr == -1.0, w0 * o0 + w1 * o1,
                        jnp.where(dr == -2.0, w2 * o0 + w3 * o1, 0.0),
                    )
                    near = jnp.where(even, near, 0.0)
                else:
                    far = jnp.where(dr == 1.0, w2 * s0 + w3 * s1, 0.0)
                    near = jnp.where(
                        dr == 1.0, w0 * o0 + w1 * o1,
                        jnp.where(dr == 0.0, w2 * o0 + w3 * o1, 0.0),
                    )
                    near = jnp.where(even, 0.0, near)
                extra = far + near
                for i in range(0, 8, 2):
                    row0 = (c0 + i) // 2 * rows + k * (rows - 2)
                    adv[row0 : row0 + 2, cols] += extra[i : i + 2]

    @pl.when(has_up)
    def _():
        pltpu.make_async_copy(got_rim.at[0], got_rim.at[0], halo_recv.at[0]).wait()
        fix_rows(0)

    @pl.when(has_down)
    def _():
        pltpu.make_async_copy(got_rim.at[1], got_rim.at[1], halo_recv.at[1]).wait()
        fix_rows(1)

    pltpu.make_async_copy(got_col, got_col, halo_recv.at[2]).wait()
    here = jnp.where(
        at((rows, LANES), 1) < HALF, got_col[0].astype(F32), got_col[1].astype(F32)
    )
    side[0, 8 : 8 + rows, :] = here
    side[1, 8 : 8 + rows, :] = jnp.where(
        at((rows, LANES), 1) < HALF, pltpu.roll(here, LANES - 1, 1), pltpu.roll(here, 1, 1)
    )
    in_west = lane < HALF
    edge = jnp.where(in_west, -1.0, 1.0)
    inner = (lane & 1) == jnp.where(in_west, 0, 1)
    for g in range(groups):
        w0, w1, w2, w3, dr, dc = [
            side_points[q * rows + 8 * g : q * rows + 8 * g + 8, :] for q in range(6)
        ]
        row_high, row_low = dr >= 0.0, (dr == -1.0) | (dr == 1.0)
        s0, s1 = choose_two(
            row_high, row_low, [side[0, 8 * g + 6 + r : 8 * g + 14 + r, :] for r in range(5)]
        )
        o0, o1 = choose_two(
            row_high, row_low, [side[1, 8 * g + 6 + r : 8 * g + 14 + r, :] for r in range(5)]
        )
        far = jnp.where(
            dc == jnp.where(in_west, -2.0, 1.0),
            jnp.where(in_west, w0, w1) * s0 + jnp.where(in_west, w2, w3) * s1,
            0.0,
        )
        near = jnp.where(
            dc == edge, w0 * o0 + w2 * o1,
            jnp.where(dc == edge - 1.0, w1 * o0 + w3 * o1, 0.0),
        )
        extra = far + jnp.where(inner, near, 0.0)
        for v in range(levels):
            band = slice(v * rows + 8 * g, v * rows + 8 * g + 8)
            west_part = pltpu.roll(extra, (LANES - 2 * v) % LANES, 1) if v else extra
            adv[band, 0:LANES] += jnp.where(lane < 2, west_part, 0.0)
            east_part = pltpu.roll(extra, (LANES - 2 - HALF - 2 * v) % LANES, 1)
            adv[band, width - LANES :] += jnp.where(lane >= LANES - 2, east_part, 0.0)

    contract_last = (((1,), (1,)), ((), ()))
    for v in range(levels):
        value = adv[v * rows : (v + 1) * rows, :]
        lead = value.astype(BF16)
        rest = (value - lead.astype(F32)).astype(BF16)
        both = lax.dot_general(tabs[...], lead, contract_last, preferred_element_type=F32)
        more = lax.dot_general(
            tabs[0 : 2 * waves, :], rest, contract_last, preferred_element_type=F32
        )
        coeffs = both[0 : 2 * waves] + both[2 * waves :] + more
        stage[v * waves : (v + 1) * waves, 0:rows] = coeffs[0:waves]
        stage[v * waves : (v + 1) * waves, HALF : HALF + rows] = coeffs[waves:]
    owners = half * n_lev
    for s in range(waves):
        for g in range(rep):
            send_1[s * rep + g] = stage[pl.ds(g * lv * waves + s, lv, stride=waves), :]

    turn_by = jnp.where(parity == 0, n_lat - 1, 1)

    def others(body):
        def column_of(a, first):
            lat = lax.rem(l + turn_by * a, n_lat)
            inside = lax.div(lat, half) == parity
            block = jnp.where(inside, lat, n_lat - 1 - lat) - parity * half
            base = lax.rem(lat, half) * n_lev

            def send(b):
                lev = lax.rem(e + b, n_lev)
                body(lat, lev, base + lev, block)

            each(first, n_lev)(send)

        each(1, n_lat)(lambda a: column_of(a, 0))
        column_of(0, 1)

    def start_1(lat, lev, owner, block):
        remote(send_1.at[owner], got_1.at[me], one_send, one_recv, lat, lev).start()

    pl.semaphore_wait(round_sem.at[1], 1)

    others(start_1)

    got_1[me] = send_1[lh * n_lev + e]

    spread_rows = 2 * waves * levels
    iota_w = (spread_rows, 2 * waves)
    repeat = one_hot(lax.div(at(iota_w, 0), levels) == at(iota_w, 1))
    for q in range(2):
        wide[q] = jnp.dot(
            repeat, tabs[2 * waves * q : 2 * waves * (q + 1), :], preferred_element_type=F32
        ).astype(BF16)

    at_row, at_col = at((LANES, LANES), 0), at((LANES, LANES), 1)
    flip = one_hot(
        ((at_row + at_col == rows - 1) & (at_row < HALF) & (at_col < HALF))
        | ((at_row + at_col == 2 * HALF + rows - 1) & (at_row >= HALF) & (at_col >= HALF))
    )
    sign = jnp.where(parity == 0, 1.0, -1.0).astype(F32)
    iota_e = (rows, 4 * LANES)
    row_e, col_e = at(iota_e, 0), at(iota_e, 1)
    part_e, lane_e = lax.div(col_e, LANES), lax.rem(col_e, LANES)
    place = HALF * lax.div(part_e, 2)
    natural = (lax.rem(part_e, 2) == 1) & (lane_e == row_e + place)
    turned = (lax.rem(part_e, 2) == 0) & (lane_e == rows - 1 - row_e + place)
    gather = (jnp.where(natural, sign, 0.0) + jnp.where(turned, 1.0, 0.0)).astype(BF16)

    wave_own = jnp.int32(0)
    for k in range(waves):
        wave_own = jnp.where(slot_ref[k] == slot, k, wave_own)
    wave_own = wave_own * (NT + 1) // waves
    column = lax.broadcasted_iota(jnp.int32, (2 * lv, steps), 1)
    degree = wave_own + 2 * column + parity
    factor = 1.0 / (
        1.0 + DAMPING * (degree * (degree + 1)).astype(F32) / float(NT * (NT + 1))
    )
    forward_scale = 1.0 / math.sqrt(rows * n_lat // 2)
    inverse_scale = math.sqrt(NLON) / math.sqrt(waves) / math.sqrt(steps)
    scale = jnp.where(wave_own == 0, inverse_scale, 2.0 * inverse_scale).astype(F32)

    legs = send_leg.at[pl.ds(0, half - 1)]
    pltpu.make_async_copy(legs, legs, leg_recv).wait()

    def all_of(ref, sem, count=n - 1):
        return pltpu.make_async_copy(ref.at[pl.ds(0, count)], ref.at[pl.ds(0, count)], sem)

    all_of(got_1, one_recv).wait()

    low = lax.broadcasted_iota(jnp.int32, (lv, LANES), 1) < HALF

    def total_1(lat):
        value = got_1[lat * n_lev]
        for d in range(1, n_lev):
            value = value + got_1[lat * n_lev + d]
        return value

    for b in range(0, half, 2):
        cols = slice(b * HALF, b * HALF + LANES)
        for which in range(2):
            lat = parity * half + b
            one = total_1(lat if which == 0 else n_lat - 1 - lat)
            two = total_1(lat + 1 if which == 0 else n_lat - 2 - lat)
            row0 = which * 2 * lv
            both_f[row0 : row0 + lv, cols] = jnp.where(low, one, pltpu.roll(two, HALF, 1))
            both_f[row0 + lv : row0 + 2 * lv, cols] = jnp.where(
                low, pltpu.roll(one, HALF, 1), two
            )
    near = both_f[0 : 2 * lv, :].astype(BF16)
    both_b[0 : 2 * lv, :] = near
    for c0 in range(0, half * HALF, LANES):
        cols = slice(c0, c0 + LANES)
        both_b[2 * lv :, cols] = jnp.dot(
            both_f[2 * lv :, cols].astype(BF16), flip, preferred_element_type=F32
        ).astype(BF16)
    matrix = basis[...].reshape(half * HALF, steps)
    raw = jnp.dot(both_b[...], matrix, preferred_element_type=F32)
    raw = (raw[2 * lv :] + sign * raw[0 : 2 * lv]) * forward_scale
    masked = jnp.where(degree <= NT, raw, 0.0)
    damped = masked * factor
    change = (damped - masked).astype(BF16)
    back = lax.dot_general(change, matrix, contract_last, preferred_element_type=F32) * scale
    both_f[0 : 2 * lv, :] = back
    for b in range(0, half, 2):
        cols = slice(b * HALF, b * HALF + LANES)
        real, imag = both_f[0:lv, cols], both_f[lv : 2 * lv, cols]
        send_2[b] = jnp.where(low, real, pltpu.roll(imag, HALF, 1))
        send_2[b + 1] = jnp.where(low, pltpu.roll(real, HALF, 1), imag)

    def start_2(lat, lev, owner, block):
        remote(send_2.at[block], got_2.at[me], two_send, two_recv, lat, lev).start()

    others(start_2)

    got_2[me] = send_2[lh]

    for vv in range(lv):
        for c in range(2):
            send_p[vv, c : c + 1, :] = damped[c * lv + vv : c * lv + vv + 1]
    home, place_p = lax.div(slot, own), lax.rem(slot, own)
    for vv in range(lv):
        lev = share * lv + vv
        mine = (home == l) & (lev == e)
        copy = remote(
            send_p.at[vv], got_p.at[2 * place_p + parity], p_send, p_recv, home, lev
        )
        pl.when(jnp.logical_not(mine))(copy.start)

        @pl.when(mine)
        def _():
            got_p[2 * place_p + parity] = send_p[vv]

    all_of(got_2, two_recv).wait()

    pairs = waves * levels
    for which in range(2):
        start = jnp.where(which == 1, parity, 1 - parity) * owners
        for o in range(owners):
            stage[which * pairs + o * lv : which * pairs + (o + 1) * lv, :] = got_2[start + o]
    for which in range(2):
        value = stage[which * pairs : (which + 1) * pairs, :]
        lead = value.astype(BF16)
        rest = (value - lead.astype(F32)).astype(BF16)
        for c in range(2):
            cols = slice((2 * c + which) * LANES, (2 * c + which + 1) * LANES)
            cross[0, c * pairs : (c + 1) * pairs, cols] = lead
            cross[1, c * pairs : (c + 1) * pairs, cols] = rest
    synth[...] = lax.dot_general(
        gather, cross[0], contract_last, preferred_element_type=F32
    ) + lax.dot_general(gather, cross[1], contract_last, preferred_element_type=F32)

    keeps = (home == l) & (share == lax.div(e, lv))
    spec_waits = [
        (keeps, all_of(got_p, p_recv, 2 * own - 1)),
        (jnp.logical_not(keeps), all_of(got_p, p_recv, 2 * own)),
    ]
    for case, copy in spec_waits:
        pl.when(case)(copy.wait)
    for k in range(2 * own):
        spec_ref[k] = got_p[k]

    pltpu.make_async_copy(got_col, got_col, halo_send.at[2]).wait()
    pltpu.make_async_copy(legs, legs, leg_send).wait()
    all_of(got_1, one_send).wait()
    all_of(got_2, two_send).wait()
    pl.when(keeps)(all_of(send_p, p_send, lv - 1).wait)
    pl.when(jnp.logical_not(keeps))(all_of(send_p, p_send, lv).wait)

    for k, there in ((0, has_down), (1, has_up)):
        pl.when(there)(
            pltpu.make_async_copy(got_rim.at[k], got_rim.at[k], halo_send.at[k]).wait
        )


def finish(adv, synth, wide, spec, out_hbm, spec_hbm, lead_all, rest_all, result, sems):
    levels, rows, width = result.shape
    spec_copy = pltpu.make_async_copy(spec, spec_hbm, sems.at[0])
    spec_copy.start()
    value = synth[...]
    lead = value.astype(BF16).astype(F32)
    rest = value - lead
    level_of = lax.rem(lax.broadcasted_iota(jnp.int32, value.shape, 1), levels)
    for v in range(levels):
        at = slice(v * rows, (v + 1) * rows)
        lead_all[at, :] = jnp.where(level_of == v, lead, 0.0).astype(BF16)
        rest_all[at, :] = jnp.where(level_of == v, rest, 0.0).astype(BF16)
    chunk = min(width, 256)
    copies = []
    for j in range(0, width, chunk):
        cols = slice(j, j + chunk)
        increment = (
            jnp.dot(lead_all[...], wide[0, :, cols], preferred_element_type=F32)
            + jnp.dot(lead_all[...], wide[1, :, cols], preferred_element_type=F32)
            + jnp.dot(rest_all[...], wide[0, :, cols], preferred_element_type=F32)
        )
        updated = adv[:, cols] + increment
        for v in range(levels):
            result[v, :, cols] = updated[v * rows : (v + 1) * rows]
        copy = pltpu.make_async_copy(
            result.at[:, :, cols], out_hbm.at[:, :, cols], sems.at[1 + j // chunk]
        )
        copy.start()
        copies.append(copy)
    for copy in copies + [spec_copy]:
        copy.wait()


def solution(mesh):
    n_lat, n_lev = mesh.shape["lat"], mesh.shape["lev"]

    def on_device(field, weights, depart_row, depart_col, legendre, wave_slot):
        levels, rows, width = field.shape
        _, waves, steps = legendre.shape
        tiles = width // LANES
        own = waves // n_lat
        n, half = n_lat * n_lev, n_lat // 2
        owners = half * n_lev
        rep = n_lev // (waves // half)
        lv = levels // rep
        pairs = waves * levels
        table = jnp.asarray(lon_table(waves))
        vmem, dma = pltpu.VMEM, pltpu.SemaphoreType.DMA
        anywhere = pl.BlockSpec(memory_space=pltpu.HBM)
        in_vmem = pl.BlockSpec(memory_space=pltpu.VMEM)
        adv, synth, wide, spec = pl.pallas_call(
            functools.partial(kernel, n_lat, n_lev),
            out_shape=(
                vmem((levels * rows, width), F32),
                vmem((rows, 2 * pairs), F32),
                vmem((2, 2 * pairs, width), BF16),
                vmem((2 * own, 2, steps), F32),
            ),
            in_specs=[anywhere] * 7,
            out_specs=(in_vmem,) * 4,
            scratch_shapes=[
                pltpu.SMEM((waves,), jnp.int32),
                vmem((levels, tiles, rows + 16, LANES), F32),
                vmem((4, levels, tiles, rows + 16, LANES), F32),
                vmem((6 * rows, width), BF16),
                vmem((rows, width), jnp.int32),
                vmem((rows, width), jnp.int32),
                vmem((rows * waves, steps), BF16),
                vmem((4 * waves, width), BF16),
                vmem((4 * waves, width), BF16),
                vmem((2, tiles, 2 * levels, LANES), F32),
                vmem((2, tiles, 2 * levels, LANES), BF16),
                vmem((2, rows, LANES), BF16),
                vmem((2, tiles + 2, 2 * levels, LANES), BF16),
                vmem((2, rows, LANES), BF16),
                vmem((6 * 16, width), BF16),
                vmem((6 * 16, width), F32),
                vmem((6 * rows, LANES), F32),
                vmem((2, rows + 16, LANES), F32),
                vmem((half, rows, steps), BF16),
                vmem((half, HALF, steps), BF16),
                vmem((2 * pairs, LANES), F32),
                vmem((owners, lv, LANES), F32),
                vmem((n, lv, LANES), F32),
                vmem((4 * lv, half * HALF), F32),
                vmem((4 * lv, half * HALF), BF16),
                vmem((half, lv, LANES), F32),
                vmem((n, lv, LANES), F32),
                vmem((2, 2 * pairs, 4 * LANES), BF16),
                vmem((lv, 2, steps), F32),
                vmem((2 * own, 2, steps), F32),
                dma((8,)),
                dma((3,)), dma((3,)),
                dma, dma,
                dma, dma,
                dma, dma,
                dma, dma,
                pltpu.SemaphoreType.REGULAR((2,)),
            ],
            compiler_params=pltpu.CompilerParams(
                collective_id=0, has_side_effects=True, vmem_limit_bytes=40 << 20
            ),
        )(
            *(
                pltpu.with_memory_space_constraint(x, pltpu.HBM)
                for x in (
                    wave_slot, field, weights.reshape(4 * rows, width), depart_row, depart_col,
                    legendre.reshape(rows * waves, steps), table,
                )
            ),
        )
        chunks = width // min(width, 256)
        updated, spectral = pl.pallas_call(
            finish,
            out_shape=(
                jax.ShapeDtypeStruct((levels, rows, width), F32),
                jax.ShapeDtypeStruct((2 * own, 2, steps), F32),
            ),
            in_specs=[in_vmem] * 4,
            out_specs=(anywhere,) * 2,
            scratch_shapes=[
                vmem((levels * rows, 2 * pairs), BF16),
                vmem((levels * rows, 2 * pairs), BF16),
                vmem((levels, rows, width), F32),
                dma((1 + chunks,)),
            ],
            compiler_params=pltpu.CompilerParams(vmem_limit_bytes=20 << 20),
        )(*(pltpu.with_memory_space_constraint(x, vmem) for x in (adv, synth, wide, spec)))
        return updated, spectral.reshape(own, 2, 1, 2, steps)

    placed = (
        P(None, "lat", "lev"),
        P(None, "lat", "lev"),
        P("lat", "lev"),
        P("lat", "lev"),
        P("lat", None, None),
        P(),
    )
    return jax.shard_map(
        on_device,
        mesh=mesh,
        in_specs=placed,
        out_specs=(P(None, "lat", "lev"), P("lat", None, "lev", None, None)),
        check_vma=False,
    )
```

```python
import functools
import math

import jax
import jax.numpy as jnp
import numpy as np
from jax import lax
from jax.experimental import pallas as pl
from jax.experimental.pallas import tpu as pltpu
from jax.sharding import PartitionSpec as P

NLON = 4096
NT = 1279
DAMPING = 4.0
LANES = 128
HALF = 64
MESH = pl.DeviceIdType.MESH
F32 = jnp.float32
BF16 = jnp.bfloat16


def lon_table(waves):
    m = (np.arange(waves, dtype=np.int64) * (NT + 1)) // waves
    phases = (m[:, None] * np.arange(NLON, dtype=np.int64)[None, :]) % NLON
    angles = phases.astype(np.float64) * (2.0 * math.pi / NLON)
    table = np.concatenate([np.cos(angles), -np.sin(angles)], axis=0) / math.sqrt(NLON)
    table = table.astype(np.float32)
    lead = table.astype(BF16)
    rest = (table - lead.astype(np.float32)).astype(BF16)
    return np.concatenate([lead, rest], axis=0)


def each(start, stop):
    def run(body):
        if stop - start <= 64:
            for i in range(start, stop):
                body(i)
        else:
            lax.fori_loop(start, stop, lambda i, carry: (body(i), carry)[1], 0)

    return run


def one_hot(mask):
    return jnp.where(mask, 1.0, 0.0).astype(BF16)


def kernel(
    n_lat, n_lev,
    slot_hbm, field_hbm, weights_hbm, drow_hbm, dcol_hbm, leg_hbm, table_hbm,
    adv, synth, wide, spec_ref,
    slot_ref, ext, shifted, points, drow, dcol, leg, tab, tabs,
    rim_rows, pack_row, pack_col, got_rim, got_col, rim_inputs, rim_points, side_points, side,
    send_leg, basis, stage, send_1, got_1, both_f, send_2, got_2, cross, send_p, got_p,
    load_sem, halo_send, halo_recv, leg_send, leg_recv, one_send, one_recv,
    two_send, two_recv, p_send, p_recv, round_sem,
):
    levels, _, _, _ = ext.shape
    rows, width = drow.shape
    tiles = width // LANES
    steps = leg.shape[1]
    waves = leg.shape[0] // rows
    n = n_lat * n_lev
    half = n_lat // 2
    group = waves // half
    rep = n_lev // group
    lv = levels // rep
    own = waves // n_lat
    l, e = lax.axis_index("lat"), lax.axis_index("lev")
    me = l * n_lev + e
    parity, lh = lax.div(l, half), lax.rem(l, half)
    share = lax.rem(e, rep)
    slot = group * lh + lax.div(e, rep)
    has_up, has_down = l > 0, l < n_lat - 1
    east, west = lax.rem(e + 1, n_lev), lax.rem(e + n_lev - 1, n_lev)

    barrier = pltpu.get_barrier_semaphore()

    def greet(lat, lev):
        pl.semaphore_signal(barrier, inc=1, device_id=(lat, lev), device_id_type=MESH)

    column = [(parity * half + lax.rem(lh + off, half), e) for off in range(1, half)]
    across = (lax.rem(l + half, n_lat), e)
    partners = [(l, lax.rem(e + off, n_lev)) for off in range(1, n_lev)]
    partners += column + [across]
    for there, lat in ((has_down, l + 1), (has_up, l - 1)):

        @pl.when(there)
        def _():
            for lev in (e, east, west):
                greet(lat, lev)

    for lat, lev in partners:
        greet(lat, lev)
    n_greet = len(partners) + jnp.where(has_up, 3, 0) + jnp.where(has_down, 3, 0)

    def load(k, src, dst):
        copy = pltpu.make_async_copy(src, dst, load_sem.at[k])
        copy.start()
        return copy

    inner_rows = pl.ds(16, rows - 16)
    inner_field = pl.ds(8, rows - 16)
    for t in range(tiles):
        cols = pl.ds(t * LANES, LANES)
        load(0, field_hbm.at[:, pl.ds(0, 8), cols], ext.at[:, t, pl.ds(8, 8), :])
        load(0, field_hbm.at[:, pl.ds(rows - 8, 8), cols], ext.at[:, t, pl.ds(rows, 8), :])
    for t in range(tiles):
        cols = pl.ds(t * LANES, LANES)
        k = 8 if t in (0, tiles - 1) else 9
        for v in range(levels):
            load(k, field_hbm.at[v, inner_field, cols], ext.at[v, t, inner_rows, :])
    load_leg = load(1, leg_hbm, leg)
    load_slot = load(2, slot_hbm, slot_ref)
    load_wts = load(3, weights_hbm, points.at[pl.ds(0, 4 * rows), :])
    for q in range(4):
        for k in range(2):
            load(
                7, weights_hbm.at[pl.ds(q * rows + k * (rows - 8), 8), :],
                rim_inputs.at[pl.ds(16 * q + 8 * k, 8), :],
            )
    load_row = load(4, drow_hbm, drow)
    load_col = load(5, dcol_hbm, dcol)
    load_tab = load(
        6, table_hbm.at[:, pl.ds(pl.multiple_of(e * width, LANES), width)], tab
    )

    def tell(k, devices):
        for there in devices:
            pl.semaphore_signal(round_sem.at[k], inc=1, device_id=there, device_id_type=MESH)

    at = lambda shape, dim: lax.broadcasted_iota(jnp.int32, shape, dim)
    for row0 in (0, rows + 8):
        zero = jnp.zeros((levels, tiles, 8, LANES), F32)
        ext[:, :, row0 : row0 + 8, :] = zero
        for move in range(4):
            shifted[move, :, :, row0 : row0 + 8, :] = zero
        for k in range(2):
            side[k, row0 : row0 + 8, :] = zero[0, 0]
    stage[...] = jnp.zeros_like(stage)
    cross[...] = jnp.zeros_like(cross)
    padded = send_leg.shape[1]
    basis[:half, padded:, :] = jnp.zeros((half, HALF - padded, steps), BF16)

    lane = at((rows, LANES), 1)
    outer_part = adv.at[pl.ds(0, 16 * levels), :]
    pltpu.make_async_copy(outer_part, outer_part, load_sem.at[0]).wait()
    edge_part = ext.at[:, pl.ds(0, 2), inner_rows, :]
    pltpu.make_async_copy(edge_part, edge_part, load_sem.at[8]).wait()
    for v in range(levels):
        for t in range(tiles):
            rim_rows[0, t, 2 * v : 2 * v + 2, :] = ext[v, t, 6 + rows : 8 + rows, :]
            rim_rows[1, t, 2 * v : 2 * v + 2, :] = ext[v, t, 8:10, :]
    pack_row[...] = rim_rows[...].astype(BF16)
    last = jnp.zeros((rows, LANES), F32)
    first = jnp.zeros((rows, LANES), F32)
    for v in range(levels):
        tail = pltpu.roll(ext[v, tiles - 1, 8 : 8 + rows, :], (2 * v + 2) % LANES, 1)
        last = jnp.where(lax.div(lane, 2) == v, tail, last)
        head = pltpu.roll(ext[v, 0, 8 : 8 + rows, :], HALF + 2 * v, 1)
        first = jnp.where(lax.div(lane - HALF, 2) == v, head, first)
    pack_col[0] = last.astype(BF16)
    pack_col[1] = first.astype(BF16)

    def remote(src, dst, ssem, rsem, lat, lev):
        return pltpu.make_async_remote_copy(
            src_ref=src, dst_ref=dst, send_sem=ssem, recv_sem=rsem,
            device_id=(lat, lev), device_id_type=MESH,
        )

    def halo(k, src, dst, lat, lev):
        return remote(src, dst, halo_send.at[k], halo_recv.at[k], lat, lev)

    flat = [
        halo(2, pack_col.at[0], got_col.at[0], l, east),
        halo(2, pack_col.at[1], got_col.at[1], l, west),
    ]
    rims = [
        [
            halo(k, pack_row.at[k], got_rim.at[k, pl.ds(1, tiles)], lat, e),
            halo(k, pack_row.at[k, tiles - 1], got_rim.at[k, 0], lat, east),
            halo(k, pack_row.at[k, 0], got_rim.at[k, tiles + 1], lat, west),
        ]
        for k, lat in ((0, l + 1), (1, l - 1))
    ]

    pl.semaphore_wait(barrier, n_greet)

    @pl.when(has_down)
    def _():
        for copy in rims[0]:
            copy.start()

    @pl.when(has_up)
    def _():
        for copy in rims[1]:
            copy.start()

    for copy in flat:
        copy.start()

    tell(0, column)

    if tiles > 2:
        other_part = ext.at[:, pl.ds(0, tiles - 2), inner_rows, :]
        pltpu.make_async_copy(other_part, other_part, load_sem.at[9]).wait()
    load_slot.wait()
    load_leg.wait()
    load_tab.wait()
    load_wts.wait()
    load_row.wait()
    load_col.wait()
    weights_in = rim_inputs.at[pl.ds(0, 64), :]
    pltpu.make_async_copy(weights_in, weights_in, load_sem.at[7]).wait()
    first = lax.broadcasted_iota(jnp.int32, (1, 4 * waves), 1)
    slot_row = jnp.zeros((1, 4 * waves), jnp.int32)
    for k in range(waves):
        slot_row = jnp.where(lax.rem(first, waves) == k, slot_ref[k], slot_row)
    iota_f = (4 * waves, 4 * waves)
    order = one_hot(
        (lax.div(at(iota_f, 0), waves) == lax.div(at(iota_f, 1), waves))
        & (lax.rem(at(iota_f, 0), waves) == slot_row)
    )
    lane = at((8, LANES), 1)
    moves = (-2, -1, 1, 2)

    def move_blocks(blocks, move):
        turned = [x if x is None else pltpu.roll(x, (-move) % LANES, 1) for x in blocks]
        zero = jnp.zeros((8, LANES), F32)
        result = []
        for t in range(1, len(blocks) - 1):
            near = turned[t - 1] if move < 0 else turned[t + 1]
            wrapped = (lane < -move) if move < 0 else (lane >= LANES - move)
            result.append(jnp.where(wrapped, zero if near is None else near, turned[t]))
        return result

    groups = rows // 8

    def shift_level(v):
        for g in range(groups):
            band = slice(8 + 8 * g, 16 + 8 * g)
            blocks = [None] + [ext[v, t, band, :] for t in range(tiles)] + [None]
            for k, move in enumerate(moves):
                for t, value in enumerate(move_blocks(blocks, move)):
                    shifted[k, v, t, band, :] = value

    for v in range(levels):
        shift_level(v)

    band = 8
    iota_g = (half * band, band * waves)
    slot_cols = jnp.zeros((1, band * waves), jnp.int32)
    lane_k = lax.rem(lax.broadcasted_iota(jnp.int32, (1, band * waves), 1), waves)
    for k in range(waves):
        slot_cols = jnp.where(lane_k == k, slot_ref[k], slot_cols)
    choose = one_hot(
        (lax.rem(at(iota_g, 0), band) == lax.div(at(iota_g, 1), waves))
        & (group * lax.div(at(iota_g, 0), band) + lax.div(e, rep) == slot_cols)
    )
    for i in range(0, rows, band):
        picked = jnp.dot(
            choose, leg[i * waves : (i + band) * waves, :], preferred_element_type=F32
        ).astype(BF16)
        for t in range(half):
            send_leg[t, i : i + band, :] = picked[t * band : (t + 1) * band]
    tabs[...] = jnp.dot(order, tab[...], preferred_element_type=F32).astype(BF16)

    for q, ref in ((4, drow), (5, dcol)):
        for k in range(2):
            row0 = 16 * q + 8 * k
            rim_inputs[row0 : row0 + 8, :] = (
                ref[k * (rows - 8) : k * (rows - 8) + 8, :].astype(F32).astype(BF16)
            )
        for cols in (slice(0, LANES), slice(width - LANES, width)):
            points[q * rows : (q + 1) * rows, cols] = ref[:, cols].astype(F32).astype(BF16)
    iota_r = (6 * 16, 6 * 16)
    row_r, col_r = at(iota_r, 0), at(iota_r, 1)
    repeat_rows = one_hot(
        (lax.div(row_r, 8) == lax.div(col_r, 8))
        & ((col_r & 7) == (row_r & 1) + jnp.where((row_r & 15) < 8, 0, 6))
    )
    rim_points[...] = jnp.dot(repeat_rows, rim_inputs[...], preferred_element_type=F32)
    row_c, col_c = at((LANES, LANES), 0), at((LANES, LANES), 1)
    from_first = one_hot((col_c < HALF) & (row_c == (col_c & 1)))
    from_last = one_hot((col_c >= HALF) & (row_c == LANES - 2 + (col_c & 1)))
    side_points[...] = jnp.dot(
        points[:, 0:LANES], from_first, preferred_element_type=F32
    ) + jnp.dot(points[:, width - LANES :], from_last, preferred_element_type=F32)

    def choose_two(high, low, values):
        one = jnp.where(high, values[2], values[0])
        two = jnp.where(high, values[3], values[1])
        three = jnp.where(high, values[4], values[2])
        return jnp.where(low, two, one), jnp.where(low, three, two)


    sub = at((8, LANES), 0)

    def advect(t, carry):
        cols = pl.ds(pl.multiple_of(t * LANES, LANES), LANES)
        corner = [points[k * rows : (k + 1) * rows, cols].astype(F32) for k in range(4)]
        zero = jnp.zeros((8, LANES), F32)
        turned = {}

        def turn(v, c, g, amount):
            if g < 0 or g >= groups:
                return zero
            key = (v, c, g, amount)
            if key not in turned:
                turned[key] = pltpu.roll(plane(v, c)[8 * g + 8 : 8 * g + 16, :], amount, 0)
            return turned[key]

        def plane(v, c):
            return ext.at[v, t] if c == 2 else shifted.at[c if c < 2 else c - 1, v, t]

        def five(v, c, g):
            ref = plane(v, c)
            load_at = lambda r: ref[8 * g + 8 + r : 8 * g + 16 + r, :]
            values = [load_at(r) for r in (-1, 0, 1)]
            if c in (0, 1, 3, 4):
                before = jnp.where(sub < 2, turn(v, c, g - 1, 2), turn(v, c, g, 2))
                after = jnp.where(sub < 6, turn(v, c, g, 6), turn(v, c, g + 1, 6))
            else:
                before, after = load_at(-2), load_at(2)
            return [before] + values + [after]

        for v in range(levels):
            for g in range(groups):
                band = slice(8 * g, 8 * g + 8)
                dr, dc = drow[band, cols], dcol[band, cols]
                row_high, row_low = dr >= 0, (dr & 1) == 1
                col_high, col_low = dc >= 0, (dc & 1) == 1
                w = [corner[k][band] for k in range(4)]
                picked = [choose_two(row_high, row_low, five(v, c, g)) for c in range(5)]
                upper = choose_two(col_high, col_low, [x[0] for x in picked])
                lower = choose_two(col_high, col_low, [x[1] for x in picked])
                total = w[0] * upper[0] + w[1] * upper[1] + w[2] * lower[0] + w[3] * lower[1]
                adv[v * rows + 8 * g : v * rows + 8 * g + 8, cols] = total
        return carry

    lax.fori_loop(0, tiles // 2, advect, 0)
    pl.semaphore_wait(round_sem.at[0], half - 1)
    tell(1, [across])
    slots_of = lambda t: basis.at[t, pl.ds(0, padded), :]
    copies_g = []
    for off in range(1, half):
        t = lax.rem(lh + off, half)
        copy = remote(
            send_leg.at[t], slots_of(lh), leg_send, leg_recv,
            parity * half + t, e,
        )
        copy.start()
        copies_g.append(copy)
    basis[lh, 0:padded, :] = send_leg[lh]


    lax.fori_loop(tiles // 2, tiles, advect, 0)

    even = (at((8, LANES), 0) & 1) == 0

    def fix_rows(k):
        for c0 in range(0, 2 * levels, 8):
            blocks = [got_rim[k, t, c0 : c0 + 8, :].astype(F32) for t in range(tiles + 2)]
            moved = [move_blocks(blocks, move) for move in moves]
            moved.insert(2, blocks[1:-1])
            for t in range(tiles):
                cols = slice(t * LANES, (t + 1) * LANES)
                w0, w1, w2, w3, dr, dc = [
                    rim_points[16 * q + 8 * k : 16 * q + 8 * k + 8, cols] for q in range(6)
                ]
                col_high, col_low = dc >= 0.0, (dc == -1.0) | (dc == 1.0)
                same = [moved[c][t] for c in range(5)]
                other = [pltpu.roll(x, 1 if k else 7, 0) for x in same]
                s0, s1 = choose_two(col_high, col_low, same)
                o0, o1 = choose_two(col_high, col_low, other)
                if k == 0:
                    far = jnp.where(dr == -2.0, w0 * s0 + w1 * s1, 0.0)
                    near = jnp.where(
                        dr == -1.0, w0 * o0 + w1 * o1,
                        jnp.where(dr == -2.0, w2 * o0 + w3 * o1, 0.0),
                    )
                    near = jnp.where(even, near, 0.0)
                else:
                    far = jnp.where(dr == 1.0, w2 * s0 + w3 * s1, 0.0)
                    near = jnp.where(
                        dr == 1.0, w0 * o0 + w1 * o1,
                        jnp.where(dr == 0.0, w2 * o0 + w3 * o1, 0.0),
                    )
                    near = jnp.where(even, 0.0, near)
                extra = far + near
                for i in range(0, 8, 2):
                    row0 = (c0 + i) // 2 * rows + k * (rows - 2)
                    adv[row0 : row0 + 2, cols] += extra[i : i + 2]

    @pl.when(has_up)
    def _():
        pltpu.make_async_copy(got_rim.at[0], got_rim.at[0], halo_recv.at[0]).wait()
        fix_rows(0)

    @pl.when(has_down)
    def _():
        pltpu.make_async_copy(got_rim.at[1], got_rim.at[1], halo_recv.at[1]).wait()
        fix_rows(1)

    pltpu.make_async_copy(got_col, got_col, halo_recv.at[2]).wait()
    here = jnp.where(
        at((rows, LANES), 1) < HALF, got_col[0].astype(F32), got_col[1].astype(F32)
    )
    side[0, 8 : 8 + rows, :] = here
    side[1, 8 : 8 + rows, :] = jnp.where(
        at((rows, LANES), 1) < HALF, pltpu.roll(here, LANES - 1, 1), pltpu.roll(here, 1, 1)
    )
    in_west = lane < HALF
    edge = jnp.where(in_west, -1.0, 1.0)
    inner = (lane & 1) == jnp.where(in_west, 0, 1)
    for g in range(groups):
        w0, w1, w2, w3, dr, dc = [
            side_points[q * rows + 8 * g : q * rows + 8 * g + 8, :] for q in range(6)
        ]
        row_high, row_low = dr >= 0.0, (dr == -1.0) | (dr == 1.0)
        s0, s1 = choose_two(
            row_high, row_low, [side[0, 8 * g + 6 + r : 8 * g + 14 + r, :] for r in range(5)]
        )
        o0, o1 = choose_two(
            row_high, row_low, [side[1, 8 * g + 6 + r : 8 * g + 14 + r, :] for r in range(5)]
        )
        far = jnp.where(
            dc == jnp.where(in_west, -2.0, 1.0),
            jnp.where(in_west, w0, w1) * s0 + jnp.where(in_west, w2, w3) * s1,
            0.0,
        )
        near = jnp.where(
            dc == edge, w0 * o0 + w2 * o1,
            jnp.where(dc == edge - 1.0, w1 * o0 + w3 * o1, 0.0),
        )
        extra = far + jnp.where(inner, near, 0.0)
        for v in range(levels):
            band = slice(v * rows + 8 * g, v * rows + 8 * g + 8)
            west_part = pltpu.roll(extra, (LANES - 2 * v) % LANES, 1) if v else extra
            adv[band, 0:LANES] += jnp.where(lane < 2, west_part, 0.0)
            east_part = pltpu.roll(extra, (LANES - 2 - HALF - 2 * v) % LANES, 1)
            adv[band, width - LANES :] += jnp.where(lane >= LANES - 2, east_part, 0.0)

    contract_last = (((1,), (1,)), ((), ()))
    for v in range(levels):
        value = adv[v * rows : (v + 1) * rows, :]
        lead = value.astype(BF16)
        rest = (value - lead.astype(F32)).astype(BF16)
        both = lax.dot_general(tabs[...], lead, contract_last, preferred_element_type=F32)
        more = lax.dot_general(
            tabs[0 : 2 * waves, :], rest, contract_last, preferred_element_type=F32
        )
        coeffs = both[0 : 2 * waves] + both[2 * waves :] + more
        stage[v * waves : (v + 1) * waves, 0:rows] = coeffs[0:waves]
        stage[v * waves : (v + 1) * waves, HALF : HALF + rows] = coeffs[waves:]
    owners = half * n_lev
    for s in range(waves):
        for g in range(rep):
            send_1[s * rep + g] = stage[pl.ds(g * lv * waves + s, lv, stride=waves), :]

    turn_by = jnp.where(parity == 0, n_lat - 1, 1)

    def others(body):
        def column_of(a, first):
            lat = lax.rem(l + turn_by * a, n_lat)
            inside = lax.div(lat, half) == parity
            block = jnp.where(inside, lat, n_lat - 1 - lat) - parity * half
            base = lax.rem(lat, half) * n_lev

            def send(b):
                lev = lax.rem(e + b, n_lev)
                body(lat, lev, base + lev, block)

            each(first, n_lev)(send)

        each(1, n_lat)(lambda a: column_of(a, 0))
        column_of(0, 1)

    def start_1(lat, lev, owner, block):
        remote(send_1.at[owner], got_1.at[me], one_send, one_recv, lat, lev).start()

    pl.semaphore_wait(round_sem.at[1], 1)

    others(start_1)

    got_1[me] = send_1[lh * n_lev + e]

    spread_rows = 2 * waves * levels
    iota_w = (spread_rows, 2 * waves)
    repeat = one_hot(lax.div(at(iota_w, 0), levels) == at(iota_w, 1))
    for q in range(2):
        wide[q] = jnp.dot(
            repeat, tabs[2 * waves * q : 2 * waves * (q + 1), :], preferred_element_type=F32
        ).astype(BF16)

    at_row, at_col = at((LANES, LANES), 0), at((LANES, LANES), 1)
    flip = one_hot(
        ((at_row + at_col == rows - 1) & (at_row < HALF) & (at_col < HALF))
        | ((at_row + at_col == 2 * HALF + rows - 1) & (at_row >= HALF) & (at_col >= HALF))
    )
    sign = jnp.where(parity == 0, 1.0, -1.0).astype(F32)
    iota_e = (rows, 4 * LANES)
    row_e, col_e = at(iota_e, 0), at(iota_e, 1)
    part_e, lane_e = lax.div(col_e, LANES), lax.rem(col_e, LANES)
    place = HALF * lax.div(part_e, 2)
    natural = (lax.rem(part_e, 2) == 1) & (lane_e == row_e + place)
    turned = (lax.rem(part_e, 2) == 0) & (lane_e == rows - 1 - row_e + place)
    gather = (jnp.where(natural, sign, 0.0) + jnp.where(turned, 1.0, 0.0)).astype(BF16)

    wave_own = jnp.int32(0)
    for k in range(waves):
        wave_own = jnp.where(slot_ref[k] == slot, k, wave_own)
    wave_own = wave_own * (NT + 1) // waves
    column = lax.broadcasted_iota(jnp.int32, (2 * lv, steps), 1)
    degree = wave_own + 2 * column + parity
    factor = 1.0 / (
        1.0 + DAMPING * (degree * (degree + 1)).astype(F32) / float(NT * (NT + 1))
    )
    forward_scale = 1.0 / math.sqrt(rows * n_lat // 2)
    inverse_scale = math.sqrt(NLON) / math.sqrt(waves) / math.sqrt(steps)
    scale = jnp.where(wave_own == 0, inverse_scale, 2.0 * inverse_scale).astype(F32)

    legs = send_leg.at[pl.ds(0, half - 1)]
    pltpu.make_async_copy(legs, legs, leg_recv).wait()

    def all_of(ref, sem, count=n - 1):
        return pltpu.make_async_copy(ref.at[pl.ds(0, count)], ref.at[pl.ds(0, count)], sem)

    for b in range(0, half, 2):
        turned = jnp.dot(
            flip, basis[b : b + 2].reshape(LANES, steps), preferred_element_type=F32
        ).astype(BF16)
        basis[half + b : half + b + 2] = turned.reshape(2, HALF, steps)

    all_of(got_1, one_recv).wait()

    low = lax.broadcasted_iota(jnp.int32, (lv, LANES), 1) < HALF

    def total_1(lat):
        value = got_1[lat * n_lev]
        for d in range(1, n_lev):
            value = value + got_1[lat * n_lev + d]
        return value

    for which in range(2):
        for b in range(0, half, 2):
            lat = parity * half + b
            one = total_1(lat if which == 0 else n_lat - 1 - lat)
            two = total_1(lat + 1 if which == 0 else n_lat - 2 - lat)
            col0 = (which * half + b) * HALF
            cols = slice(col0, col0 + LANES)
            both_f[0:lv, cols] = jnp.where(low, one, pltpu.roll(two, HALF, 1))
            both_f[lv:, cols] = jnp.where(low, pltpu.roll(one, HALF, 1), two)
    inside = half * HALF
    terms = both_f[...].astype(BF16)
    matrix = basis[...].reshape(2 * inside, steps)
    raw = sign * jnp.dot(
        terms[:, :inside], matrix[:inside], preferred_element_type=F32
    ) + jnp.dot(terms[:, inside:], matrix[inside:], preferred_element_type=F32)
    raw = raw * forward_scale
    masked = jnp.where(degree <= NT, raw, 0.0)
    damped = masked * factor
    change = (damped - masked).astype(BF16)
    back = lax.dot_general(
        change, matrix[:inside], contract_last, preferred_element_type=F32
    )
    both_f[:, :inside] = back * scale
    for b in range(0, half, 2):
        cols = slice(b * HALF, b * HALF + LANES)
        real, imag = both_f[0:lv, cols], both_f[lv:, cols]
        send_2[b] = jnp.where(low, real, pltpu.roll(imag, HALF, 1)).astype(BF16)
        send_2[b + 1] = jnp.where(low, pltpu.roll(real, HALF, 1), imag).astype(BF16)

    def start_2(lat, lev, owner, block):
        remote(send_2.at[block], got_2.at[me], two_send, two_recv, lat, lev).start()

    others(start_2)

    got_2[me] = send_2[lh]

    for vv in range(lv):
        for c in range(2):
            send_p[vv, c : c + 1, :] = damped[c * lv + vv : c * lv + vv + 1]
    home, place_p = lax.div(slot, own), lax.rem(slot, own)
    for vv in range(lv):
        lev = share * lv + vv
        mine = (home == l) & (lev == e)
        copy = remote(
            send_p.at[vv], got_p.at[2 * place_p + parity], p_send, p_recv, home, lev
        )
        pl.when(jnp.logical_not(mine))(copy.start)

        @pl.when(mine)
        def _():
            got_p[2 * place_p + parity] = send_p[vv]

    all_of(got_2, two_recv).wait()

    pairs = waves * levels
    for which in range(2):
        start = jnp.where(which == 1, parity, 1 - parity) * owners
        for o in range(owners):
            stage[which * pairs + o * lv : which * pairs + (o + 1) * lv, :] = got_2[
                start + o
            ].astype(F32)
    for which in range(2):
        value = stage[which * pairs : (which + 1) * pairs, :].astype(BF16)
        for c in range(2):
            cols = slice((2 * c + which) * LANES, (2 * c + which + 1) * LANES)
            cross[c * pairs : (c + 1) * pairs, cols] = value
    synth[...] = lax.dot_general(
        gather, cross[...], contract_last, preferred_element_type=F32
    )

    keeps = (home == l) & (share == lax.div(e, lv))
    spec_waits = [
        (keeps, all_of(got_p, p_recv, 2 * own - 1)),
        (jnp.logical_not(keeps), all_of(got_p, p_recv, 2 * own)),
    ]
    for case, copy in spec_waits:
        pl.when(case)(copy.wait)
    for k in range(2 * own):
        spec_ref[k] = got_p[k]

    pltpu.make_async_copy(got_col, got_col, halo_send.at[2]).wait()
    pltpu.make_async_copy(legs, legs, leg_send).wait()
    all_of(got_1, one_send).wait()
    all_of(got_2, two_send).wait()
    pl.when(keeps)(all_of(send_p, p_send, lv - 1).wait)
    pl.when(jnp.logical_not(keeps))(all_of(send_p, p_send, lv).wait)

    for k, there in ((0, has_down), (1, has_up)):
        pl.when(there)(
            pltpu.make_async_copy(got_rim.at[k], got_rim.at[k], halo_send.at[k]).wait
        )


def finish(adv, synth, wide, spec, out_hbm, spec_hbm, lead_all, rest_all, result, sems):
    levels, rows, width = result.shape
    spec_copy = pltpu.make_async_copy(spec, spec_hbm, sems.at[0])
    spec_copy.start()
    value = synth[...]
    lead = value.astype(BF16).astype(F32)
    rest = value - lead
    level_of = lax.rem(lax.broadcasted_iota(jnp.int32, value.shape, 1), levels)
    for v in range(levels):
        at = slice(v * rows, (v + 1) * rows)
        lead_all[at, :] = jnp.where(level_of == v, lead, 0.0).astype(BF16)
        rest_all[at, :] = jnp.where(level_of == v, rest, 0.0).astype(BF16)
    chunk = min(width, 256)
    for j in range(0, width, chunk):
        cols = slice(j, j + chunk)
        increment = (
            jnp.dot(lead_all[...], wide[0, :, cols], preferred_element_type=F32)
            + jnp.dot(lead_all[...], wide[1, :, cols], preferred_element_type=F32)
            + jnp.dot(rest_all[...], wide[0, :, cols], preferred_element_type=F32)
        )
        updated = adv[:, cols] + increment
        for v in range(levels):
            result[v, :, cols] = updated[v * rows : (v + 1) * rows]
        pltpu.make_async_copy(
            result.at[:, :, cols], out_hbm.at[:, :, cols], sems.at[1]
        ).start()
    pltpu.make_async_copy(result, out_hbm, sems.at[1]).wait()
    spec_copy.wait()


def solution(mesh):
    n_lat, n_lev = mesh.shape["lat"], mesh.shape["lev"]

    def on_device(field, weights, depart_row, depart_col, legendre, wave_slot):
        levels, rows, width = field.shape
        _, waves, steps = legendre.shape
        tiles = width // LANES
        own = waves // n_lat
        n, half = n_lat * n_lev, n_lat // 2
        owners = half * n_lev
        rep = n_lev // (waves // half)
        lv = levels // rep
        pairs = waves * levels
        table = jnp.asarray(lon_table(waves))
        vmem, dma = pltpu.VMEM, pltpu.SemaphoreType.DMA
        anywhere = pl.BlockSpec(memory_space=pltpu.HBM)
        in_vmem = pl.BlockSpec(memory_space=pltpu.VMEM)
        adv, synth, wide, spec = pl.pallas_call(
            functools.partial(kernel, n_lat, n_lev),
            out_shape=(
                vmem((levels * rows, width), F32),
                vmem((rows, 2 * pairs), F32),
                vmem((2, 2 * pairs, width), BF16),
                vmem((2 * own, 2, steps), F32),
            ),
            in_specs=[anywhere] * 7,
            out_specs=(in_vmem,) * 4,
            scratch_shapes=[
                pltpu.SMEM((waves,), jnp.int32),
                vmem((levels, tiles, rows + 16, LANES), F32),
                vmem((4, levels, tiles, rows + 16, LANES), F32),
                vmem((6 * rows, width), BF16),
                vmem((rows, width), jnp.int32),
                vmem((rows, width), jnp.int32),
                vmem((rows * waves, steps), BF16),
                vmem((4 * waves, width), BF16),
                vmem((4 * waves, width), BF16),
                vmem((2, tiles, 2 * levels, LANES), F32),
                vmem((2, tiles, 2 * levels, LANES), BF16),
                vmem((2, rows, LANES), BF16),
                vmem((2, tiles + 2, 2 * levels, LANES), BF16),
                vmem((2, rows, LANES), BF16),
                vmem((6 * 16, width), BF16),
                vmem((6 * 16, width), F32),
                vmem((6 * rows, LANES), F32),
                vmem((2, rows + 16, LANES), F32),
                vmem((half, rows, steps), BF16),
                vmem((n_lat, HALF, steps), BF16),
                vmem((2 * pairs, LANES), F32),
                vmem((owners, lv, LANES), F32),
                vmem((n, lv, LANES), F32),
                vmem((2 * lv, n_lat * HALF), F32),
                vmem((half, lv, LANES), BF16),
                vmem((n, lv, LANES), BF16),
                vmem((2 * pairs, 4 * LANES), BF16),
                vmem((lv, 2, steps), F32),
                vmem((2 * own, 2, steps), F32),
                dma((10,)),
                dma((3,)), dma((3,)),
                dma, dma,
                dma, dma,
                dma, dma,
                dma, dma,
                pltpu.SemaphoreType.REGULAR((2,)),
            ],
            compiler_params=pltpu.CompilerParams(
                collective_id=0, has_side_effects=True, vmem_limit_bytes=40 << 20
            ),
        )(
            *(
                pltpu.with_memory_space_constraint(x, pltpu.HBM)
                for x in (
                    wave_slot, field, weights.reshape(4 * rows, width), depart_row, depart_col,
                    legendre.reshape(rows * waves, steps), table,
                )
            ),
        )
        updated, spectral = pl.pallas_call(
            finish,
            out_shape=(
                jax.ShapeDtypeStruct((levels, rows, width), F32),
                jax.ShapeDtypeStruct((2 * own, 2, steps), F32),
            ),
            in_specs=[in_vmem] * 4,
            out_specs=(anywhere,) * 2,
            scratch_shapes=[
                vmem((levels * rows, 2 * pairs), BF16),
                vmem((levels * rows, 2 * pairs), BF16),
                vmem((levels, rows, width), F32),
                dma((2,)),
            ],
            compiler_params=pltpu.CompilerParams(vmem_limit_bytes=20 << 20),
        )(*(pltpu.with_memory_space_constraint(x, vmem) for x in (adv, synth, wide, spec)))
        return updated, spectral.reshape(own, 2, 1, 2, steps)

    placed = (
        P(None, "lat", "lev"),
        P(None, "lat", "lev"),
        P("lat", "lev"),
        P("lat", "lev"),
        P("lat", None, None),
        P(),
    )
    return jax.shard_map(
        on_device,
        mesh=mesh,
        in_specs=placed,
        out_specs=(P(None, "lat", "lev"), P("lat", None, "lev", None, None)),
        check_vma=False,
    )
```

```python
import functools
import math

import jax
import jax.numpy as jnp
import numpy as np
from jax import lax
from jax.experimental import pallas as pl
from jax.experimental.pallas import tpu as pltpu
from jax.sharding import PartitionSpec as P

NLON = 4096
NT = 1279
DAMPING = 4.0
LANES = 128
HALF = 64
MESH = pl.DeviceIdType.MESH
F32 = jnp.float32
BF16 = jnp.bfloat16


def lon_table(waves):
    m = (np.arange(waves, dtype=np.int64) * (NT + 1)) // waves
    phases = (m[:, None] * np.arange(NLON, dtype=np.int64)[None, :]) % NLON
    angles = phases.astype(np.float64) * (2.0 * math.pi / NLON)
    table = np.concatenate([np.cos(angles), -np.sin(angles)], axis=0) / math.sqrt(NLON)
    table = table.astype(np.float32)
    lead = table.astype(BF16)
    rest = (table - lead.astype(np.float32)).astype(BF16)
    return np.concatenate([lead, rest], axis=0)


def each(start, stop):
    def run(body):
        if stop - start <= 64:
            for i in range(start, stop):
                body(i)
        else:
            lax.fori_loop(start, stop, lambda i, carry: (body(i), carry)[1], 0)

    return run


def one_hot(mask):
    return jnp.where(mask, 1.0, 0.0).astype(BF16)


def kernel(
    n_lat, n_lev,
    slot_hbm, field_hbm, weights_hbm, drow_hbm, dcol_hbm, leg_hbm, table_hbm,
    adv, synth, wide, spec_ref,
    slot_ref, ext, shifted, points, drow, dcol, leg, tab, tabs,
    rim_rows, pack_row, pack_col, got_rim, got_col, rim_inputs, rim_points, side_points, side,
    send_leg, basis, stage, split, send_1, got_1, both_f, send_2, got_2, cross, send_p, got_p,
    load_sem, halo_send, halo_recv, leg_send, leg_recv, one_send, one_recv,
    two_send, two_recv, p_send, p_recv, round_sem,
):
    levels, _, _, _ = ext.shape
    rows, width = drow.shape
    tiles = width // LANES
    steps = leg.shape[1]
    waves = leg.shape[0] // rows
    n = n_lat * n_lev
    half = n_lat // 2
    group = waves // half
    rep = n_lev // group
    lv = levels // rep
    own = waves // n_lat
    l, e = lax.axis_index("lat"), lax.axis_index("lev")
    me = l * n_lev + e
    parity, lh = lax.div(l, half), lax.rem(l, half)
    share = lax.rem(e, rep)
    slot = group * lh + lax.div(e, rep)
    has_up, has_down = l > 0, l < n_lat - 1
    east, west = lax.rem(e + 1, n_lev), lax.rem(e + n_lev - 1, n_lev)

    barrier = pltpu.get_barrier_semaphore()

    def greet(lat, lev):
        pl.semaphore_signal(barrier, inc=1, device_id=(lat, lev), device_id_type=MESH)

    column = [(parity * half + lax.rem(lh + off, half), e) for off in range(1, half)]
    across = (lax.rem(l + half, n_lat), e)
    partners = [(l, lax.rem(e + off, n_lev)) for off in range(1, n_lev)]
    partners += column + [across]
    for there, lat in ((has_down, l + 1), (has_up, l - 1)):

        @pl.when(there)
        def _():
            for lev in (e, east, west):
                greet(lat, lev)

    for lat, lev in partners:
        greet(lat, lev)
    n_greet = len(partners) + jnp.where(has_up, 3, 0) + jnp.where(has_down, 3, 0)

    def load(k, src, dst):
        copy = pltpu.make_async_copy(src, dst, load_sem.at[k])
        copy.start()
        return copy

    inner_rows = pl.ds(16, rows - 16)
    inner_field = pl.ds(8, rows - 16)
    for t in range(tiles):
        cols = pl.ds(t * LANES, LANES)
        load(0, field_hbm.at[:, pl.ds(0, 8), cols], ext.at[:, t, pl.ds(8, 8), :])
        load(0, field_hbm.at[:, pl.ds(rows - 8, 8), cols], ext.at[:, t, pl.ds(rows, 8), :])
    for t in range(tiles):
        cols = pl.ds(t * LANES, LANES)
        k = 6 if t in (0, tiles - 1) else 7
        for v in range(levels):
            load(k, field_hbm.at[v, inner_field, cols], ext.at[v, t, inner_rows, :])
    load_leg = load(1, leg_hbm, leg)
    load_slot = load(2, slot_hbm, slot_ref)
    load(3, weights_hbm, points.at[pl.ds(0, 4 * rows), :])
    for q in range(4):
        for k in range(2):
            load(
                5, weights_hbm.at[pl.ds(q * rows + k * (rows - 8), 8), :],
                rim_inputs.at[pl.ds(16 * q + 8 * k, 8), :],
            )
    load(3, drow_hbm, drow)
    load(3, dcol_hbm, dcol)
    load_tab = load(
        4, table_hbm.at[:, pl.ds(pl.multiple_of(e * width, LANES), width)], tab
    )

    def tell(k, devices):
        for there in devices:
            pl.semaphore_signal(round_sem.at[k], inc=1, device_id=there, device_id_type=MESH)

    at = lambda shape, dim: lax.broadcasted_iota(jnp.int32, shape, dim)
    for row0 in (0, rows + 8):
        zero = jnp.zeros((levels, tiles, 8, LANES), F32)
        ext[:, :, row0 : row0 + 8, :] = zero
        for move in range(4):
            shifted[move, :, :, row0 : row0 + 8, :] = zero
        for k in range(2):
            side[k, row0 : row0 + 8, :] = zero[0, 0]
    stage[...] = jnp.zeros_like(stage)
    cross[...] = jnp.zeros_like(cross)
    padded = send_leg.shape[1]
    basis[:half, padded:, :] = jnp.zeros((half, HALF - padded, steps), BF16)

    lane = at((rows, LANES), 1)
    outer_part = adv.at[pl.ds(0, 16 * levels), :]
    pltpu.make_async_copy(outer_part, outer_part, load_sem.at[0]).wait()
    edge_part = ext.at[:, pl.ds(0, 2), inner_rows, :]
    pltpu.make_async_copy(edge_part, edge_part, load_sem.at[6]).wait()
    for v in range(levels):
        for t in range(tiles):
            rim_rows[0, t, 2 * v : 2 * v + 2, :] = ext[v, t, 6 + rows : 8 + rows, :]
            rim_rows[1, t, 2 * v : 2 * v + 2, :] = ext[v, t, 8:10, :]
    pack_row[...] = rim_rows[...].astype(BF16)
    last = jnp.zeros((rows, LANES), F32)
    first = jnp.zeros((rows, LANES), F32)
    for v in range(levels):
        tail = pltpu.roll(ext[v, tiles - 1, 8 : 8 + rows, :], (2 * v + 2) % LANES, 1)
        last = jnp.where(lax.div(lane, 2) == v, tail, last)
        head = pltpu.roll(ext[v, 0, 8 : 8 + rows, :], HALF + 2 * v, 1)
        first = jnp.where(lax.div(lane - HALF, 2) == v, head, first)
    pack_col[0] = last.astype(BF16)
    pack_col[1] = first.astype(BF16)

    def remote(src, dst, ssem, rsem, lat, lev):
        return pltpu.make_async_remote_copy(
            src_ref=src, dst_ref=dst, send_sem=ssem, recv_sem=rsem,
            device_id=(lat, lev), device_id_type=MESH,
        )

    def halo(k, src, dst, lat, lev):
        return remote(src, dst, halo_send.at[k], halo_recv.at[k], lat, lev)

    flat = [
        halo(2, pack_col.at[0], got_col.at[0], l, east),
        halo(2, pack_col.at[1], got_col.at[1], l, west),
    ]
    rims = [
        [
            halo(k, pack_row.at[k], got_rim.at[k, pl.ds(1, tiles)], lat, e),
            halo(3 + k, pack_row.at[k, tiles - 1], got_rim.at[k, 0], lat, east),
            halo(3 + k, pack_row.at[k, 0], got_rim.at[k, tiles + 1], lat, west),
        ]
        for k, lat in ((0, l + 1), (1, l - 1))
    ]

    pl.semaphore_wait(barrier, n_greet)

    @pl.when(has_down)
    def _():
        for copy in rims[0]:
            copy.start()

    @pl.when(has_up)
    def _():
        for copy in rims[1]:
            copy.start()

    for copy in flat:
        copy.start()

    tell(0, column)

    if tiles > 2:
        other_part = ext.at[:, pl.ds(0, tiles - 2), inner_rows, :]
        pltpu.make_async_copy(other_part, other_part, load_sem.at[7]).wait()
    load_slot.wait()
    load_leg.wait()
    load_tab.wait()
    point_part = adv.at[pl.ds(0, 4 * rows), :]
    pltpu.make_async_copy(point_part, point_part, load_sem.at[3]).wait()
    weights_in = rim_inputs.at[pl.ds(0, 64), :]
    pltpu.make_async_copy(weights_in, weights_in, load_sem.at[5]).wait()
    first = lax.broadcasted_iota(jnp.int32, (1, 4 * waves), 1)
    slot_row = jnp.zeros((1, 4 * waves), jnp.int32)
    for k in range(waves):
        slot_row = jnp.where(lax.rem(first, waves) == k, slot_ref[k], slot_row)
    iota_f = (4 * waves, 4 * waves)
    order = one_hot(
        (lax.div(at(iota_f, 0), waves) == lax.div(at(iota_f, 1), waves))
        & (lax.rem(at(iota_f, 0), waves) == slot_row)
    )
    lane = at((8, LANES), 1)
    moves = (-2, -1, 1, 2)

    def move_blocks(blocks, move):
        turned = [x if x is None else pltpu.roll(x, (-move) % LANES, 1) for x in blocks]
        zero = jnp.zeros((8, LANES), F32)
        result = []
        for t in range(1, len(blocks) - 1):
            near = turned[t - 1] if move < 0 else turned[t + 1]
            wrapped = (lane < -move) if move < 0 else (lane >= LANES - move)
            result.append(jnp.where(wrapped, zero if near is None else near, turned[t]))
        return result

    groups = rows // 8

    def shift_level(v):
        for g in range(groups):
            band = slice(8 + 8 * g, 16 + 8 * g)
            blocks = [None] + [ext[v, t, band, :] for t in range(tiles)] + [None]
            for k, move in enumerate(moves):
                for t, value in enumerate(move_blocks(blocks, move)):
                    shifted[k, v, t, band, :] = value

    for v in range(levels):
        shift_level(v)

    band = 8
    iota_g = (half * band, band * waves)
    slot_cols = jnp.zeros((1, band * waves), jnp.int32)
    lane_k = lax.rem(lax.broadcasted_iota(jnp.int32, (1, band * waves), 1), waves)
    for k in range(waves):
        slot_cols = jnp.where(lane_k == k, slot_ref[k], slot_cols)
    choose = one_hot(
        (lax.rem(at(iota_g, 0), band) == lax.div(at(iota_g, 1), waves))
        & (group * lax.div(at(iota_g, 0), band) + lax.div(e, rep) == slot_cols)
    )
    for i in range(0, rows, band):
        picked = jnp.dot(
            choose, leg[i * waves : (i + band) * waves, :], preferred_element_type=F32
        ).astype(BF16)
        for t in range(half):
            send_leg[t, i : i + band, :] = picked[t * band : (t + 1) * band]
    tabs[...] = jnp.dot(order, tab[...], preferred_element_type=F32).astype(BF16)

    for q, ref in ((4, drow), (5, dcol)):
        for k in range(2):
            row0 = 16 * q + 8 * k
            rim_inputs[row0 : row0 + 8, :] = (
                ref[k * (rows - 8) : k * (rows - 8) + 8, :].astype(F32).astype(BF16)
            )
        for cols in (slice(0, LANES), slice(width - LANES, width)):
            points[q * rows : (q + 1) * rows, cols] = ref[:, cols].astype(F32).astype(BF16)
    iota_r = (6 * 16, 6 * 16)
    row_r, col_r = at(iota_r, 0), at(iota_r, 1)
    repeat_rows = one_hot(
        (lax.div(row_r, 8) == lax.div(col_r, 8))
        & ((col_r & 7) == (row_r & 1) + jnp.where((row_r & 15) < 8, 0, 6))
    )
    rim_points[...] = jnp.dot(repeat_rows, rim_inputs[...], preferred_element_type=F32)
    row_c, col_c = at((LANES, LANES), 0), at((LANES, LANES), 1)
    from_first = one_hot((col_c < HALF) & (row_c == (col_c & 1)))
    from_last = one_hot((col_c >= HALF) & (row_c == LANES - 2 + (col_c & 1)))
    side_points[...] = jnp.dot(
        points[:, 0:LANES], from_first, preferred_element_type=F32
    ) + jnp.dot(points[:, width - LANES :], from_last, preferred_element_type=F32)

    def choose_two(high, low, values):
        one = jnp.where(high, values[2], values[0])
        two = jnp.where(high, values[3], values[1])
        three = jnp.where(high, values[4], values[2])
        return jnp.where(low, two, one), jnp.where(low, three, two)


    sub = at((8, LANES), 0)

    def advect(t, carry):
        cols = pl.ds(pl.multiple_of(t * LANES, LANES), LANES)
        corner = [points[k * rows : (k + 1) * rows, cols].astype(F32) for k in range(4)]
        zero = jnp.zeros((8, LANES), F32)
        turned = {}

        def turn(v, c, g, amount):
            if g < 0 or g >= groups:
                return zero
            key = (v, c, g, amount)
            if key not in turned:
                turned[key] = pltpu.roll(plane(v, c)[8 * g + 8 : 8 * g + 16, :], amount, 0)
            return turned[key]

        def plane(v, c):
            return ext.at[v, t] if c == 2 else shifted.at[c if c < 2 else c - 1, v, t]

        def five(v, c, g):
            ref = plane(v, c)
            load_at = lambda r: ref[8 * g + 8 + r : 8 * g + 16 + r, :]
            values = [load_at(r) for r in (-1, 0, 1)]
            if c in (0, 1, 3, 4):
                before = jnp.where(sub < 2, turn(v, c, g - 1, 2), turn(v, c, g, 2))
                after = jnp.where(sub < 6, turn(v, c, g, 6), turn(v, c, g + 1, 6))
            else:
                before, after = load_at(-2), load_at(2)
            return [before] + values + [after]

        for v in range(levels):
            for g in range(groups):
                band = slice(8 * g, 8 * g + 8)
                dr, dc = drow[band, cols], dcol[band, cols]
                row_high, row_low = dr >= 0, (dr & 1) == 1
                col_high, col_low = dc >= 0, (dc & 1) == 1
                w = [corner[k][band] for k in range(4)]
                picked = [choose_two(row_high, row_low, five(v, c, g)) for c in range(5)]
                upper = choose_two(col_high, col_low, [x[0] for x in picked])
                lower = choose_two(col_high, col_low, [x[1] for x in picked])
                total = w[0] * upper[0] + w[1] * upper[1] + w[2] * lower[0] + w[3] * lower[1]
                adv[v * rows + 8 * g : v * rows + 8 * g + 8, cols] = total
        return carry

    lax.fori_loop(0, tiles // 2, advect, 0)
    pl.semaphore_wait(round_sem.at[0], half - 1)
    tell(1, [across])
    slots_of = lambda t: basis.at[t, pl.ds(0, padded), :]
    copies_g = []
    for off in range(1, half):
        t = lax.rem(lh + off, half)
        copy = remote(
            send_leg.at[t], slots_of(lh), leg_send, leg_recv,
            parity * half + t, e,
        )
        copy.start()
        copies_g.append(copy)
    basis[lh, 0:padded, :] = send_leg[lh]


    lax.fori_loop(tiles // 2, tiles, advect, 0)

    even = (at((8, LANES), 0) & 1) == 0

    def fix_rows(k, first_tile, last_tile):
        for c0 in range(0, 2 * levels, 8):
            blocks = [
                got_rim[k, t, c0 : c0 + 8, :].astype(F32)
                for t in range(first_tile, last_tile + 3)
            ]
            moved = [move_blocks(blocks, move) for move in moves]
            moved.insert(2, blocks[1:-1])
            for t in range(first_tile, last_tile + 1):
                cols = slice(t * LANES, (t + 1) * LANES)
                w0, w1, w2, w3, dr, dc = [
                    rim_points[16 * q + 8 * k : 16 * q + 8 * k + 8, cols] for q in range(6)
                ]
                col_high, col_low = dc >= 0.0, (dc == -1.0) | (dc == 1.0)
                same = [moved[c][t - first_tile] for c in range(5)]
                other = [pltpu.roll(x, 1 if k else 7, 0) for x in same]
                s0, s1 = choose_two(col_high, col_low, same)
                o0, o1 = choose_two(col_high, col_low, other)
                if k == 0:
                    far = jnp.where(dr == -2.0, w0 * s0 + w1 * s1, 0.0)
                    near = jnp.where(
                        dr == -1.0, w0 * o0 + w1 * o1,
                        jnp.where(dr == -2.0, w2 * o0 + w3 * o1, 0.0),
                    )
                    near = jnp.where(even, near, 0.0)
                else:
                    far = jnp.where(dr == 1.0, w2 * s0 + w3 * s1, 0.0)
                    near = jnp.where(
                        dr == 1.0, w0 * o0 + w1 * o1,
                        jnp.where(dr == 0.0, w2 * o0 + w3 * o1, 0.0),
                    )
                    near = jnp.where(even, 0.0, near)
                extra = far + near
                for i in range(0, 8, 2):
                    row0 = (c0 + i) // 2 * rows + k * (rows - 2)
                    adv[row0 : row0 + 2, cols] += extra[i : i + 2]

    rim_middle = [got_rim.at[k, pl.ds(1, tiles)] for k in range(2)]
    rim_corner = [got_rim.at[k, pl.ds(0, 2)] for k in range(2)]
    for k, there in ((0, has_up), (1, has_down)):

        @pl.when(there)
        def _():
            pltpu.make_async_copy(rim_middle[k], rim_middle[k], halo_recv.at[k]).wait()
            if tiles > 2:
                fix_rows(k, 1, tiles - 2)

    pltpu.make_async_copy(got_col, got_col, halo_recv.at[2]).wait()
    here = jnp.where(
        at((rows, LANES), 1) < HALF, got_col[0].astype(F32), got_col[1].astype(F32)
    )
    side[0, 8 : 8 + rows, :] = here
    side[1, 8 : 8 + rows, :] = jnp.where(
        at((rows, LANES), 1) < HALF, pltpu.roll(here, LANES - 1, 1), pltpu.roll(here, 1, 1)
    )
    in_west = lane < HALF
    edge = jnp.where(in_west, -1.0, 1.0)
    inner = (lane & 1) == jnp.where(in_west, 0, 1)
    for g in range(groups):
        w0, w1, w2, w3, dr, dc = [
            side_points[q * rows + 8 * g : q * rows + 8 * g + 8, :] for q in range(6)
        ]
        row_high, row_low = dr >= 0.0, (dr == -1.0) | (dr == 1.0)
        s0, s1 = choose_two(
            row_high, row_low, [side[0, 8 * g + 6 + r : 8 * g + 14 + r, :] for r in range(5)]
        )
        o0, o1 = choose_two(
            row_high, row_low, [side[1, 8 * g + 6 + r : 8 * g + 14 + r, :] for r in range(5)]
        )
        far = jnp.where(
            dc == jnp.where(in_west, -2.0, 1.0),
            jnp.where(in_west, w0, w1) * s0 + jnp.where(in_west, w2, w3) * s1,
            0.0,
        )
        near = jnp.where(
            dc == edge, w0 * o0 + w2 * o1,
            jnp.where(dc == edge - 1.0, w1 * o0 + w3 * o1, 0.0),
        )
        extra = far + jnp.where(inner, near, 0.0)
        for v in range(levels):
            band = slice(v * rows + 8 * g, v * rows + 8 * g + 8)
            west_part = pltpu.roll(extra, (LANES - 2 * v) % LANES, 1) if v else extra
            adv[band, 0:LANES] += jnp.where(lane < 2, west_part, 0.0)
            east_part = pltpu.roll(extra, (LANES - 2 - HALF - 2 * v) % LANES, 1)
            adv[band, width - LANES :] += jnp.where(lane >= LANES - 2, east_part, 0.0)

    for k, there in ((0, has_up), (1, has_down)):

        @pl.when(there)
        def _():
            pltpu.make_async_copy(rim_corner[k], rim_corner[k], halo_recv.at[3 + k]).wait()
            fix_rows(k, 0, 0)
            fix_rows(k, tiles - 1, tiles - 1)

    contract_last = (((1,), (1,)), ((), ()))
    for pair in range(levels // 2):
        for k in range(2):
            v = 2 * pair + k
            value = adv[v * rows : (v + 1) * rows, :]
            lead = value.astype(BF16)
            split[pair, k * rows : (k + 1) * rows, :] = lead
            split[pair, (2 + k) * rows : (3 + k) * rows, :] = (
                value - lead.astype(F32)
            ).astype(BF16)
        both = lax.dot_general(
            tabs[...], split[pair, 0 : 2 * rows, :], contract_last, preferred_element_type=F32
        )
        more = lax.dot_general(
            tabs[0 : 2 * waves, :], split[pair, 2 * rows :, :], contract_last,
            preferred_element_type=F32,
        )
        stage[2 * waves * pair : 2 * waves * (pair + 1), 0 : 2 * rows] = (
            both[0 : 2 * waves] + both[2 * waves :] + more
        )
    owners = half * n_lev
    for s in range(waves):
        for g in range(rep):
            send_1[s * rep + g] = stage[pl.ds(g * lv * waves + s, lv, stride=waves), :]

    turn_by = jnp.where(parity == 0, n_lat - 1, 1)

    def others(body):
        def column_of(a, first):
            lat = lax.rem(l + turn_by * a, n_lat)
            inside = lax.div(lat, half) == parity
            block = jnp.where(inside, lat, n_lat - 1 - lat) - parity * half
            base = lax.rem(lat, half) * n_lev

            def send(b):
                lev = lax.rem(e + b, n_lev)
                body(lat, lev, base + lev, block)

            each(first, n_lev)(send)

        each(1, n_lat)(lambda a: column_of(a, 0))
        column_of(0, 1)

    def start_1(lat, lev, owner, block):
        remote(send_1.at[owner], got_1.at[me], one_send, one_recv, lat, lev).start()

    pl.semaphore_wait(round_sem.at[1], 1)

    others(start_1)

    got_1[me] = send_1[lh * n_lev + e]

    spread_rows = 2 * waves * levels
    iota_w = (spread_rows, 2 * waves)
    row_w = at(iota_w, 0)
    repeat = one_hot(
        (row_w & 1) * waves + lax.div(lax.rem(row_w, waves * levels), levels) == at(iota_w, 1)
    )
    for q in range(2):
        wide[q] = jnp.dot(
            repeat, tabs[2 * waves * q : 2 * waves * (q + 1), :], preferred_element_type=F32
        ).astype(BF16)

    at_row, at_col = at((LANES, LANES), 0), at((LANES, LANES), 1)
    flip = one_hot(
        ((at_row + at_col == rows - 1) & (at_row < HALF) & (at_col < HALF))
        | ((at_row + at_col == 2 * HALF + rows - 1) & (at_row >= HALF) & (at_col >= HALF))
    )
    sign = jnp.where(parity == 0, 1.0, -1.0).astype(F32)
    iota_e = (rows, 4 * LANES)
    row_e, col_e = at(iota_e, 0), at(iota_e, 1)
    part_e, lane_e = lax.div(col_e, LANES), lax.rem(col_e, LANES)
    place = HALF * lax.div(part_e, 2)
    natural = (lax.rem(part_e, 2) == 1) & (lane_e == row_e + place)
    turned = (lax.rem(part_e, 2) == 0) & (lane_e == rows - 1 - row_e + place)
    gather = (jnp.where(natural, sign, 0.0) + jnp.where(turned, 1.0, 0.0)).astype(BF16)

    wave_own = jnp.int32(0)
    for k in range(waves):
        wave_own = jnp.where(slot_ref[k] == slot, k, wave_own)
    wave_own = wave_own * (NT + 1) // waves
    column = lax.broadcasted_iota(jnp.int32, (2 * lv, steps), 1)
    degree = wave_own + 2 * column + parity
    factor = 1.0 / (
        1.0 + DAMPING * (degree * (degree + 1)).astype(F32) / float(NT * (NT + 1))
    )
    forward_scale = 1.0 / math.sqrt(rows * n_lat // 2)
    inverse_scale = math.sqrt(NLON) / math.sqrt(waves) / math.sqrt(steps)
    scale = jnp.where(wave_own == 0, inverse_scale, 2.0 * inverse_scale).astype(F32)

    legs = send_leg.at[pl.ds(0, half - 1)]
    pltpu.make_async_copy(legs, legs, leg_recv).wait()

    def all_of(ref, sem, count=n - 1):
        return pltpu.make_async_copy(ref.at[pl.ds(0, count)], ref.at[pl.ds(0, count)], sem)

    for b in range(0, half, 2):
        turned = jnp.dot(
            flip, basis[b : b + 2].reshape(LANES, steps), preferred_element_type=F32
        ).astype(BF16)
        basis[half + b : half + b + 2] = turned.reshape(2, HALF, steps)

    all_of(got_1, one_recv).wait()

    low = lax.broadcasted_iota(jnp.int32, (lv, LANES), 1) < HALF

    def total_1(lat):
        value = got_1[lat * n_lev]
        for d in range(1, n_lev):
            value = value + got_1[lat * n_lev + d]
        return value

    for which in range(2):
        for b in range(0, half, 2):
            lat = parity * half + b
            one = total_1(lat if which == 0 else n_lat - 1 - lat)
            two = total_1(lat + 1 if which == 0 else n_lat - 2 - lat)
            col0 = (which * half + b) * HALF
            cols = slice(col0, col0 + LANES)
            both_f[0:lv, cols] = jnp.where(low, one, pltpu.roll(two, HALF, 1))
            both_f[lv:, cols] = jnp.where(
                low, pltpu.roll(one, LANES - rows, 1), pltpu.roll(two, HALF - rows, 1)
            )
    inside = half * HALF
    terms = both_f[...].astype(BF16)
    matrix = basis[...].reshape(2 * inside, steps)
    raw = sign * jnp.dot(
        terms[:, :inside], matrix[:inside], preferred_element_type=F32
    ) + jnp.dot(terms[:, inside:], matrix[inside:], preferred_element_type=F32)
    raw = raw * forward_scale
    masked = jnp.where(degree <= NT, raw, 0.0)
    damped = masked * factor
    change = (damped - masked).astype(BF16)
    back = lax.dot_general(
        change, matrix[:inside], contract_last, preferred_element_type=F32
    )
    both_f[:, :inside] = back * scale
    for b in range(0, half, 2):
        cols = slice(b * HALF, b * HALF + LANES)
        real, imag = both_f[0:lv, cols], both_f[lv:, cols]
        send_2[b] = jnp.where(low, real, pltpu.roll(imag, HALF, 1)).astype(BF16)
        send_2[b + 1] = jnp.where(low, pltpu.roll(real, HALF, 1), imag).astype(BF16)

    def start_2(lat, lev, owner, block):
        remote(send_2.at[block], got_2.at[me], two_send, two_recv, lat, lev).start()

    others(start_2)

    got_2[me] = send_2[lh]

    for vv in range(lv):
        for c in range(2):
            row0 = lv * (vv % 2) + 2 * (vv // 2) + c
            send_p[vv, c : c + 1, :] = damped[row0 : row0 + 1]
    home, place_p = lax.div(slot, own), lax.rem(slot, own)
    for vv in range(lv):
        lev = share * lv + vv
        mine = (home == l) & (lev == e)
        copy = remote(
            send_p.at[vv], got_p.at[2 * place_p + parity], p_send, p_recv, home, lev
        )
        pl.when(jnp.logical_not(mine))(copy.start)

        @pl.when(mine)
        def _():
            got_p[2 * place_p + parity] = send_p[vv]

    all_of(got_2, two_recv).wait()

    pairs = waves * levels
    for which in range(2):
        start = jnp.where(which == 1, parity, 1 - parity) * owners
        for o in range(owners):
            stage[which * pairs + o * lv : which * pairs + (o + 1) * lv, :] = got_2[
                start + o
            ].astype(F32)
    for which in range(2):
        value = stage[which * pairs : (which + 1) * pairs, :].astype(BF16)
        for c in range(2):
            cols = slice((2 * c + which) * LANES, (2 * c + which + 1) * LANES)
            cross[c * pairs : (c + 1) * pairs, cols] = value
    synth[...] = lax.dot_general(
        gather, cross[...], contract_last, preferred_element_type=F32
    )

    keeps = (home == l) & (share == lax.div(e, lv))
    spec_waits = [
        (keeps, all_of(got_p, p_recv, 2 * own - 1)),
        (jnp.logical_not(keeps), all_of(got_p, p_recv, 2 * own)),
    ]
    for case, copy in spec_waits:
        pl.when(case)(copy.wait)
    for k in range(2 * own):
        spec_ref[k] = got_p[k]

    pltpu.make_async_copy(got_col, got_col, halo_send.at[2]).wait()
    pltpu.make_async_copy(legs, legs, leg_send).wait()
    all_of(got_1, one_send).wait()
    all_of(got_2, two_send).wait()
    pl.when(keeps)(all_of(send_p, p_send, lv - 1).wait)
    pl.when(jnp.logical_not(keeps))(all_of(send_p, p_send, lv).wait)

    for k, there in ((0, has_down), (1, has_up)):
        for ref, sem in ((rim_middle[k], halo_send.at[k]), (rim_corner[k], halo_send.at[3 + k])):
            pl.when(there)(pltpu.make_async_copy(ref, ref, sem).wait)


def finish(adv, synth, wide, spec, out_hbm, spec_hbm, lead_all, rest_all, result, sems):
    levels, rows, width = result.shape
    spec_copy = pltpu.make_async_copy(spec, spec_hbm, sems.at[0])
    spec_copy.start()
    value = synth[...]
    lead = value.astype(BF16).astype(F32)
    rest = value - lead
    column = lax.broadcasted_iota(jnp.int32, value.shape, 1)
    level_of = lax.rem(column, levels)
    level_of = level_of - (level_of & 1) + lax.div(column, value.shape[1] // 2)
    for v in range(levels):
        at = slice(v * rows, (v + 1) * rows)
        lead_all[at, :] = jnp.where(level_of == v, lead, 0.0).astype(BF16)
        rest_all[at, :] = jnp.where(level_of == v, rest, 0.0).astype(BF16)
    chunk = min(width, 256)
    for j in range(0, width, chunk):
        cols = slice(j, j + chunk)
        increment = (
            jnp.dot(lead_all[...], wide[0, :, cols], preferred_element_type=F32)
            + jnp.dot(lead_all[...], wide[1, :, cols], preferred_element_type=F32)
            + jnp.dot(rest_all[...], wide[0, :, cols], preferred_element_type=F32)
        )
        updated = adv[:, cols] + increment
        for v in range(levels):
            result[v, :, cols] = updated[v * rows : (v + 1) * rows]
        pltpu.make_async_copy(
            result.at[:, :, cols], out_hbm.at[:, :, cols], sems.at[1]
        ).start()
    pltpu.make_async_copy(result, out_hbm, sems.at[1]).wait()
    spec_copy.wait()


def solution(mesh):
    n_lat, n_lev = mesh.shape["lat"], mesh.shape["lev"]

    def on_device(field, weights, depart_row, depart_col, legendre, wave_slot):
        levels, rows, width = field.shape
        _, waves, steps = legendre.shape
        tiles = width // LANES
        own = waves // n_lat
        n, half = n_lat * n_lev, n_lat // 2
        owners = half * n_lev
        rep = n_lev // (waves // half)
        lv = levels // rep
        pairs = waves * levels
        table = jnp.asarray(lon_table(waves))
        vmem, dma = pltpu.VMEM, pltpu.SemaphoreType.DMA
        anywhere = pl.BlockSpec(memory_space=pltpu.HBM)
        in_vmem = pl.BlockSpec(memory_space=pltpu.VMEM)
        adv, synth, wide, spec = pl.pallas_call(
            functools.partial(kernel, n_lat, n_lev),
            out_shape=(
                vmem((levels * rows, width), F32),
                vmem((rows, 2 * pairs), F32),
                vmem((2, 2 * pairs, width), BF16),
                vmem((2 * own, 2, steps), F32),
            ),
            in_specs=[anywhere] * 7,
            out_specs=(in_vmem,) * 4,
            scratch_shapes=[
                pltpu.SMEM((waves,), jnp.int32),
                vmem((levels, tiles, rows + 16, LANES), F32),
                vmem((4, levels, tiles, rows + 16, LANES), F32),
                vmem((6 * rows, width), BF16),
                vmem((rows, width), jnp.int32),
                vmem((rows, width), jnp.int32),
                vmem((rows * waves, steps), BF16),
                vmem((4 * waves, width), BF16),
                vmem((4 * waves, width), BF16),
                vmem((2, tiles, 2 * levels, LANES), F32),
                vmem((2, tiles, 2 * levels, LANES), BF16),
                vmem((2, rows, LANES), BF16),
                vmem((2, tiles + 2, 2 * levels, LANES), BF16),
                vmem((2, rows, LANES), BF16),
                vmem((6 * 16, width), BF16),
                vmem((6 * 16, width), F32),
                vmem((6 * rows, LANES), F32),
                vmem((2, rows + 16, LANES), F32),
                vmem((half, rows, steps), BF16),
                vmem((n_lat, HALF, steps), BF16),
                vmem((2 * pairs, LANES), F32),
                vmem((levels // 2, 4 * rows, width), BF16),
                vmem((owners, lv, LANES), F32),
                vmem((n, lv, LANES), F32),
                vmem((2 * lv, n_lat * HALF), F32),
                vmem((half, lv, LANES), BF16),
                vmem((n, lv, LANES), BF16),
                vmem((2 * pairs, 4 * LANES), BF16),
                vmem((lv, 2, steps), F32),
                vmem((2 * own, 2, steps), F32),
                dma((8,)),
                dma((5,)), dma((5,)),
                dma, dma,
                dma, dma,
                dma, dma,
                dma, dma,
                pltpu.SemaphoreType.REGULAR((2,)),
            ],
            compiler_params=pltpu.CompilerParams(
                collective_id=0, has_side_effects=True, vmem_limit_bytes=40 << 20
            ),
        )(
            *(
                pltpu.with_memory_space_constraint(x, pltpu.HBM)
                for x in (
                    wave_slot, field, weights.reshape(4 * rows, width), depart_row, depart_col,
                    legendre.reshape(rows * waves, steps), table,
                )
            ),
        )
        updated, spectral = pl.pallas_call(
            finish,
            out_shape=(
                jax.ShapeDtypeStruct((levels, rows, width), F32),
                jax.ShapeDtypeStruct((2 * own, 2, steps), F32),
            ),
            in_specs=[in_vmem] * 4,
            out_specs=(anywhere,) * 2,
            scratch_shapes=[
                vmem((levels * rows, 2 * pairs), BF16),
                vmem((levels * rows, 2 * pairs), BF16),
                vmem((levels, rows, width), F32),
                dma((2,)),
            ],
            compiler_params=pltpu.CompilerParams(vmem_limit_bytes=20 << 20),
        )(*(pltpu.with_memory_space_constraint(x, vmem) for x in (adv, synth, wide, spec)))
        return updated, spectral.reshape(own, 2, 1, 2, steps)

    placed = (
        P(None, "lat", "lev"),
        P(None, "lat", "lev"),
        P("lat", "lev"),
        P("lat", "lev"),
        P("lat", None, None),
        P(),
    )
    return jax.shard_map(
        on_device,
        mesh=mesh,
        in_specs=placed,
        out_specs=(P(None, "lat", "lev"), P("lat", None, "lev", None, None)),
        check_vma=False,
    )
```

```python
import functools
import math

import jax
import jax.numpy as jnp
import numpy as np
from jax import lax
from jax.experimental import pallas as pl
from jax.experimental.pallas import tpu as pltpu
from jax.sharding import PartitionSpec as P

NLON = 4096
NT = 1279
DAMPING = 4.0
LANES = 128
HALF = 64
MESH = pl.DeviceIdType.MESH
F32 = jnp.float32
BF16 = jnp.bfloat16


def lon_table(waves):
    m = (np.arange(waves, dtype=np.int64) * (NT + 1)) // waves
    phases = (m[:, None] * np.arange(NLON, dtype=np.int64)[None, :]) % NLON
    angles = phases.astype(np.float64) * (2.0 * math.pi / NLON)
    table = np.concatenate([np.cos(angles), -np.sin(angles)], axis=0) / math.sqrt(NLON)
    table = table.astype(np.float32)
    lead = table.astype(BF16)
    rest = (table - lead.astype(np.float32)).astype(BF16)
    return np.concatenate([lead, rest], axis=0)


def each(start, stop):
    def run(body):
        if stop - start <= 64:
            for i in range(start, stop):
                body(i)
        else:
            lax.fori_loop(start, stop, lambda i, carry: (body(i), carry)[1], 0)

    return run


def one_hot(mask):
    return jnp.where(mask, 1.0, 0.0).astype(BF16)


def kernel(
    n_lat, n_lev,
    slot_hbm, field_hbm, weights_hbm, drow_hbm, dcol_hbm, leg_hbm, table_hbm,
    adv, synth, wide, spec_ref,
    slot_ref, ext, shifted, points, drow, dcol, leg, tab, tabs,
    rim_rows, pack_row, pack_col, got_rim, got_col, rim_inputs, rim_points, side_points, side,
    send_leg, basis, stage, split, send_1, got_1, both_f, send_2, got_2, cross, send_p, got_p,
    load_sem, halo_send, halo_recv, leg_send, leg_recv, one_send, one_recv,
    two_send, two_recv, p_send, p_recv, round_sem,
):
    levels, _, _, _ = ext.shape
    rows, width = drow.shape
    tiles = width // LANES
    steps = leg.shape[1]
    waves = leg.shape[0] // rows
    n = n_lat * n_lev
    half = n_lat // 2
    group = waves // half
    rep = n_lev // group
    lv = levels // rep
    own = waves // n_lat
    l, e = lax.axis_index("lat"), lax.axis_index("lev")
    me = l * n_lev + e
    parity, lh = lax.div(l, half), lax.rem(l, half)
    share = lax.rem(e, rep)
    slot = group * lh + lax.div(e, rep)
    has_up, has_down = l > 0, l < n_lat - 1
    east, west = lax.rem(e + 1, n_lev), lax.rem(e + n_lev - 1, n_lev)

    barrier = pltpu.get_barrier_semaphore()

    def greet(lat, lev):
        pl.semaphore_signal(barrier, inc=1, device_id=(lat, lev), device_id_type=MESH)

    column = [(parity * half + lax.rem(lh + off, half), e) for off in range(1, half)]
    across = (lax.rem(l + half, n_lat), e)
    partners = [(l, lax.rem(e + off, n_lev)) for off in range(1, n_lev)]
    partners += column + [across]
    for there, lat in ((has_down, l + 1), (has_up, l - 1)):

        @pl.when(there)
        def _():
            for lev in (e, east, west):
                greet(lat, lev)

    for lat, lev in partners:
        greet(lat, lev)
    n_greet = len(partners) + jnp.where(has_up, 3, 0) + jnp.where(has_down, 3, 0)

    def load(k, src, dst):
        copy = pltpu.make_async_copy(src, dst, load_sem.at[k])
        copy.start()
        return copy

    inner_rows = pl.ds(16, rows - 16)
    inner_field = pl.ds(8, rows - 16)
    for t in range(tiles):
        cols = pl.ds(t * LANES, LANES)
        load(0, field_hbm.at[:, pl.ds(0, 8), cols], ext.at[:, t, pl.ds(8, 8), :])
        load(0, field_hbm.at[:, pl.ds(rows - 8, 8), cols], ext.at[:, t, pl.ds(rows, 8), :])
    for t in range(tiles):
        cols = pl.ds(t * LANES, LANES)
        k = 6 if t in (0, tiles - 1) else 7
        for v in range(levels):
            load(k, field_hbm.at[v, inner_field, cols], ext.at[v, t, inner_rows, :])
    load_leg = load(1, leg_hbm, leg)
    load_slot = load(2, slot_hbm, slot_ref)
    load(3, weights_hbm, points.at[pl.ds(0, 4 * rows), :])
    for q in range(4):
        for k in range(2):
            load(
                5, weights_hbm.at[pl.ds(q * rows + k * (rows - 8), 8), :],
                rim_inputs.at[pl.ds(16 * q + 8 * k, 8), :],
            )
    load(3, drow_hbm, drow)
    load(3, dcol_hbm, dcol)
    load_tab = load(
        4, table_hbm.at[:, pl.ds(pl.multiple_of(e * width, LANES), width)], tab
    )

    def tell(k, devices):
        for there in devices:
            pl.semaphore_signal(round_sem.at[k], inc=1, device_id=there, device_id_type=MESH)

    at = lambda shape, dim: lax.broadcasted_iota(jnp.int32, shape, dim)
    for row0 in (0, rows + 8):
        zero = jnp.zeros((levels, tiles, 8, LANES), F32)
        ext[:, :, row0 : row0 + 8, :] = zero
        for move in range(4):
            shifted[move, :, :, row0 : row0 + 8, :] = zero
        for k in range(2):
            side[k, row0 : row0 + 8, :] = zero[0, 0]
    stage[...] = jnp.zeros_like(stage)
    cross[...] = jnp.zeros_like(cross)
    padded = send_leg.shape[1]
    basis[:half, padded:, :] = jnp.zeros((half, HALF - padded, steps), BF16)

    lane = at((rows, LANES), 1)
    outer_part = adv.at[pl.ds(0, 16 * levels), :]
    pltpu.make_async_copy(outer_part, outer_part, load_sem.at[0]).wait()
    edge_part = ext.at[:, pl.ds(0, 2), inner_rows, :]
    pltpu.make_async_copy(edge_part, edge_part, load_sem.at[6]).wait()
    for v in range(levels):
        for t in range(tiles):
            rim_rows[0, t, 2 * v : 2 * v + 2, :] = ext[v, t, 6 + rows : 8 + rows, :]
            rim_rows[1, t, 2 * v : 2 * v + 2, :] = ext[v, t, 8:10, :]
    pack_row[...] = rim_rows[...].astype(BF16)
    last = jnp.zeros((rows, LANES), F32)
    first = jnp.zeros((rows, LANES), F32)
    for v in range(levels):
        tail = pltpu.roll(ext[v, tiles - 1, 8 : 8 + rows, :], (2 * v + 2) % LANES, 1)
        last = jnp.where(lax.div(lane, 2) == v, tail, last)
        head = pltpu.roll(ext[v, 0, 8 : 8 + rows, :], HALF + 2 * v, 1)
        first = jnp.where(lax.div(lane - HALF, 2) == v, head, first)
    pack_col[0] = last.astype(BF16)
    pack_col[1] = first.astype(BF16)

    def remote(src, dst, ssem, rsem, lat, lev):
        return pltpu.make_async_remote_copy(
            src_ref=src, dst_ref=dst, send_sem=ssem, recv_sem=rsem,
            device_id=(lat, lev), device_id_type=MESH,
        )

    def halo(k, src, dst, lat, lev):
        return remote(src, dst, halo_send.at[k], halo_recv.at[k], lat, lev)

    flat = [
        halo(2, pack_col.at[0], got_col.at[0], l, east),
        halo(2, pack_col.at[1], got_col.at[1], l, west),
    ]
    rims = [
        [
            halo(k, pack_row.at[k], got_rim.at[k, pl.ds(1, tiles)], lat, e),
            halo(3 + k, pack_row.at[k, tiles - 1], got_rim.at[k, 0], lat, east),
            halo(3 + k, pack_row.at[k, 0], got_rim.at[k, tiles + 1], lat, west),
        ]
        for k, lat in ((0, l + 1), (1, l - 1))
    ]

    pl.semaphore_wait(barrier, n_greet)

    @pl.when(has_down)
    def _():
        for copy in rims[0]:
            copy.start()

    @pl.when(has_up)
    def _():
        for copy in rims[1]:
            copy.start()

    for copy in flat:
        copy.start()

    tell(0, column)

    if tiles > 2:
        other_part = ext.at[:, pl.ds(0, tiles - 2), inner_rows, :]
        pltpu.make_async_copy(other_part, other_part, load_sem.at[7]).wait()
    load_slot.wait()
    load_leg.wait()
    load_tab.wait()
    point_part = adv.at[pl.ds(0, 4 * rows), :]
    pltpu.make_async_copy(point_part, point_part, load_sem.at[3]).wait()
    weights_in = rim_inputs.at[pl.ds(0, 64), :]
    pltpu.make_async_copy(weights_in, weights_in, load_sem.at[5]).wait()
    first = lax.broadcasted_iota(jnp.int32, (1, 4 * waves), 1)
    slot_row = jnp.zeros((1, 4 * waves), jnp.int32)
    for k in range(waves):
        slot_row = jnp.where(lax.rem(first, waves) == k, slot_ref[k], slot_row)
    iota_f = (4 * waves, 4 * waves)
    order = one_hot(
        (lax.div(at(iota_f, 0), waves) == lax.div(at(iota_f, 1), waves))
        & (lax.rem(at(iota_f, 0), waves) == slot_row)
    )
    lane = at((8, LANES), 1)
    moves = (-2, -1, 1, 2)

    def move_blocks(blocks, move):
        turned = [x if x is None else pltpu.roll(x, (-move) % LANES, 1) for x in blocks]
        zero = jnp.zeros((8, LANES), F32)
        result = []
        for t in range(1, len(blocks) - 1):
            near = turned[t - 1] if move < 0 else turned[t + 1]
            wrapped = (lane < -move) if move < 0 else (lane >= LANES - move)
            result.append(jnp.where(wrapped, zero if near is None else near, turned[t]))
        return result

    groups = rows // 8

    def shift_level(v):
        for g in range(groups):
            band = slice(8 + 8 * g, 16 + 8 * g)
            blocks = [None] + [ext[v, t, band, :] for t in range(tiles)] + [None]
            for k, move in enumerate(moves):
                for t, value in enumerate(move_blocks(blocks, move)):
                    shifted[k, v, t, band, :] = value

    for v in range(levels):
        shift_level(v)

    band = 8
    iota_g = (half * band, band * waves)
    slot_cols = jnp.zeros((1, band * waves), jnp.int32)
    lane_k = lax.rem(lax.broadcasted_iota(jnp.int32, (1, band * waves), 1), waves)
    for k in range(waves):
        slot_cols = jnp.where(lane_k == k, slot_ref[k], slot_cols)
    choose = one_hot(
        (lax.rem(at(iota_g, 0), band) == lax.div(at(iota_g, 1), waves))
        & (group * lax.div(at(iota_g, 0), band) + lax.div(e, rep) == slot_cols)
    )
    for i in range(0, rows, band):
        picked = jnp.dot(
            choose, leg[i * waves : (i + band) * waves, :], preferred_element_type=F32
        ).astype(BF16)
        for t in range(half):
            send_leg[t, i : i + band, :] = picked[t * band : (t + 1) * band]
    tabs[...] = jnp.dot(order, tab[...], preferred_element_type=F32).astype(BF16)

    for q, ref in ((4, drow), (5, dcol)):
        for k in range(2):
            row0 = 16 * q + 8 * k
            rim_inputs[row0 : row0 + 8, :] = (
                ref[k * (rows - 8) : k * (rows - 8) + 8, :].astype(F32).astype(BF16)
            )
        for cols in (slice(0, LANES), slice(width - LANES, width)):
            points[q * rows : (q + 1) * rows, cols] = ref[:, cols].astype(F32).astype(BF16)
    iota_r = (6 * 16, 6 * 16)
    row_r, col_r = at(iota_r, 0), at(iota_r, 1)
    repeat_rows = one_hot(
        (lax.div(row_r, 8) == lax.div(col_r, 8))
        & ((col_r & 7) == (row_r & 1) + jnp.where((row_r & 15) < 8, 0, 6))
    )
    rim_points[...] = jnp.dot(repeat_rows, rim_inputs[...], preferred_element_type=F32)
    row_c, col_c = at((LANES, LANES), 0), at((LANES, LANES), 1)
    from_first = one_hot((col_c < HALF) & (row_c == (col_c & 1)))
    from_last = one_hot((col_c >= HALF) & (row_c == LANES - 2 + (col_c & 1)))
    side_points[...] = jnp.dot(
        points[:, 0:LANES], from_first, preferred_element_type=F32
    ) + jnp.dot(points[:, width - LANES :], from_last, preferred_element_type=F32)

    def choose_two(high, low, values):
        one = jnp.where(high, values[2], values[0])
        two = jnp.where(high, values[3], values[1])
        three = jnp.where(high, values[4], values[2])
        return jnp.where(low, two, one), jnp.where(low, three, two)


    sub = at((8, LANES), 0)

    def advect(t, carry):
        cols = pl.ds(pl.multiple_of(t * LANES, LANES), LANES)
        corner = [points[k * rows : (k + 1) * rows, cols].astype(F32) for k in range(4)]
        zero = jnp.zeros((8, LANES), F32)
        turned = {}

        def turn(v, c, g, amount):
            if g < 0 or g >= groups:
                return zero
            key = (v, c, g, amount)
            if key not in turned:
                turned[key] = pltpu.roll(plane(v, c)[8 * g + 8 : 8 * g + 16, :], amount, 0)
            return turned[key]

        def plane(v, c):
            return ext.at[v, t] if c == 2 else shifted.at[c if c < 2 else c - 1, v, t]

        def five(v, c, g):
            ref = plane(v, c)
            load_at = lambda r: ref[8 * g + 8 + r : 8 * g + 16 + r, :]
            values = [load_at(r) for r in (-1, 0, 1)]
            if c in (0, 1, 3, 4):
                before = jnp.where(sub < 2, turn(v, c, g - 1, 2), turn(v, c, g, 2))
                after = jnp.where(sub < 6, turn(v, c, g, 6), turn(v, c, g + 1, 6))
            else:
                before, after = load_at(-2), load_at(2)
            return [before] + values + [after]

        for v in range(levels):
            for g in range(groups):
                band = slice(8 * g, 8 * g + 8)
                dr, dc = drow[band, cols], dcol[band, cols]
                row_high, row_low = dr >= 0, (dr & 1) == 1
                col_high, col_low = dc >= 0, (dc & 1) == 1
                w = [corner[k][band] for k in range(4)]
                picked = [choose_two(row_high, row_low, five(v, c, g)) for c in range(5)]
                upper = choose_two(col_high, col_low, [x[0] for x in picked])
                lower = choose_two(col_high, col_low, [x[1] for x in picked])
                total = w[0] * upper[0] + w[1] * upper[1] + w[2] * lower[0] + w[3] * lower[1]
                adv[v * rows + 8 * g : v * rows + 8 * g + 8, cols] = total
        return carry

    lax.fori_loop(0, tiles // 2, advect, 0)
    pl.semaphore_wait(round_sem.at[0], half - 1)
    tell(1, [across])
    slots_of = lambda t: basis.at[t, pl.ds(0, padded), :]
    copies_g = []
    for off in range(1, half):
        t = lax.rem(lh + off, half)
        copy = remote(
            send_leg.at[t], slots_of(lh), leg_send, leg_recv,
            parity * half + t, e,
        )
        copy.start()
        copies_g.append(copy)
    basis[lh, 0:padded, :] = send_leg[lh]


    lax.fori_loop(tiles // 2, tiles, advect, 0)

    even = (at((8, LANES), 0) & 1) == 0

    def fix_rows(k, first_tile, last_tile):
        for c0 in range(0, 2 * levels, 8):
            blocks = [
                got_rim[k, t, c0 : c0 + 8, :].astype(F32)
                for t in range(first_tile, last_tile + 3)
            ]
            moved = [move_blocks(blocks, move) for move in moves]
            moved.insert(2, blocks[1:-1])
            for t in range(first_tile, last_tile + 1):
                cols = slice(t * LANES, (t + 1) * LANES)
                w0, w1, w2, w3, dr, dc = [
                    rim_points[16 * q + 8 * k : 16 * q + 8 * k + 8, cols] for q in range(6)
                ]
                col_high, col_low = dc >= 0.0, (dc == -1.0) | (dc == 1.0)
                same = [moved[c][t - first_tile] for c in range(5)]
                other = [pltpu.roll(x, 1 if k else 7, 0) for x in same]
                s0, s1 = choose_two(col_high, col_low, same)
                o0, o1 = choose_two(col_high, col_low, other)
                if k == 0:
                    far = jnp.where(dr == -2.0, w0 * s0 + w1 * s1, 0.0)
                    near = jnp.where(
                        dr == -1.0, w0 * o0 + w1 * o1,
                        jnp.where(dr == -2.0, w2 * o0 + w3 * o1, 0.0),
                    )
                    near = jnp.where(even, near, 0.0)
                else:
                    far = jnp.where(dr == 1.0, w2 * s0 + w3 * s1, 0.0)
                    near = jnp.where(
                        dr == 1.0, w0 * o0 + w1 * o1,
                        jnp.where(dr == 0.0, w2 * o0 + w3 * o1, 0.0),
                    )
                    near = jnp.where(even, 0.0, near)
                extra = far + near
                for i in range(0, 8, 2):
                    row0 = (c0 + i) // 2 * rows + k * (rows - 2)
                    adv[row0 : row0 + 2, cols] += extra[i : i + 2]

    pltpu.make_async_copy(got_col, got_col, halo_recv.at[2]).wait()
    here = jnp.where(
        at((rows, LANES), 1) < HALF, got_col[0].astype(F32), got_col[1].astype(F32)
    )
    side[0, 8 : 8 + rows, :] = here
    side[1, 8 : 8 + rows, :] = jnp.where(
        at((rows, LANES), 1) < HALF, pltpu.roll(here, LANES - 1, 1), pltpu.roll(here, 1, 1)
    )
    in_west = lane < HALF
    edge = jnp.where(in_west, -1.0, 1.0)
    inner = (lane & 1) == jnp.where(in_west, 0, 1)
    for g in range(groups):
        w0, w1, w2, w3, dr, dc = [
            side_points[q * rows + 8 * g : q * rows + 8 * g + 8, :] for q in range(6)
        ]
        row_high, row_low = dr >= 0.0, (dr == -1.0) | (dr == 1.0)
        s0, s1 = choose_two(
            row_high, row_low, [side[0, 8 * g + 6 + r : 8 * g + 14 + r, :] for r in range(5)]
        )
        o0, o1 = choose_two(
            row_high, row_low, [side[1, 8 * g + 6 + r : 8 * g + 14 + r, :] for r in range(5)]
        )
        far = jnp.where(
            dc == jnp.where(in_west, -2.0, 1.0),
            jnp.where(in_west, w0, w1) * s0 + jnp.where(in_west, w2, w3) * s1,
            0.0,
        )
        near = jnp.where(
            dc == edge, w0 * o0 + w2 * o1,
            jnp.where(dc == edge - 1.0, w1 * o0 + w3 * o1, 0.0),
        )
        extra = far + jnp.where(inner, near, 0.0)
        for v in range(levels):
            band = slice(v * rows + 8 * g, v * rows + 8 * g + 8)
            west_part = pltpu.roll(extra, (LANES - 2 * v) % LANES, 1) if v else extra
            adv[band, 0:LANES] += jnp.where(lane < 2, west_part, 0.0)
            east_part = pltpu.roll(extra, (LANES - 2 - HALF - 2 * v) % LANES, 1)
            adv[band, width - LANES :] += jnp.where(lane >= LANES - 2, east_part, 0.0)

    rim_middle = [got_rim.at[k, pl.ds(1, tiles)] for k in range(2)]
    rim_corner = [got_rim.at[k, pl.ds(0, 2)] for k in range(2)]
    for k, there in ((0, has_up), (1, has_down)):

        @pl.when(there)
        def _():
            pltpu.make_async_copy(rim_middle[k], rim_middle[k], halo_recv.at[k]).wait()
            if tiles > 2:
                fix_rows(k, 1, tiles - 2)

    for k, there in ((0, has_up), (1, has_down)):

        @pl.when(there)
        def _():
            pltpu.make_async_copy(rim_corner[k], rim_corner[k], halo_recv.at[3 + k]).wait()
            fix_rows(k, 0, 0)
            fix_rows(k, tiles - 1, tiles - 1)

    contract_last = (((1,), (1,)), ((), ()))
    for pair in range(levels // 2):
        for k in range(2):
            v = 2 * pair + k
            value = adv[v * rows : (v + 1) * rows, :]
            lead = value.astype(BF16)
            split[pair, k * rows : (k + 1) * rows, :] = lead
            split[pair, (2 + k) * rows : (3 + k) * rows, :] = (
                value - lead.astype(F32)
            ).astype(BF16)
        both = lax.dot_general(
            tabs[...], split[pair, 0 : 2 * rows, :], contract_last, preferred_element_type=F32
        )
        more = lax.dot_general(
            tabs[0 : 2 * waves, :], split[pair, 2 * rows :, :], contract_last,
            preferred_element_type=F32,
        )
        stage[2 * waves * pair : 2 * waves * (pair + 1), 0 : 2 * rows] = (
            both[0 : 2 * waves] + both[2 * waves :] + more
        )
    owners = half * n_lev
    for s in range(waves):
        for g in range(rep):
            send_1[s * rep + g] = stage[pl.ds(g * lv * waves + s, lv, stride=waves), :]

    by_distance = sorted(range(n_lev), key=lambda b: -min(b, n_lev - b))

    def others(body):
        def column_of(a):
            lat = jnp.where(parity == 0, n_lat - 1 - a, a)
            inside = lax.div(lat, half) == parity
            block = jnp.where(inside, lat, n_lat - 1 - lat) - parity * half
            base = lax.rem(lat, half) * n_lev
            for b in by_distance:
                lev = lax.rem(e + b, n_lev)
                copy = body(lat, lev, base + lev, block)
                if b:
                    copy.start()
                else:
                    pl.when(lat != l)(copy.start)

        each(0, n_lat)(column_of)

    def start_1(lat, lev, owner, block):
        return remote(send_1.at[owner], got_1.at[me], one_send, one_recv, lat, lev)

    pl.semaphore_wait(round_sem.at[1], 1)

    others(start_1)

    got_1[me] = send_1[lh * n_lev + e]

    spread_rows = 2 * waves * levels
    iota_w = (spread_rows, 2 * waves)
    row_w = at(iota_w, 0)
    repeat = one_hot(
        (row_w & 1) * waves + lax.div(lax.rem(row_w, waves * levels), levels) == at(iota_w, 1)
    )
    for q in range(2):
        wide[q] = jnp.dot(
            repeat, tabs[2 * waves * q : 2 * waves * (q + 1), :], preferred_element_type=F32
        ).astype(BF16)

    at_row, at_col = at((LANES, LANES), 0), at((LANES, LANES), 1)
    flip = one_hot(
        ((at_row + at_col == rows - 1) & (at_row < HALF) & (at_col < HALF))
        | ((at_row + at_col == 2 * HALF + rows - 1) & (at_row >= HALF) & (at_col >= HALF))
    )
    sign = jnp.where(parity == 0, 1.0, -1.0).astype(F32)
    iota_e = (rows, 4 * LANES)
    row_e, col_e = at(iota_e, 0), at(iota_e, 1)
    part_e, lane_e = lax.div(col_e, LANES), lax.rem(col_e, LANES)
    place = HALF * lax.div(part_e, 2)
    natural = (lax.rem(part_e, 2) == 1) & (lane_e == row_e + place)
    turned = (lax.rem(part_e, 2) == 0) & (lane_e == rows - 1 - row_e + place)
    gather = (jnp.where(natural, sign, 0.0) + jnp.where(turned, 1.0, 0.0)).astype(BF16)

    wave_own = jnp.int32(0)
    for k in range(waves):
        wave_own = jnp.where(slot_ref[k] == slot, k, wave_own)
    wave_own = wave_own * (NT + 1) // waves
    column = lax.broadcasted_iota(jnp.int32, (2 * lv, steps), 1)
    degree = wave_own + 2 * column + parity
    factor = 1.0 / (
        1.0 + DAMPING * (degree * (degree + 1)).astype(F32) / float(NT * (NT + 1))
    )
    forward_scale = 1.0 / math.sqrt(rows * n_lat // 2)
    inverse_scale = math.sqrt(NLON) / math.sqrt(waves) / math.sqrt(steps)
    scale = jnp.where(wave_own == 0, inverse_scale, 2.0 * inverse_scale).astype(F32)

    legs = send_leg.at[pl.ds(0, half - 1)]
    pltpu.make_async_copy(legs, legs, leg_recv).wait()

    def all_of(ref, sem, count=n - 1):
        return pltpu.make_async_copy(ref.at[pl.ds(0, count)], ref.at[pl.ds(0, count)], sem)

    for b in range(0, half, 2):
        turned = jnp.dot(
            flip, basis[b : b + 2].reshape(LANES, steps), preferred_element_type=F32
        ).astype(BF16)
        basis[half + b : half + b + 2] = turned.reshape(2, HALF, steps)

    all_of(got_1, one_recv).wait()

    low = lax.broadcasted_iota(jnp.int32, (lv, LANES), 1) < HALF

    def total_1(lat):
        value = got_1[lat * n_lev]
        for d in range(1, n_lev):
            value = value + got_1[lat * n_lev + d]
        return value

    for which in range(2):
        for b in range(0, half, 2):
            lat = parity * half + b
            one = total_1(lat if which == 0 else n_lat - 1 - lat)
            two = total_1(lat + 1 if which == 0 else n_lat - 2 - lat)
            col0 = (which * half + b) * HALF
            cols = slice(col0, col0 + LANES)
            both_f[0:lv, cols] = jnp.where(low, one, pltpu.roll(two, HALF, 1))
            both_f[lv:, cols] = jnp.where(
                low, pltpu.roll(one, LANES - rows, 1), pltpu.roll(two, HALF - rows, 1)
            )
    inside = half * HALF
    terms = both_f[...].astype(BF16)
    matrix = basis[...].reshape(2 * inside, steps)
    raw = sign * jnp.dot(
        terms[:, :inside], matrix[:inside], preferred_element_type=F32
    ) + jnp.dot(terms[:, inside:], matrix[inside:], preferred_element_type=F32)
    raw = raw * forward_scale
    masked = jnp.where(degree <= NT, raw, 0.0)
    damped = masked * factor
    change = (damped - masked).astype(BF16)
    back = lax.dot_general(
        change, matrix[:inside], contract_last, preferred_element_type=F32
    )
    both_f[:, :inside] = back * scale
    for b in range(0, half, 2):
        cols = slice(b * HALF, b * HALF + LANES)
        real, imag = both_f[0:lv, cols], both_f[lv:, cols]
        send_2[b] = jnp.where(low, real, pltpu.roll(imag, HALF, 1)).astype(BF16)
        send_2[b + 1] = jnp.where(low, pltpu.roll(real, HALF, 1), imag).astype(BF16)

    def start_2(lat, lev, owner, block):
        return remote(send_2.at[block], got_2.at[me], two_send, two_recv, lat, lev)

    others(start_2)

    got_2[me] = send_2[lh]

    for vv in range(lv):
        for c in range(2):
            row0 = lv * (vv % 2) + 2 * (vv // 2) + c
            send_p[vv, c : c + 1, :] = damped[row0 : row0 + 1]
    home, place_p = lax.div(slot, own), lax.rem(slot, own)
    for vv in range(lv):
        lev = share * lv + vv
        mine = (home == l) & (lev == e)
        copy = remote(
            send_p.at[vv], got_p.at[2 * place_p + parity], p_send, p_recv, home, lev
        )
        pl.when(jnp.logical_not(mine))(copy.start)

        @pl.when(mine)
        def _():
            got_p[2 * place_p + parity] = send_p[vv]

    all_of(got_2, two_recv).wait()

    pairs = waves * levels
    for which in range(2):
        start = jnp.where(which == 1, parity, 1 - parity) * owners
        for o in range(owners):
            stage[which * pairs + o * lv : which * pairs + (o + 1) * lv, :] = got_2[
                start + o
            ].astype(F32)
    for which in range(2):
        value = stage[which * pairs : (which + 1) * pairs, :].astype(BF16)
        for c in range(2):
            cols = slice((2 * c + which) * LANES, (2 * c + which + 1) * LANES)
            cross[c * pairs : (c + 1) * pairs, cols] = value
    synth[...] = lax.dot_general(
        gather, cross[...], contract_last, preferred_element_type=F32
    )

    keeps = (home == l) & (share == lax.div(e, lv))
    spec_waits = [
        (keeps, all_of(got_p, p_recv, 2 * own - 1)),
        (jnp.logical_not(keeps), all_of(got_p, p_recv, 2 * own)),
    ]
    for case, copy in spec_waits:
        pl.when(case)(copy.wait)
    for k in range(2 * own):
        spec_ref[k] = got_p[k]

    pltpu.make_async_copy(got_col, got_col, halo_send.at[2]).wait()
    pltpu.make_async_copy(legs, legs, leg_send).wait()
    all_of(got_1, one_send).wait()
    all_of(got_2, two_send).wait()
    pl.when(keeps)(all_of(send_p, p_send, lv - 1).wait)
    pl.when(jnp.logical_not(keeps))(all_of(send_p, p_send, lv).wait)

    for k, there in ((0, has_down), (1, has_up)):
        for ref, sem in ((rim_middle[k], halo_send.at[k]), (rim_corner[k], halo_send.at[3 + k])):
            pl.when(there)(pltpu.make_async_copy(ref, ref, sem).wait)


def finish(adv, synth, wide, spec, out_hbm, spec_hbm, lead_all, rest_all, result, sems):
    levels, rows, width = result.shape
    spec_copy = pltpu.make_async_copy(spec, spec_hbm, sems.at[0])
    spec_copy.start()
    value = synth[...]
    lead = value.astype(BF16).astype(F32)
    rest = value - lead
    column = lax.broadcasted_iota(jnp.int32, value.shape, 1)
    level_of = lax.rem(column, levels)
    level_of = level_of - (level_of & 1) + lax.div(column, value.shape[1] // 2)
    for v in range(levels):
        at = slice(v * rows, (v + 1) * rows)
        lead_all[at, :] = jnp.where(level_of == v, lead, 0.0).astype(BF16)
        rest_all[at, :] = jnp.where(level_of == v, rest, 0.0).astype(BF16)
    chunk = min(width, 256)
    for j in range(0, width, chunk):
        cols = slice(j, j + chunk)
        increment = (
            jnp.dot(lead_all[...], wide[0, :, cols], preferred_element_type=F32)
            + jnp.dot(lead_all[...], wide[1, :, cols], preferred_element_type=F32)
            + jnp.dot(rest_all[...], wide[0, :, cols], preferred_element_type=F32)
        )
        updated = adv[:, cols] + increment
        for v in range(levels):
            result[v, :, cols] = updated[v * rows : (v + 1) * rows]
        pltpu.make_async_copy(
            result.at[:, :, cols], out_hbm.at[:, :, cols], sems.at[1]
        ).start()
    pltpu.make_async_copy(result, out_hbm, sems.at[1]).wait()
    spec_copy.wait()


def solution(mesh):
    n_lat, n_lev = mesh.shape["lat"], mesh.shape["lev"]

    def on_device(field, weights, depart_row, depart_col, legendre, wave_slot):
        levels, rows, width = field.shape
        _, waves, steps = legendre.shape
        tiles = width // LANES
        own = waves // n_lat
        n, half = n_lat * n_lev, n_lat // 2
        owners = half * n_lev
        rep = n_lev // (waves // half)
        lv = levels // rep
        pairs = waves * levels
        table = jnp.asarray(lon_table(waves))
        vmem, dma = pltpu.VMEM, pltpu.SemaphoreType.DMA
        anywhere = pl.BlockSpec(memory_space=pltpu.HBM)
        in_vmem = pl.BlockSpec(memory_space=pltpu.VMEM)
        adv, synth, wide, spec = pl.pallas_call(
            functools.partial(kernel, n_lat, n_lev),
            out_shape=(
                vmem((levels * rows, width), F32),
                vmem((rows, 2 * pairs), F32),
                vmem((2, 2 * pairs, width), BF16),
                vmem((2 * own, 2, steps), F32),
            ),
            in_specs=[anywhere] * 7,
            out_specs=(in_vmem,) * 4,
            scratch_shapes=[
                pltpu.SMEM((waves,), jnp.int32),
                vmem((levels, tiles, rows + 16, LANES), F32),
                vmem((4, levels, tiles, rows + 16, LANES), F32),
                vmem((6 * rows, width), BF16),
                vmem((rows, width), jnp.int32),
                vmem((rows, width), jnp.int32),
                vmem((rows * waves, steps), BF16),
                vmem((4 * waves, width), BF16),
                vmem((4 * waves, width), BF16),
                vmem((2, tiles, 2 * levels, LANES), F32),
                vmem((2, tiles, 2 * levels, LANES), BF16),
                vmem((2, rows, LANES), BF16),
                vmem((2, tiles + 2, 2 * levels, LANES), BF16),
                vmem((2, rows, LANES), BF16),
                vmem((6 * 16, width), BF16),
                vmem((6 * 16, width), F32),
                vmem((6 * rows, LANES), F32),
                vmem((2, rows + 16, LANES), F32),
                vmem((half, rows, steps), BF16),
                vmem((n_lat, HALF, steps), BF16),
                vmem((2 * pairs, LANES), F32),
                vmem((levels // 2, 4 * rows, width), BF16),
                vmem((owners, lv, LANES), F32),
                vmem((n, lv, LANES), F32),
                vmem((2 * lv, n_lat * HALF), F32),
                vmem((half, lv, LANES), BF16),
                vmem((n, lv, LANES), BF16),
                vmem((2 * pairs, 4 * LANES), BF16),
                vmem((lv, 2, steps), F32),
                vmem((2 * own, 2, steps), F32),
                dma((8,)),
                dma((5,)), dma((5,)),
                dma, dma,
                dma, dma,
                dma, dma,
                dma, dma,
                pltpu.SemaphoreType.REGULAR((2,)),
            ],
            compiler_params=pltpu.CompilerParams(
                collective_id=0, has_side_effects=True, vmem_limit_bytes=40 << 20
            ),
        )(
            *(
                pltpu.with_memory_space_constraint(x, pltpu.HBM)
                for x in (
                    wave_slot, field, weights.reshape(4 * rows, width), depart_row, depart_col,
                    legendre.reshape(rows * waves, steps), table,
                )
            ),
        )
        updated, spectral = pl.pallas_call(
            finish,
            out_shape=(
                jax.ShapeDtypeStruct((levels, rows, width), F32),
                jax.ShapeDtypeStruct((2 * own, 2, steps), F32),
            ),
            in_specs=[in_vmem] * 4,
            out_specs=(anywhere,) * 2,
            scratch_shapes=[
                vmem((levels * rows, 2 * pairs), BF16),
                vmem((levels * rows, 2 * pairs), BF16),
                vmem((levels, rows, width), F32),
                dma((2,)),
            ],
            compiler_params=pltpu.CompilerParams(vmem_limit_bytes=20 << 20),
        )(*(pltpu.with_memory_space_constraint(x, vmem) for x in (adv, synth, wide, spec)))
        return updated, spectral.reshape(own, 2, 1, 2, steps)

    placed = (
        P(None, "lat", "lev"),
        P(None, "lat", "lev"),
        P("lat", "lev"),
        P("lat", "lev"),
        P("lat", None, None),
        P(),
    )
    return jax.shard_map(
        on_device,
        mesh=mesh,
        in_specs=placed,
        out_specs=(P(None, "lat", "lev"), P("lat", None, "lev", None, None)),
        check_vma=False,
    )
```
